32 devices in a mesh: days: 2 (over y), chan: 4 (over z), tm: 2 (over x), freq: 2 (over core).
Axes of the slice: x: 2, y: 2, z: 4, core: 2. Of those that a mesh axis runs over, the one named last changes fastest.
Arguments:
- recording: bfloat16 [2048, 2048], P(('days', 'chan', 'freq'), 'tm'), parts along dimension 0, may hold values from -6 to 6
- trailing: bfloat16 [2048, 1024], P(('days', 'chan', 'freq')), parts along dimension 0, may hold values from -6 to 6
- whiten_filter: bfloat16 [1024, 64], P(('chan', 'freq')), may hold values from -0.75 to 0.75
- pair_list: int32 [8, 4], P(('days', 'chan')), parts along dimension 0, may hold values from -1 to 3, as said below
Outputs:
- cross_spectra: float32 [8, 4, 4, 2, 256, 256], P(('days', 'chan'), None, ('tm', 'freq')), parts along dimension 0
The draws below stay inside these ranges and needn't reach their ends.
There are 2 independent parts, one for each index of `days`. The reference program is written for one: setup_inputs(seed, part) draws one part's arguments, and reference() takes and returns one part's arrays. A program takes and returns all parts, laid end to end along the dimension named above; an argument that names none is the same for every part. Nothing has to cross between parts.
Inputs may be any that keep to these rules, and one draw needn't show every extreme that they name: `pair_list`: row a lists in its first slots distinct blocks b with |b - a| <= 3, then -1 in the remaining slots; every row lists at least one block, and some row of every draw fills all 4 slots.
All inputs are finite; a program needn't handle non-finite values.
Results may differ from the reference program's by a relative error of at most 0.0046.
Values may be sent and summed in bfloat16 or wider, within the bound.
A program may use at most 64 MiB of HBM per device.

```python
import math
import jax
import jax.numpy as jnp
from jax import lax

BLK = 256
WHIT = 64
WIN = 2048
FB = 512
REACH = 3
SLOTS = 4
HOP = 1024
NB = 4
CHANNELS = 1024
SEGS = 2
SAMPLES = 2048
BANDS = 4
BANDW = 128
N_CHAN = 4


def draw_pair_list(key, part):
    first_key = jax.random.fold_in(key, 11)
    second_key = jax.random.fold_in(key, 12)
    third_key = jax.random.fold_in(key, 13)
    fourth_key = jax.random.fold_in(key, 14)
    spread = 2 * REACH + 1
    owners = jnp.arange(NB, dtype=jnp.int32)[:, None]
    columns = jnp.arange(spread, dtype=jnp.int32)[None, :]
    candidates = owners + columns - REACH
    is_valid = (candidates >= 0) & (candidates < NB)
    scores = jax.random.randint(first_key, (NB, spread), 0, 65536, dtype=jnp.int32) * spread + columns
    scores = jnp.where(is_valid, scores, -1)
    ranking = jnp.argsort(-scores, axis=1, stable=True)
    picked = jnp.take_along_axis(candidates, ranking, axis=1)[:, :SLOTS]
    counts = jax.random.randint(second_key, (NB,), 1, 3, dtype=jnp.int32)
    is_heavy = jax.random.randint(third_key, (NB,), 0, 4, dtype=jnp.int32) == 0
    counts = jnp.where(is_heavy, SLOTS, counts)
    forced = jax.random.randint(fourth_key, (), 0, NB, dtype=jnp.int32)
    counts = jnp.where(jnp.arange(NB, dtype=jnp.int32) == forced, SLOTS, counts)
    counts = jnp.minimum(counts, SLOTS)
    slot_index = jnp.arange(SLOTS, dtype=jnp.int32)[None, :]
    return jnp.where(slot_index < counts[:, None], picked, -1).astype(jnp.int32)


def shard_levels(rng, extent, split, least, top_value):
    def one(dim, shards_of):
        steps = jax.random.uniform(jax.random.fold_in(jax.random.fold_in(rng, 6), dim), (shards_of,), jnp.float32, least / len(split), top_value / len(split))
        return jnp.repeat(jnp.exp(steps), extent[dim] // shards_of).reshape((-1,) + (1,) * (len(extent) - dim - 1))

    loudness = one(*split[0])
    for cut in split[1:]:
        loudness = loudness * one(*cut)
    return loudness


def bell_draw(rng, extent, scale, bound, cuts=(), kind=jnp.bfloat16):
    array = scale * jax.random.normal(rng, extent, jnp.float32)
    if cuts:
        array = array * shard_levels(rng, extent, cuts, -0.22, 0.18)
    return jnp.clip(array, -bound, bound).astype(kind)


def setup_inputs(seed: int = 0, part: int = 0) -> dict:
    seeds = jax.random.split(jax.random.key(seed), 5)
    part_keys = jax.random.split(jax.random.fold_in(seeds[4], part), 5)
    recording = bell_draw(part_keys[0], (CHANNELS, SAMPLES), 1.0, 6.0, ((0, 8), (1, 2)))
    trailing = bell_draw(part_keys[1], (CHANNELS, HOP), 1.0, 6.0, ((0, 8),))
    whiten_filter = bell_draw(seeds[2], (CHANNELS, WHIT), WHIT ** -0.5, 0.75, ((0, 8),))
    pair_list = draw_pair_list(jax.random.fold_in(jax.random.fold_in(seeds[4], part), 71), part)
    return dict(recording=recording, trailing=trailing, whiten_filter=whiten_filter, pair_list=pair_list)


def fourier_table(first_bin, bin_count, length):
    samples = jnp.arange(length, dtype=jnp.int32)[:, None]
    bin_index = first_bin + jnp.arange(bin_count, dtype=jnp.int32)[None, :]
    phase = samples * bin_index % length
    angle = 2.0 * math.pi / length * phase.astype(jnp.float32)
    taper = 0.5 - 0.5 * jnp.cos(2.0 * math.pi / length * jnp.arange(length, dtype=jnp.int32).astype(jnp.float32))
    normaliser = 1.0 / math.sqrt(0.375 * length)
    cosine = (taper[:, None] * jnp.cos(angle) * normaliser).astype(jnp.bfloat16)
    sine_table = (-taper[:, None] * jnp.sin(angle) * normaliser).astype(jnp.bfloat16)
    return (cosine, sine_table)

def reference(recording, trailing, whiten_filter, pair_list):
    signal = jnp.concatenate([recording, trailing], axis=1)
    channels = signal.shape[0]
    cosine, sine_table = fourier_table(0, FB, WIN)
    joined = jnp.concatenate([cosine, sine_table], axis=1).astype(jnp.float32)

    def transform(segment):
        start = (segment * HOP).astype(jnp.int32)
        pieces = lax.dynamic_slice_in_dim(signal, start, WIN, 1)
        return jnp.dot(pieces.astype(jnp.float32), joined).astype(jnp.bfloat16)
    raw = lax.map(transform, jnp.arange(SEGS, dtype=jnp.int32))
    raw = raw.transpose(1, 0, 2).reshape(channels, SEGS * 2 * FB)
    rim_width = WHIT // 2
    padded = jnp.pad(raw, ((rim_width, rim_width), (0, 0)))
    offset = jnp.arange(BLK + WHIT, dtype=jnp.int32)[None, :] - jnp.arange(BLK, dtype=jnp.int32)[:, None]
    inside = (offset >= 0) & (offset < WHIT)
    clipped = jnp.clip(offset, 0, WHIT - 1)

    def whiten_block(index):
        start = (index * BLK).astype(jnp.int32)
        window_rows = lax.dynamic_slice_in_dim(padded, start, BLK + WHIT, 0)
        weight_rows = lax.dynamic_slice_in_dim(whiten_filter, start, BLK, 0)
        band_matrix = jnp.where(inside, jnp.take_along_axis(weight_rows, clipped, axis=1), jnp.zeros((), weight_rows.dtype))
        predicted = jnp.dot(band_matrix.astype(jnp.float32), window_rows.astype(jnp.float32))
        own_rows = lax.dynamic_slice_in_dim(raw, start, BLK, 0)
        return (own_rows.astype(jnp.float32) - predicted).astype(jnp.bfloat16)
    spectra = lax.map(whiten_block, jnp.arange(N_CHAN, dtype=jnp.int32))
    arranged = spectra.reshape(NB, BLK, SEGS, 2, BANDS, BANDW).transpose(0, 3, 4, 1, 2, 5)
    arranged = arranged.reshape(NB, 2, BANDS, BLK, SEGS * BANDW)
    scaling = 1.0 / math.sqrt(SEGS * BANDW)

    def owner(owner_index):
        own_block = lax.dynamic_index_in_dim(arranged, owner_index, 0, keepdims=False).astype(jnp.float32)

        def one_slot(partner_index):
            partner = lax.dynamic_index_in_dim(arranged, jnp.maximum(partner_index, 0), 0, keepdims=False).astype(jnp.float32)
            real_part = jnp.einsum('gik,gjk->gij', own_block[0], partner[0]) + jnp.einsum('gik,gjk->gij', own_block[1], partner[1])
            imag_part = jnp.einsum('gik,gjk->gij', own_block[1], partner[0]) - jnp.einsum('gik,gjk->gij', own_block[0], partner[1])
            crossed = jnp.stack([real_part, imag_part], axis=1) * scaling
            return jnp.where(partner_index >= 0, crossed, jnp.zeros((), crossed.dtype))
        return lax.map(one_slot, lax.dynamic_index_in_dim(pair_list, owner_index, 0, keepdims=False))
    return lax.map(owner, jnp.arange(NB, dtype=jnp.int32))
```

```python
import functools
import math

import jax
import jax.numpy as jnp
from jax import lax
from jax.experimental import pallas as pl
from jax.experimental.pallas import tpu as pltpu
from jax.sharding import PartitionSpec as P

FB = 512
REACH = 3
SLOTS = 4


def shifted(block, axis, distance):
    devices = range(lax.axis_size(axis))
    route = [(i - distance, i) for i in devices if i - distance in devices]
    return lax.ppermute(block, axis, route)


def extended(value, sides, width):
    for axis, dim in sides:
        size, length = (lax.axis_size(axis), value.shape[dim])
        up = [(i, (i + 1) % size) for i in range(size - 1)]
        down = [(j, i) for i, j in up]
        last = lax.slice_in_dim(value, length - width, length, axis=dim)
        initial = lax.slice_in_dim(value, 0, width, axis=dim)
        before = lax.ppermute(last, axis, up)
        after = lax.ppermute(initial, axis, down)
        value = jnp.concatenate([before, value, after], axis=dim)
    return value


def fourier_table(first_bin, bin_count, length):
    samples = jnp.arange(length, dtype=jnp.int32)[:, None]
    bin_index = first_bin + jnp.arange(bin_count, dtype=jnp.int32)[None, :]
    phase = samples * bin_index % length
    angle = 2.0 * math.pi / length * phase.astype(jnp.float32)
    taper = 0.5 - 0.5 * jnp.cos(
        2.0 * math.pi / length * jnp.arange(length, dtype=jnp.int32).astype(jnp.float32)
    )
    normaliser = 1.0 / math.sqrt(0.375 * length)
    cosine = (taper[:, None] * jnp.cos(angle) * normaliser).astype(jnp.bfloat16)
    sine_table = (-taper[:, None] * jnp.sin(angle) * normaliser).astype(jnp.bfloat16)
    return (cosine, sine_table)


def general(recording, trailing, whiten_filter, pair_list):
    local_rows, local_span = recording.shape
    hop_size = trailing.shape[1]
    window_size = 2 * hop_size
    segment_count = local_span // hop_size
    following = shifted(recording, "tm", -1)
    is_last = lax.axis_index("tm") == lax.axis_size("tm") - 1
    following = jnp.where(is_last, trailing, following)
    signal = jnp.concatenate([recording, following], axis=1)
    segments = jnp.stack([signal], axis=1)
    stacked_segments = segments.reshape(local_rows * segment_count, window_size)
    bin_step = min(256, FB)
    real_bins = []
    imag_bins = []
    for first_bin in range(0, FB, bin_step):
        cosine, sine_table = fourier_table(first_bin, bin_step, window_size)
        joined = jnp.concatenate([cosine, sine_table], axis=1)
        product = jnp.dot(stacked_segments, joined, preferred_element_type=jnp.float32).astype(
            jnp.bfloat16
        )
        real_bins.append(product[:, :bin_step])
        imag_bins.append(product[:, bin_step:])
    real_spec = jnp.concatenate(real_bins, axis=1)
    imag_spec = jnp.concatenate(imag_bins, axis=1)
    raw_spectra = jnp.stack([real_spec, imag_spec])
    tap_count = whiten_filter.shape[1]
    rim_width = tap_count // 2
    reach_rows = local_rows + tap_count
    skewed = jnp.pad(whiten_filter, ((0, 0), (0, local_rows + 1))).reshape(-1)
    band_matrix = skewed[: local_rows * reach_rows].reshape(local_rows, reach_rows)
    padded = extended(raw_spectra, ((("chan", "freq"), 1),), rim_width)
    predicted = jnp.einsum("ij,ajk->aik", band_matrix, padded, preferred_element_type=jnp.float32)
    whitened = (raw_spectra.astype(jnp.float32) - predicted).astype(jnp.bfloat16)
    spectra = whitened.reshape(2, local_rows, segment_count, FB)
    tm_count = lax.axis_size("tm")
    freq_count = lax.axis_size("freq")
    pieces = lax.all_to_all(spectra[None], ("tm", "freq"), split_axis=4, concat_axis=0, tiled=True)
    band_width = pieces.shape[-1]
    pieces = pieces.reshape(tm_count, freq_count, 2, local_rows, segment_count, band_width)
    banded = pieces.transpose(2, 1, 3, 0, 4, 5).reshape(
        2, freq_count * local_rows, tm_count * segment_count, band_width
    )
    block_rows = banded.shape[1]
    own_block = banded.reshape(2, block_rows, -1)
    depth = own_block.shape[2]
    scaling = 1.0 / math.sqrt(depth)
    block_index = lax.axis_index("chan")
    slot_list = pair_list[0]
    nearby = []
    for distance in range(-REACH, REACH + 1):
        if distance == 0:
            nearby.append(own_block)
        else:
            nearby.append(shifted(own_block, "chan", -distance))
    stacked = jnp.stack(nearby)

    def fetch_partner(partner_index):
        return lax.dynamic_index_in_dim(
            stacked, partner_index - block_index + REACH, 0, keepdims=False
        )

    left_side = jnp.concatenate([own_block[0], own_block[1]], axis=1)
    flipped = jnp.concatenate([own_block[1], -own_block[0]], axis=1)
    contract = (((1,), (1,)), ((), ()))

    def one_slot(partner_index):
        partner = fetch_partner(partner_index)
        right_side = jnp.concatenate([partner[0], partner[1]], axis=1)
        real_part = (
            lax.dot_general(left_side, right_side, contract, preferred_element_type=jnp.float32)
            * scaling
        )
        imag_part = (
            lax.dot_general(flipped, right_side, contract, preferred_element_type=jnp.float32)
            * scaling
        )
        crossed = jnp.stack([real_part, imag_part])
        return jnp.where(partner_index >= 0, crossed, jnp.zeros((), jnp.float32))

    result = jnp.stack([one_slot(slot_list[slot_index]) for slot_index in range(SLOTS)])
    return result.reshape(1, SLOTS, 1, 2, block_rows, block_rows)


MESH = pl.DeviceIdType.MESH
PIECES = 4
STEP = 32
SPECTRA_VMEM = 60 * 2**20
SLOT_VMEM = 4 * 2**20


def spectra_kernel(
    chan_count,
    scaling,
    rec_ref,
    trail_ref,
    filt_ref,
    crossed,
    samples,
    filters,
    bands,
    table,
    coarse,
    raw,
    gathered,
    turned,
    local_sems,
    span_sems,
    core_sems,
    pass_sems,
    filter_sems,
    swap_sems,
    block_sems,
):
    me = lax.axis_index("chan")
    tm = lax.axis_index("tm")
    core = lax.axis_index("freq")
    rows, hop = rec_ref.shape
    window = 2 * hop
    width = table.shape[1] // 2
    block_rows = 2 * rows
    taps = filt_ref.shape[0]
    rim = taps // 2
    piece = rows // PIECES
    has_left = me > 0
    has_right = me < chan_count - 1
    other = 1 - core
    other_tm = {"tm": 1 - tm}
    other_core = {"freq": 1 - core}
    left = {"chan": me - 1}
    right = {"chan": me + 1}

    def remote(source, target, sems, index, device):
        return pltpu.make_async_remote_copy(
            src_ref=source,
            dst_ref=target,
            send_sem=sems.at[(0,) + index],
            recv_sem=sems.at[(1,) + index],
            device_id=device,
            device_id_type=MESH,
        )

    def half(which):
        return pl.ds(pl.multiple_of(which * rows, rows), rows)

    barrier = pltpu.get_barrier_semaphore()
    pl.semaphore_signal(barrier, inc=1, device_id=other_tm, device_id_type=MESH)
    pl.semaphore_signal(barrier, inc=1, device_id=other_core, device_id_type=MESH)

    for near, neighbour in ((has_left, left), (has_right, right)):

        @pl.when(near)
        def _():
            pl.semaphore_signal(barrier, inc=1, device_id=neighbour, device_id_type=MESH)

    own_copies = [
        pltpu.make_async_copy(rec_ref, samples.at[tm, half(core)], local_sems.at[0]),
        pltpu.make_async_copy(trail_ref, samples.at[2, half(core)], local_sems.at[1]),
        pltpu.make_async_copy(filt_ref, filters.at[core, me], local_sems.at[2]),
    ]
    for copy in own_copies:
        copy.start()

    neighbours = 2 + has_left.astype(jnp.int32) + has_right.astype(jnp.int32)
    pl.semaphore_wait(barrier, neighbours)

    def piece_start(which, step):
        return pl.multiple_of(
            (1 - which) * step * piece + which * (PIECES - 1 - step) * piece, piece
        )

    def piece_in_block(which, step):
        start = which * rows + piece_start(which, step)
        return pl.ds(pl.multiple_of(start, piece), piece)

    span_copies = [
        remote(
            rec_ref.at[pl.ds(piece_start(core, p), piece)],
            samples.at[tm, piece_in_block(core, p)],
            span_sems,
            (p,),
            other_tm,
        )
        for p in range(PIECES)
    ]
    for copy in span_copies:
        copy.start()
    core_copies = [
        remote(rec_ref, samples.at[tm, half(core)], core_sems, (0,), other_core),
        remote(trail_ref, samples.at[2, half(core)], core_sems, (1,), other_core),
        remote(filt_ref, filters.at[core, me], core_sems, (2,), other_core),
    ]
    for copy in core_copies:
        copy.start()

    def exists(direction, distance):
        return me - distance >= 0 if direction == 0 else me + distance < chan_count

    ahead = (has_right, has_left)

    def weights_copy(direction, distance, sem):
        source = me - distance if direction == 0 else me + distance
        at = filters.at[core, jnp.clip(source, 0, chan_count - 1)]
        return remote(
            filt_ref if distance == 0 else at,
            at,
            filter_sems,
            (direction, sem),
            right if direction == 0 else left,
        )

    for direction in range(2):

        @pl.when(ahead[direction])
        def _():
            weights_copy(direction, 0, 0).start()

    first_bin = (tm * 2 + core) * width
    unit = 2.0 * math.pi / window
    bins = first_bin + lax.broadcasted_iota(jnp.int32, (1, width), 1)

    def angles(count, scale, factor):
        steps = scale * lax.broadcasted_iota(jnp.int32, (count, width), 0)
        return unit * jnp.bitwise_and(steps * factor, window - 1).astype(jnp.float32)

    parts = window // STEP
    coarse_angle = angles(parts, STEP, bins)
    coarse_turn = angles(parts, STEP, 1)
    coarse[0] = jnp.cos(coarse_angle)
    coarse[1] = jnp.sin(coarse_angle)
    coarse[2] = jnp.cos(coarse_turn)
    coarse[3] = jnp.sin(coarse_turn)
    fine_angle = angles(STEP, 1, bins)
    fine_turn = angles(STEP, 1, 1)
    fine_cos, fine_sin = jnp.cos(fine_angle), jnp.sin(fine_angle)
    turn_cos, turn_sin = jnp.cos(fine_turn), jnp.sin(fine_turn)
    normaliser = 1.0 / math.sqrt(0.375 * window)

    def fill(part, carry):
        c, s, tc, ts = (coarse[k, pl.ds(part, 1), :] for k in range(4))
        taper = (0.5 - 0.5 * (tc * turn_cos - ts * turn_sin)) * normaliser
        at = pl.ds(pl.multiple_of(part * STEP, STEP), STEP)
        table[at, :width] = (taper * (c * fine_cos - s * fine_sin)).astype(jnp.bfloat16)
        table[at, width:] = (-taper * (s * fine_cos + c * fine_sin)).astype(jnp.bfloat16)
        return carry

    lax.fori_loop(0, parts, fill, 0)

    edge = jnp.zeros((rim, raw.shape[1]), raw.dtype)
    raw[0:rim] = edge
    raw[rim + chan_count * block_rows :] = edge

    for copy in own_copies:
        copy.wait()
    remote(rec_ref, samples.at[tm, half(other)], core_sems, (0,), other_core).wait_recv()
    remote(trail_ref, samples.at[2, half(other)], core_sems, (1,), other_core).wait_recv()

    def own_rows(block, start, count):
        return pl.ds(pl.multiple_of(rim + block * block_rows + start, piece), count)

    tiers = [(0, 0)]
    for p in range(1, PIECES):
        tiers += [(0, p), (1, p - 1)]
    tiers.append((1, PIECES - 1))

    def block_copy(direction, distance, tier, sem):
        which, p = tiers[tier]
        here = core if which == 0 else other
        source = me - distance if direction == 0 else me + distance
        source = jnp.clip(source, 0, chan_count - 1)
        at = raw.at[own_rows(source, here * rows + piece_start(here, p), piece)]
        return remote(at, at, block_sems, (direction, sem, tier), right if direction == 0 else left)

    def outgoing(direction, distance, tier):
        return block_copy(direction, distance, tier, distance)

    def landed(direction, distance, tier):
        return block_copy(direction, distance, tier, distance - 1)

    def transform(which, p, tier):
        at = which * rows + piece_start(which, p)
        chosen = pl.ds(pl.multiple_of(at, piece), piece)
        product = jnp.dot(
            samples[0:2, chosen].reshape(2 * piece, hop),
            table[:hop],
            preferred_element_type=jnp.float32,
        ) + jnp.dot(
            samples[1:3, chosen].reshape(2 * piece, hop),
            table[hop:],
            preferred_element_type=jnp.float32,
        )
        product = product.astype(jnp.bfloat16)
        where = own_rows(me, at, piece)
        for segment in range(2):
            found = product[segment * piece : (segment + 1) * piece]
            raw[where, segment * width : (segment + 1) * width] = found[:, :width]
            raw[where, (2 + segment) * width : (3 + segment) * width] = found[:, width:]
        for direction in range(2):

            @pl.when(ahead[direction])
            def _():
                outgoing(direction, 0, tier).start()

    pass_copies = []
    for tier, (which, p) in enumerate(tiers):
        if which == 0:
            mine = samples.at[1 - tm, piece_in_block(core, p)]
            remote(mine, mine, span_sems, (p,), other_tm).wait_recv()
            passing = remote(mine, mine, pass_sems, (p,), other_core)
            passing.start()
            pass_copies.append(passing)
            transform(core, p, tier)
        else:
            theirs = samples.at[1 - tm, piece_in_block(other, p)]
            remote(theirs, theirs, pass_sems, (p,), other_core).wait_recv()
            transform(other, p, tier)

    remote(filt_ref, filters.at[other, me], core_sems, (2,), other_core).wait_recv()

    def swapped(which, direction, distance):
        source = me - distance if direction == 0 else me + distance
        at = filters.at[which, jnp.clip(source, 0, chan_count - 1)]
        return remote(at, at, swap_sems, (direction, distance - 1), other_core)

    def take_weights(direction, distance):
        @pl.when(exists(direction, distance))
        def _():
            weights_copy(direction, distance, distance - 1).wait_recv()
            swapped(core, direction, distance).start()

        @pl.when(jnp.logical_and(exists(direction, distance), ahead[direction]))
        def _():
            weights_copy(direction, distance, distance).start()

    def spread(block):
        for which in range(2):
            weights = jnp.transpose(filters[which, block].astype(jnp.float32))
            wide = jnp.concatenate([weights, jnp.zeros((rows, 128 - taps), jnp.float32)], axis=1)
            for p in range(PIECES):
                rolled = pltpu.roll(
                    wide[p * piece : (p + 1) * piece], 0, 1, stride=1, stride_axis=0
                )
                bands[block, which * PIECES + p] = rolled.astype(jnp.bfloat16)

    spread(me)

    def whiten(block, tile):
        start = pl.multiple_of(block * block_rows + tile * piece, piece)
        near = raw[pl.ds(start, piece + taps)]
        predicted = jnp.dot(
            bands[block, tile][:, : piece + taps], near, preferred_element_type=jnp.float32
        )
        mine = near[rim : rim + piece].astype(jnp.float32)
        gathered[block, tile * piece : (tile + 1) * piece] = (mine - predicted).astype(
            jnp.bfloat16
        )

    contract = (((1,), (1,)), ((), ()))

    def cross(block):
        partner = gathered[block]
        for part, side in enumerate((gathered[me], turned[...])):
            crossed[block, part] = (
                lax.dot_general(side, partner, contract, preferred_element_type=jnp.float32)
                * scaling
            )

    tile_count = 2 * PIECES
    for tile in range(1, tile_count - 1):
        whiten(me, tile)

    def finish_own():
        whiten(me, 0)
        whiten(me, tile_count - 1)
        own = gathered[me]
        middle = own.shape[1] // 2
        turned[...] = jnp.concatenate([own[:, middle:], -own[:, :middle]], axis=1)
        cross(me)

    def finish(direction, distance):
        @pl.when(exists(direction, distance))
        def _():
            block = me - distance if direction == 0 else me + distance
            whiten(block, 0 if direction == 0 else tile_count - 1)
            cross(block)

    furthest = chan_count - 1
    for distance in range(1, chan_count):
        for direction in range(2):
            take_weights(direction, distance)
        for tier in range(len(tiers)):
            for direction in range(2):

                @pl.when(exists(direction, distance))
                def _():
                    landed(direction, distance, tier).wait_recv()

                if distance < furthest:

                    @pl.when(jnp.logical_and(exists(direction, distance), ahead[direction]))
                    def _():
                        outgoing(direction, distance, tier).start()

            if tier == PIECES:
                for direction in range(2):

                    @pl.when(exists(direction, distance))
                    def _():
                        swapped(other, direction, distance).wait_recv()
                        spread(me - distance if direction == 0 else me + distance)

                if distance == 1:
                    finish_own()
                else:
                    for direction in range(2):
                        finish(direction, distance - 1)

        for direction in range(2):

            @pl.when(exists(direction, distance))
            def _():
                block = me - distance if direction == 0 else me + distance
                for tile in range(tile_count - 1):
                    whiten(block, tile + 1 if direction == 0 else tile)

    for direction in range(2):
        finish(direction, furthest)

    for copy in span_copies + core_copies + pass_copies:
        copy.wait_send()

    for distance in range(chan_count):
        for direction in range(2):
            if distance > 0:

                @pl.when(exists(direction, distance))
                def _():
                    swapped(core, direction, distance).wait_send()

            if distance < furthest:

                @pl.when(jnp.logical_and(exists(direction, distance), ahead[direction]))
                def _():
                    weights_copy(direction, distance, distance).wait_send()

        for tier in range(len(tiers)):
            for direction in range(2):

                @pl.when(jnp.logical_and(exists(direction, distance), ahead[direction]))
                def _():
                    outgoing(direction, distance, tier).wait_send()


def slot_kernel(pairs_ref, crossed, out_ref, blank, sems):
    def store(slot, source):
        return pltpu.make_async_copy(source, out_ref.at[0, slot, 0], sems.at[slot])

    for slot in range(SLOTS):

        @pl.when(pairs_ref[0, slot] >= 0)
        def _():
            store(slot, crossed.at[jnp.maximum(pairs_ref[0, slot], 0)]).start()

    blank[...] = jnp.zeros(blank.shape, blank.dtype)

    for slot in range(SLOTS):

        @pl.when(pairs_ref[0, slot] < 0)
        def _():
            store(slot, blank).start()

    for slot in range(SLOTS):
        store(slot, blank).wait()


def fused(recording, trailing, whiten_filter, pair_list):
    rows, hop = recording.shape
    chan_count = lax.axis_size("chan")
    taps = whiten_filter.shape[1]
    width = FB // (lax.axis_size("tm") * lax.axis_size("freq"))
    block_rows = 2 * rows
    depth = 2 * width
    vmem = pl.BlockSpec(memory_space=pltpu.VMEM)
    hbm = pl.BlockSpec(memory_space=pltpu.HBM)
    crossed = pl.pallas_call(
        functools.partial(spectra_kernel, chan_count, 1.0 / math.sqrt(depth)),
        out_shape=pltpu.VMEM((chan_count, 2, block_rows, block_rows), jnp.float32),
        in_specs=[hbm] * 3,
        out_specs=vmem,
        scratch_shapes=[
            pltpu.VMEM((3, block_rows, hop), jnp.bfloat16),
            pltpu.VMEM((2, chan_count, taps, rows), jnp.bfloat16),
            pltpu.VMEM((chan_count, 2 * PIECES, rows // PIECES, 128), jnp.bfloat16),
            pltpu.VMEM((2 * hop, 2 * width), jnp.bfloat16),
            pltpu.VMEM((4, 2 * hop // STEP, width), jnp.float32),
            pltpu.VMEM((chan_count * block_rows + taps, 2 * depth), jnp.bfloat16),
            pltpu.VMEM((chan_count, block_rows, 2 * depth), jnp.bfloat16),
            pltpu.VMEM((block_rows, 2 * depth), jnp.bfloat16),
            pltpu.SemaphoreType.DMA((3,)),
            pltpu.SemaphoreType.DMA((2, PIECES)),
            pltpu.SemaphoreType.DMA((2, 3)),
            pltpu.SemaphoreType.DMA((2, PIECES)),
            pltpu.SemaphoreType.DMA((2, 2, chan_count - 1)),
            pltpu.SemaphoreType.DMA((2, 2, chan_count - 1)),
            pltpu.SemaphoreType.DMA((2, 2, chan_count - 1, 2 * PIECES)),
        ],
        compiler_params=pltpu.CompilerParams(collective_id=0, has_side_effects=True, vmem_limit_bytes=SPECTRA_VMEM),
    )(recording, trailing, whiten_filter.T)
    return pl.pallas_call(
        slot_kernel,
        out_shape=jax.ShapeDtypeStruct((1, SLOTS, 1, 2, block_rows, block_rows), jnp.float32),
        in_specs=[pl.BlockSpec(memory_space=pltpu.SMEM), vmem],
        out_specs=hbm,
        scratch_shapes=[
            pltpu.VMEM((2, block_rows, block_rows), jnp.float32),
            pltpu.SemaphoreType.DMA((SLOTS,)),
        ],
        compiler_params=pltpu.CompilerParams(vmem_limit_bytes=SLOT_VMEM),
    )(pair_list, crossed)


def local(recording, trailing, whiten_filter, pair_list):
    shapes = (recording.shape, trailing.shape, whiten_filter.shape)
    counts = (lax.axis_size("tm"), lax.axis_size("freq"))
    whole_reach = 1 < lax.axis_size("chan") <= REACH + 1
    if shapes == ((128, 1024), (128, 1024), (128, 64)) and counts == (2, 2) and whole_reach:
        return fused(recording, trailing, whiten_filter, pair_list)
    return general(recording, trailing, whiten_filter, pair_list)


def solution(mesh):
    placed = (
        P(("days", "chan", "freq"), "tm"),
        P(("days", "chan", "freq"), None),
        P(("chan", "freq"), None),
        P(("days", "chan"), None),
    )
    return jax.shard_map(
        local,
        mesh=mesh,
        in_specs=placed,
        out_specs=P(("days", "chan"), None, ("tm", "freq"), None, None, None),
        check_vma=False,
    )
```

```python
import functools
import math

import jax
import jax.numpy as jnp
from jax import lax
from jax.experimental import pallas as pl
from jax.experimental.pallas import tpu as pltpu
from jax.sharding import PartitionSpec as P

FB = 512
REACH = 3
SLOTS = 4


def shifted(block, axis, distance):
    devices = range(lax.axis_size(axis))
    route = [(i - distance, i) for i in devices if i - distance in devices]
    return lax.ppermute(block, axis, route)


def extended(value, sides, width):
    for axis, dim in sides:
        size, length = (lax.axis_size(axis), value.shape[dim])
        up = [(i, (i + 1) % size) for i in range(size - 1)]
        down = [(j, i) for i, j in up]
        last = lax.slice_in_dim(value, length - width, length, axis=dim)
        initial = lax.slice_in_dim(value, 0, width, axis=dim)
        before = lax.ppermute(last, axis, up)
        after = lax.ppermute(initial, axis, down)
        value = jnp.concatenate([before, value, after], axis=dim)
    return value


def fourier_table(first_bin, bin_count, length):
    samples = jnp.arange(length, dtype=jnp.int32)[:, None]
    bin_index = first_bin + jnp.arange(bin_count, dtype=jnp.int32)[None, :]
    phase = samples * bin_index % length
    angle = 2.0 * math.pi / length * phase.astype(jnp.float32)
    taper = 0.5 - 0.5 * jnp.cos(
        2.0 * math.pi / length * jnp.arange(length, dtype=jnp.int32).astype(jnp.float32)
    )
    normaliser = 1.0 / math.sqrt(0.375 * length)
    cosine = (taper[:, None] * jnp.cos(angle) * normaliser).astype(jnp.bfloat16)
    sine_table = (-taper[:, None] * jnp.sin(angle) * normaliser).astype(jnp.bfloat16)
    return (cosine, sine_table)


def general(recording, trailing, whiten_filter, pair_list):
    local_rows, local_span = recording.shape
    hop_size = trailing.shape[1]
    window_size = 2 * hop_size
    segment_count = local_span // hop_size
    following = shifted(recording, "tm", -1)
    is_last = lax.axis_index("tm") == lax.axis_size("tm") - 1
    following = jnp.where(is_last, trailing, following)
    signal = jnp.concatenate([recording, following], axis=1)
    segments = jnp.stack([signal], axis=1)
    stacked_segments = segments.reshape(local_rows * segment_count, window_size)
    bin_step = min(256, FB)
    real_bins = []
    imag_bins = []
    for first_bin in range(0, FB, bin_step):
        cosine, sine_table = fourier_table(first_bin, bin_step, window_size)
        joined = jnp.concatenate([cosine, sine_table], axis=1)
        product = jnp.dot(stacked_segments, joined, preferred_element_type=jnp.float32).astype(
            jnp.bfloat16
        )
        real_bins.append(product[:, :bin_step])
        imag_bins.append(product[:, bin_step:])
    real_spec = jnp.concatenate(real_bins, axis=1)
    imag_spec = jnp.concatenate(imag_bins, axis=1)
    raw_spectra = jnp.stack([real_spec, imag_spec])
    tap_count = whiten_filter.shape[1]
    rim_width = tap_count // 2
    reach_rows = local_rows + tap_count
    skewed = jnp.pad(whiten_filter, ((0, 0), (0, local_rows + 1))).reshape(-1)
    band_matrix = skewed[: local_rows * reach_rows].reshape(local_rows, reach_rows)
    padded = extended(raw_spectra, ((("chan", "freq"), 1),), rim_width)
    predicted = jnp.einsum("ij,ajk->aik", band_matrix, padded, preferred_element_type=jnp.float32)
    whitened = (raw_spectra.astype(jnp.float32) - predicted).astype(jnp.bfloat16)
    spectra = whitened.reshape(2, local_rows, segment_count, FB)
    tm_count = lax.axis_size("tm")
    freq_count = lax.axis_size("freq")
    pieces = lax.all_to_all(spectra[None], ("tm", "freq"), split_axis=4, concat_axis=0, tiled=True)
    band_width = pieces.shape[-1]
    pieces = pieces.reshape(tm_count, freq_count, 2, local_rows, segment_count, band_width)
    banded = pieces.transpose(2, 1, 3, 0, 4, 5).reshape(
        2, freq_count * local_rows, tm_count * segment_count, band_width
    )
    block_rows = banded.shape[1]
    own_block = banded.reshape(2, block_rows, -1)
    depth = own_block.shape[2]
    scaling = 1.0 / math.sqrt(depth)
    block_index = lax.axis_index("chan")
    slot_list = pair_list[0]
    nearby = []
    for distance in range(-REACH, REACH + 1):
        if distance == 0:
            nearby.append(own_block)
        else:
            nearby.append(shifted(own_block, "chan", -distance))
    stacked = jnp.stack(nearby)

    def fetch_partner(partner_index):
        return lax.dynamic_index_in_dim(
            stacked, partner_index - block_index + REACH, 0, keepdims=False
        )

    left_side = jnp.concatenate([own_block[0], own_block[1]], axis=1)
    flipped = jnp.concatenate([own_block[1], -own_block[0]], axis=1)
    contract = (((1,), (1,)), ((), ()))

    def one_slot(partner_index):
        partner = fetch_partner(partner_index)
        right_side = jnp.concatenate([partner[0], partner[1]], axis=1)
        real_part = (
            lax.dot_general(left_side, right_side, contract, preferred_element_type=jnp.float32)
            * scaling
        )
        imag_part = (
            lax.dot_general(flipped, right_side, contract, preferred_element_type=jnp.float32)
            * scaling
        )
        crossed = jnp.stack([real_part, imag_part])
        return jnp.where(partner_index >= 0, crossed, jnp.zeros((), jnp.float32))

    result = jnp.stack([one_slot(slot_list[slot_index]) for slot_index in range(SLOTS)])
    return result.reshape(1, SLOTS, 1, 2, block_rows, block_rows)


MESH = pl.DeviceIdType.MESH
PIECES = 4
STEP = 32
SPECTRA_VMEM = 60 * 2**20
SLOT_VMEM = 4 * 2**20


def spectra_kernel(
    chan_count,
    scaling,
    rec_ref,
    trail_ref,
    filt_ref,
    crossed,
    samples,
    filters,
    bands,
    table,
    coarse,
    raw,
    gathered,
    turned,
    local_sems,
    send_sems,
    span_sems,
    pass_sems,
    core_sems,
    filter_sems,
    block_sems,
):
    me = lax.axis_index("chan")
    tm = lax.axis_index("tm")
    core = lax.axis_index("freq")
    rows, hop = rec_ref.shape
    window = 2 * hop
    width = table.shape[1] // 2
    block_rows = 2 * rows
    taps = filt_ref.shape[0]
    rim = taps // 2
    piece = rows // PIECES
    group = piece * PIECES // 2
    furthest = chan_count - 1
    has_left = me > 0
    has_right = me < chan_count - 1
    other = 1 - core
    other_tm = {"tm": 1 - tm}
    other_core = {"freq": 1 - core}
    left = {"chan": me - 1}
    right = {"chan": me + 1}
    ahead = (has_right, has_left)
    onward = (right, left)
    span_send, pass_send, core_send, swap_send = range(4)
    filter_send, block_send = (4, 5), (6, 7)

    def remote(source, target, send, recv, device):
        return pltpu.make_async_remote_copy(
            src_ref=source,
            dst_ref=target,
            send_sem=send_sems.at[send],
            recv_sem=recv,
            device_id=device,
            device_id_type=MESH,
        )

    def half(which):
        return pl.ds(pl.multiple_of(which * rows, rows), rows)

    barrier = pltpu.get_barrier_semaphore()
    pl.semaphore_signal(barrier, inc=1, device_id=other_tm, device_id_type=MESH)
    pl.semaphore_signal(barrier, inc=1, device_id=other_core, device_id_type=MESH)

    for near, neighbour in zip(ahead, onward):

        @pl.when(near)
        def _():
            pl.semaphore_signal(barrier, inc=1, device_id=neighbour, device_id_type=MESH)

    own_copies = [
        pltpu.make_async_copy(rec_ref, samples.at[tm, half(core)], local_sems.at[0]),
        pltpu.make_async_copy(trail_ref, samples.at[2, half(core)], local_sems.at[1]),
        pltpu.make_async_copy(filt_ref, filters.at[core, me], local_sems.at[2]),
    ]
    for copy in own_copies:
        copy.start()

    neighbours = 2 + has_left.astype(jnp.int32) + has_right.astype(jnp.int32)
    pl.semaphore_wait(barrier, neighbours)

    def piece_start(which, step):
        return pl.multiple_of(
            (1 - which) * step * piece + which * (PIECES - 1 - step) * piece, piece
        )

    def piece_in_block(which, step):
        start = which * rows + piece_start(which, step)
        return pl.ds(pl.multiple_of(start, piece), piece)

    def span_copy(p):
        return remote(
            rec_ref.at[pl.ds(piece_start(core, p), piece)],
            samples.at[tm, piece_in_block(core, p)],
            span_send,
            span_sems.at[p],
            other_tm,
        )

    for p in range(PIECES):
        span_copy(p).start()

    def core_copy(index, which):
        source, place = ((rec_ref, tm), (trail_ref, 2))[index]
        at = samples.at[place, half(which)]
        return remote(source, at, core_send, core_sems.at[index], other_core)

    for index in range(2):
        core_copy(index, core).start()

    def source_of(direction, distance):
        source = me - distance if direction == 0 else me + distance
        return jnp.clip(source, 0, chan_count - 1)

    def exists(direction, distance):
        return me - distance >= 0 if direction == 0 else me + distance < chan_count

    def weights_copy(direction, distance, sem):
        at = filters.at[core, source_of(direction, distance)]
        return remote(
            filt_ref if distance == 0 else at,
            at,
            filter_send[direction],
            filter_sems.at[direction, sem],
            onward[direction],
        )

    for direction in range(2):

        @pl.when(ahead[direction])
        def _():
            weights_copy(direction, 0, 0).start()

    first_bin = (tm * 2 + core) * width
    unit = 2.0 * math.pi / window
    bins = first_bin + lax.broadcasted_iota(jnp.int32, (1, width), 1)

    def angles(count, scale, factor):
        steps = scale * lax.broadcasted_iota(jnp.int32, (count, width), 0)
        return unit * jnp.bitwise_and(steps * factor, window - 1).astype(jnp.float32)

    parts = window // STEP
    coarse_angle = angles(parts, STEP, bins)
    coarse_turn = angles(parts, STEP, 1)
    coarse[0] = jnp.cos(coarse_angle)
    coarse[1] = jnp.sin(coarse_angle)
    coarse[2] = jnp.cos(coarse_turn)
    coarse[3] = jnp.sin(coarse_turn)
    fine_angle = angles(STEP, 1, bins)
    fine_turn = angles(STEP, 1, 1)
    fine_cos, fine_sin = jnp.cos(fine_angle), jnp.sin(fine_angle)
    turn_cos, turn_sin = jnp.cos(fine_turn), jnp.sin(fine_turn)
    normaliser = 1.0 / math.sqrt(0.375 * window)

    def fill(part, carry):
        c, s, tc, ts = (coarse[k, pl.ds(part, 1), :] for k in range(4))
        taper = (0.5 - 0.5 * (tc * turn_cos - ts * turn_sin)) * normaliser
        at = pl.ds(pl.multiple_of(part * STEP, STEP), STEP)
        table[at, :width] = (taper * (c * fine_cos - s * fine_sin)).astype(jnp.bfloat16)
        table[at, width:] = (-taper * (s * fine_cos + c * fine_sin)).astype(jnp.bfloat16)
        return carry

    lax.fori_loop(0, parts, fill, 0)

    edge = jnp.zeros((rim, raw.shape[1]), raw.dtype)
    raw[0:rim] = edge
    raw[rim + chan_count * block_rows :] = edge

    for copy in own_copies:
        copy.wait()
    for index in range(2):
        core_copy(index, other).wait_recv()

    def own_rows(block, start, count):
        return pl.ds(pl.multiple_of(rim + block * block_rows + start, piece), count)

    groups = [(0, 0), (1, 0), (0, 1), (1, 1)]

    def block_copy(at, direction, distance, index):
        place = raw.at[at]
        return remote(
            place,
            place,
            block_send[direction],
            block_sems.at[direction, distance, index],
            onward[direction],
        )

    def group_rows(direction, distance, index):
        which, step = groups[index]
        here = core if which == 0 else other
        start = here * rows + (1 - here) * step * group + here * (1 - step) * group
        return own_rows(source_of(direction, distance), start, group)

    def transform(which, p, index):
        at = which * rows + piece_start(which, p)
        chosen = pl.ds(pl.multiple_of(at, piece), piece)
        product = jnp.dot(
            samples[0:2, chosen].reshape(2 * piece, hop),
            table[:hop],
            preferred_element_type=jnp.float32,
        ) + jnp.dot(
            samples[1:3, chosen].reshape(2 * piece, hop),
            table[hop:],
            preferred_element_type=jnp.float32,
        )
        product = product.astype(jnp.bfloat16)
        where = own_rows(me, at, piece)
        for segment in range(2):
            found = product[segment * piece : (segment + 1) * piece]
            raw[where, segment * width : (segment + 1) * width] = found[:, :width]
            raw[where, (2 + segment) * width : (3 + segment) * width] = found[:, width:]
        for direction in range(2):

            @pl.when(ahead[direction])
            def _():
                block_copy(where, direction, 0, index).start()

    def take_weights(distance):
        for direction in range(2):

            @pl.when(exists(direction, distance))
            def _():
                weights_copy(direction, distance, distance - 1).wait_recv()

            if distance < furthest:

                @pl.when(jnp.logical_and(exists(direction, distance), ahead[direction]))
                def _():
                    weights_copy(direction, distance, distance).start()

    def passed(which, p):
        at = samples.at[1 - tm, piece_in_block(which, p)]
        return remote(at, at, pass_send, pass_sems.at[p], other_core)

    tiers = [(0, 0)]
    for p in range(1, PIECES):
        tiers += [(0, p), (1, p - 1)]
    tiers.append((1, PIECES - 1))
    for which, p in tiers:
        index = groups.index((which, 2 * p // PIECES))
        if which == 0:
            span_copy(p).wait_recv()
            passed(core, p).start()
            transform(core, p, index)
        else:
            passed(other, p).wait_recv()
            transform(other, p, index)
        if (which, p) == (0, 2):
            take_weights(1)

    take_weights(2)

    def spread(block, carry):
        for which in range(2):
            weights = jnp.transpose(filters[which, block].astype(jnp.float32))
            wide = jnp.concatenate([weights, jnp.zeros((rows, 128 - taps), jnp.float32)], axis=1)
            for p in range(PIECES):
                rolled = pltpu.roll(
                    wide[p * piece : (p + 1) * piece], 0, 1, stride=1, stride_axis=0
                )
                bands[block, which * PIECES + p] = rolled.astype(jnp.bfloat16)
        return carry

    def whiten(block, tile):
        start = pl.multiple_of(block * block_rows + tile * piece, piece)
        near = raw[pl.ds(start, piece + taps)]
        predicted = jnp.dot(
            bands[block, tile][:, : piece + taps], near, preferred_element_type=jnp.float32
        )
        mine = near[rim : rim + piece].astype(jnp.float32)
        gathered[block, tile * piece : (tile + 1) * piece] = (mine - predicted).astype(
            jnp.bfloat16
        )

    contract = (((1,), (1,)), ((), ()))

    def cross(block):
        partner = gathered[block]
        for part, side in enumerate((gathered[me], turned[...])):
            crossed[block, part] = (
                lax.dot_general(side, partner, contract, preferred_element_type=jnp.float32)
                * scaling
            )

    tile_count = 2 * PIECES

    def finish_own():
        for tile in range(tile_count):
            whiten(me, tile)
        own = gathered[me]
        middle = own.shape[1] // 2
        turned[...] = jnp.concatenate([own[:, middle:], -own[:, :middle]], axis=1)
        cross(me)

    def inner(distance):
        for direction in range(2):

            @pl.when(exists(direction, distance))
            def _():
                block = me - distance if direction == 0 else me + distance
                for tile in range(tile_count - 1):
                    whiten(block, tile + 1 if direction == 0 else tile)

    def finish(distance):
        for direction in range(2):

            @pl.when(exists(direction, distance))
            def _():
                block = me - distance if direction == 0 else me + distance
                whiten(block, 0 if direction == 0 else tile_count - 1)
                cross(block)

    def arrive(distance, index):
        for direction in range(2):
            at = group_rows(direction, distance, index)

            @pl.when(exists(direction, distance))
            def _():
                block_copy(at, direction, distance - 1, index).wait_recv()

            if distance < furthest:

                @pl.when(jnp.logical_and(exists(direction, distance), ahead[direction]))
                def _():
                    block_copy(at, direction, distance, index).start()

    def swap(which):
        at = filters.at[which]
        return remote(at, at, swap_send, core_sems.at[2], other_core)

    for index in range(4):
        arrive(1, index)
    take_weights(3)
    swap(core).start()
    arrive(2, 0)
    arrive(2, 1)
    swap(other).wait_recv()
    lax.fori_loop(0, chan_count, spread, 0)
    arrive(2, 2)
    finish_own()
    arrive(2, 3)
    inner(1)
    finish(1)
    inner(2)
    for index in range(4):
        arrive(3, index)
    finish(2)
    inner(3)
    finish(3)

    whole = samples.at[tm, half(core)]
    remote(whole, whole, span_send, span_sems.at[0], other_tm).wait_send()
    remote(whole, whole, pass_send, pass_sems.at[0], other_core).wait_send()
    both = samples.at[0:2, half(core)]
    remote(both, both, core_send, core_sems.at[0], other_core).wait_send()
    swap(core).wait_send()

    for direction in range(2):
        for count in range(1, chan_count):

            @pl.when(me == (count - 1 if direction == 0 else chan_count - count))
            def _():
                sent = filters.at[core, 0:count]
                remote(
                    sent, sent, filter_send[direction], filter_sems.at[0, 0], onward[direction]
                ).wait_send()
                sent = raw.at[0 : count * block_rows]
                remote(
                    sent, sent, block_send[direction], block_sems.at[0, 0, 0], onward[direction]
                ).wait_send()


def slot_kernel(pairs_ref, crossed, out_ref, blank, sems):
    def store(slot, source):
        return pltpu.make_async_copy(source, out_ref.at[0, slot, 0], sems.at[slot])

    for slot in range(SLOTS):

        @pl.when(pairs_ref[0, slot] >= 0)
        def _():
            store(slot, crossed.at[jnp.maximum(pairs_ref[0, slot], 0)]).start()

    blank[...] = jnp.zeros(blank.shape, blank.dtype)

    for slot in range(SLOTS):

        @pl.when(pairs_ref[0, slot] < 0)
        def _():
            store(slot, blank).start()

    for slot in range(SLOTS):
        store(slot, blank).wait()


def fused(recording, trailing, whiten_filter, pair_list):
    rows, hop = recording.shape
    chan_count = lax.axis_size("chan")
    taps = whiten_filter.shape[1]
    width = FB // (lax.axis_size("tm") * lax.axis_size("freq"))
    block_rows = 2 * rows
    depth = 2 * width
    vmem = pl.BlockSpec(memory_space=pltpu.VMEM)
    hbm = pl.BlockSpec(memory_space=pltpu.HBM)
    crossed = pl.pallas_call(
        functools.partial(spectra_kernel, chan_count, 1.0 / math.sqrt(depth)),
        out_shape=pltpu.VMEM((chan_count, 2, block_rows, block_rows), jnp.float32),
        in_specs=[hbm] * 3,
        out_specs=vmem,
        scratch_shapes=[
            pltpu.VMEM((3, block_rows, hop), jnp.bfloat16),
            pltpu.VMEM((2, chan_count, taps, rows), jnp.bfloat16),
            pltpu.VMEM((chan_count, 2 * PIECES, rows // PIECES, 128), jnp.bfloat16),
            pltpu.VMEM((2 * hop, 2 * width), jnp.bfloat16),
            pltpu.VMEM((4, 2 * hop // STEP, width), jnp.float32),
            pltpu.VMEM((chan_count * block_rows + taps, 2 * depth), jnp.bfloat16),
            pltpu.VMEM((chan_count, block_rows, 2 * depth), jnp.bfloat16),
            pltpu.VMEM((block_rows, 2 * depth), jnp.bfloat16),
            pltpu.SemaphoreType.DMA((3,)),
            pltpu.SemaphoreType.DMA((8,)),
            pltpu.SemaphoreType.DMA((PIECES,)),
            pltpu.SemaphoreType.DMA((PIECES,)),
            pltpu.SemaphoreType.DMA((3,)),
            pltpu.SemaphoreType.DMA((2, chan_count - 1)),
            pltpu.SemaphoreType.DMA((2, chan_count - 1, 4)),
        ],
        compiler_params=pltpu.CompilerParams(
            collective_id=0, has_side_effects=True, vmem_limit_bytes=SPECTRA_VMEM
        ),
    )(recording, trailing, whiten_filter.T)
    return pl.pallas_call(
        slot_kernel,
        out_shape=jax.ShapeDtypeStruct((1, SLOTS, 1, 2, block_rows, block_rows), jnp.float32),
        in_specs=[pl.BlockSpec(memory_space=pltpu.SMEM), vmem],
        out_specs=hbm,
        scratch_shapes=[
            pltpu.VMEM((2, block_rows, block_rows), jnp.float32),
            pltpu.SemaphoreType.DMA((SLOTS,)),
        ],
        compiler_params=pltpu.CompilerParams(vmem_limit_bytes=SLOT_VMEM),
    )(pair_list, crossed)


def local(recording, trailing, whiten_filter, pair_list):
    shapes = (recording.shape, trailing.shape, whiten_filter.shape)
    counts = (lax.axis_size("tm"), lax.axis_size("freq"))
    whole_reach = lax.axis_size("chan") == REACH + 1
    if shapes == ((128, 1024), (128, 1024), (128, 64)) and counts == (2, 2) and whole_reach:
        return fused(recording, trailing, whiten_filter, pair_list)
    return general(recording, trailing, whiten_filter, pair_list)


def solution(mesh):
    placed = (
        P(("days", "chan", "freq"), "tm"),
        P(("days", "chan", "freq"), None),
        P(("chan", "freq"), None),
        P(("days", "chan"), None),
    )
    return jax.shard_map(
        local,
        mesh=mesh,
        in_specs=placed,
        out_specs=P(("days", "chan"), None, ("tm", "freq"), None, None, None),
        check_vma=False,
    )
```

```python
import functools
import math

import jax
import jax.numpy as jnp
from jax import lax
from jax.experimental import pallas as pl
from jax.experimental.pallas import tpu as pltpu
from jax.sharding import PartitionSpec as P

FB = 512
REACH = 3
SLOTS = 4


def shifted(block, axis, distance):
    devices = range(lax.axis_size(axis))
    route = [(i - distance, i) for i in devices if i - distance in devices]
    return lax.ppermute(block, axis, route)


def extended(value, sides, width):
    for axis, dim in sides:
        size, length = (lax.axis_size(axis), value.shape[dim])
        up = [(i, (i + 1) % size) for i in range(size - 1)]
        down = [(j, i) for i, j in up]
        last = lax.slice_in_dim(value, length - width, length, axis=dim)
        initial = lax.slice_in_dim(value, 0, width, axis=dim)
        before = lax.ppermute(last, axis, up)
        after = lax.ppermute(initial, axis, down)
        value = jnp.concatenate([before, value, after], axis=dim)
    return value


def fourier_table(first_bin, bin_count, length):
    samples = jnp.arange(length, dtype=jnp.int32)[:, None]
    bin_index = first_bin + jnp.arange(bin_count, dtype=jnp.int32)[None, :]
    phase = samples * bin_index % length
    angle = 2.0 * math.pi / length * phase.astype(jnp.float32)
    taper = 0.5 - 0.5 * jnp.cos(
        2.0 * math.pi / length * jnp.arange(length, dtype=jnp.int32).astype(jnp.float32)
    )
    normaliser = 1.0 / math.sqrt(0.375 * length)
    cosine = (taper[:, None] * jnp.cos(angle) * normaliser).astype(jnp.bfloat16)
    sine_table = (-taper[:, None] * jnp.sin(angle) * normaliser).astype(jnp.bfloat16)
    return (cosine, sine_table)


def general(recording, trailing, whiten_filter, pair_list):
    local_rows, local_span = recording.shape
    hop_size = trailing.shape[1]
    window_size = 2 * hop_size
    segment_count = local_span // hop_size
    following = shifted(recording, "tm", -1)
    is_last = lax.axis_index("tm") == lax.axis_size("tm") - 1
    following = jnp.where(is_last, trailing, following)
    signal = jnp.concatenate([recording, following], axis=1)
    segments = jnp.stack([signal], axis=1)
    stacked_segments = segments.reshape(local_rows * segment_count, window_size)
    bin_step = min(256, FB)
    real_bins = []
    imag_bins = []
    for first_bin in range(0, FB, bin_step):
        cosine, sine_table = fourier_table(first_bin, bin_step, window_size)
        joined = jnp.concatenate([cosine, sine_table], axis=1)
        product = jnp.dot(stacked_segments, joined, preferred_element_type=jnp.float32).astype(
            jnp.bfloat16
        )
        real_bins.append(product[:, :bin_step])
        imag_bins.append(product[:, bin_step:])
    real_spec = jnp.concatenate(real_bins, axis=1)
    imag_spec = jnp.concatenate(imag_bins, axis=1)
    raw_spectra = jnp.stack([real_spec, imag_spec])
    tap_count = whiten_filter.shape[1]
    rim_width = tap_count // 2
    reach_rows = local_rows + tap_count
    skewed = jnp.pad(whiten_filter, ((0, 0), (0, local_rows + 1))).reshape(-1)
    band_matrix = skewed[: local_rows * reach_rows].reshape(local_rows, reach_rows)
    padded = extended(raw_spectra, ((("chan", "freq"), 1),), rim_width)
    predicted = jnp.einsum("ij,ajk->aik", band_matrix, padded, preferred_element_type=jnp.float32)
    whitened = (raw_spectra.astype(jnp.float32) - predicted).astype(jnp.bfloat16)
    spectra = whitened.reshape(2, local_rows, segment_count, FB)
    tm_count = lax.axis_size("tm")
    freq_count = lax.axis_size("freq")
    pieces = lax.all_to_all(spectra[None], ("tm", "freq"), split_axis=4, concat_axis=0, tiled=True)
    band_width = pieces.shape[-1]
    pieces = pieces.reshape(tm_count, freq_count, 2, local_rows, segment_count, band_width)
    banded = pieces.transpose(2, 1, 3, 0, 4, 5).reshape(
        2, freq_count * local_rows, tm_count * segment_count, band_width
    )
    block_rows = banded.shape[1]
    own_block = banded.reshape(2, block_rows, -1)
    depth = own_block.shape[2]
    scaling = 1.0 / math.sqrt(depth)
    block_index = lax.axis_index("chan")
    slot_list = pair_list[0]
    nearby = []
    for distance in range(-REACH, REACH + 1):
        if distance == 0:
            nearby.append(own_block)
        else:
            nearby.append(shifted(own_block, "chan", -distance))
    stacked = jnp.stack(nearby)

    def fetch_partner(partner_index):
        return lax.dynamic_index_in_dim(
            stacked, partner_index - block_index + REACH, 0, keepdims=False
        )

    left_side = jnp.concatenate([own_block[0], own_block[1]], axis=1)
    flipped = jnp.concatenate([own_block[1], -own_block[0]], axis=1)
    contract = (((1,), (1,)), ((), ()))

    def one_slot(partner_index):
        partner = fetch_partner(partner_index)
        right_side = jnp.concatenate([partner[0], partner[1]], axis=1)
        real_part = (
            lax.dot_general(left_side, right_side, contract, preferred_element_type=jnp.float32)
            * scaling
        )
        imag_part = (
            lax.dot_general(flipped, right_side, contract, preferred_element_type=jnp.float32)
            * scaling
        )
        crossed = jnp.stack([real_part, imag_part])
        return jnp.where(partner_index >= 0, crossed, jnp.zeros((), jnp.float32))

    result = jnp.stack([one_slot(slot_list[slot_index]) for slot_index in range(SLOTS)])
    return result.reshape(1, SLOTS, 1, 2, block_rows, block_rows)


MESH = pl.DeviceIdType.MESH
PIECES = 4
STEP = 32
SPECTRA_VMEM = 60 * 2**20
SLOT_VMEM = 4 * 2**20


def spectra_kernel(
    chan_count,
    scaling,
    rec_ref,
    trail_ref,
    filt_ref,
    crossed,
    samples,
    filters,
    bands,
    table,
    coarse,
    raw,
    gathered,
    turned,
    ready,
    local_sems,
    send_sems,
    span_sems,
    pass_sems,
    core_sems,
    filter_sems,
    block_sems,
):
    me = lax.axis_index("chan")
    tm = lax.axis_index("tm")
    core = lax.axis_index("freq")
    rows, hop = rec_ref.shape
    window = 2 * hop
    width = table.shape[1] // 2
    block_rows = 2 * rows
    taps = filt_ref.shape[0]
    rim = taps // 2
    piece = rows // PIECES
    group = piece * PIECES // 2
    furthest = chan_count - 1
    has_left = me > 0
    has_right = me < chan_count - 1
    other = 1 - core
    other_tm = {"tm": 1 - tm}
    other_core = {"freq": 1 - core}
    left = {"chan": me - 1}
    right = {"chan": me + 1}
    ahead = (has_right, has_left)
    onward = (right, left)
    span_send, pass_send, core_send, swap_send = range(4)
    filter_send, block_send = (4, 5), (6, 7)

    def remote(source, target, send, recv, device):
        return pltpu.make_async_remote_copy(
            src_ref=source,
            dst_ref=target,
            send_sem=send_sems.at[send],
            recv_sem=recv,
            device_id=device,
            device_id_type=MESH,
        )

    def half(which):
        return pl.ds(pl.multiple_of(which * rows, rows), rows)

    barrier = pltpu.get_barrier_semaphore()
    later = ((has_right, right), (tm == 0, other_tm), (core == 1, other_core))
    earlier = ((has_left, left), (tm == 1, other_tm), (core == 0, other_core))
    for near, device in later:

        @pl.when(near)
        def _():
            pl.semaphore_signal(barrier, inc=1, device_id=device, device_id_type=MESH)

    own_copies = [
        pltpu.make_async_copy(rec_ref, samples.at[tm, half(core)], local_sems.at[0]),
        pltpu.make_async_copy(trail_ref, samples.at[2, half(core)], local_sems.at[1]),
        pltpu.make_async_copy(filt_ref, filters.at[core, me], local_sems.at[2]),
    ]
    for copy in own_copies:
        copy.start()

    awaited = sum(near.astype(jnp.int32) for near, _ in earlier)

    @pl.when(awaited > 0)
    def _():
        pl.semaphore_wait(barrier, awaited)

    for link, (near, device) in enumerate(earlier):

        @pl.when(near)
        def _():
            pl.semaphore_signal(ready.at[link], inc=1, device_id=device, device_id_type=MESH)

    def meet(link):
        @pl.when(later[link][0])
        def _():
            pl.semaphore_wait(ready.at[link], 1)

    def piece_start(which, step):
        return pl.multiple_of(
            (1 - which) * step * piece + which * (PIECES - 1 - step) * piece, piece
        )

    def piece_in_block(which, step):
        start = which * rows + piece_start(which, step)
        return pl.ds(pl.multiple_of(start, piece), piece)

    def span_copy(p):
        return remote(
            rec_ref.at[pl.ds(piece_start(core, p), piece)],
            samples.at[tm, piece_in_block(core, p)],
            span_send,
            span_sems.at[p],
            other_tm,
        )

    meet(1)
    for p in range(PIECES):
        span_copy(p).start()

    def core_copy(index, which):
        source, place = ((rec_ref, tm), (trail_ref, 2))[index]
        at = samples.at[place, half(which)]
        return remote(source, at, core_send, core_sems.at[index], other_core)

    meet(2)
    for index in range(2):
        core_copy(index, core).start()

    def source_of(direction, distance):
        source = me - distance if direction == 0 else me + distance
        return jnp.clip(source, 0, chan_count - 1)

    def exists(direction, distance):
        return me - distance >= 0 if direction == 0 else me + distance < chan_count

    def weights_copy(direction, distance, sem):
        at = filters.at[core, source_of(direction, distance)]
        return remote(
            filt_ref if distance == 0 else at,
            at,
            filter_send[direction],
            filter_sems.at[direction, sem],
            onward[direction],
        )

    for direction in (1, 0):
        if direction == 0:
            meet(0)

        @pl.when(ahead[direction])
        def _():
            weights_copy(direction, 0, 0).start()

    first_bin = (tm * 2 + core) * width
    unit = 2.0 * math.pi / window
    bins = first_bin + lax.broadcasted_iota(jnp.int32, (1, width), 1)

    def angles(count, scale, factor):
        steps = scale * lax.broadcasted_iota(jnp.int32, (count, width), 0)
        return unit * jnp.bitwise_and(steps * factor, window - 1).astype(jnp.float32)

    parts = window // STEP
    coarse_angle = angles(parts, STEP, bins)
    coarse_turn = angles(parts, STEP, 1)
    coarse[0] = jnp.cos(coarse_angle)
    coarse[1] = jnp.sin(coarse_angle)
    coarse[2] = jnp.cos(coarse_turn)
    coarse[3] = jnp.sin(coarse_turn)
    fine_angle = angles(STEP, 1, bins)
    fine_turn = angles(STEP, 1, 1)
    fine_cos, fine_sin = jnp.cos(fine_angle), jnp.sin(fine_angle)
    turn_cos, turn_sin = jnp.cos(fine_turn), jnp.sin(fine_turn)
    normaliser = 1.0 / math.sqrt(0.375 * window)

    def fill(part, carry):
        c, s, tc, ts = (coarse[k, pl.ds(part, 1), :] for k in range(4))
        taper = (0.5 - 0.5 * (tc * turn_cos - ts * turn_sin)) * normaliser
        at = pl.ds(pl.multiple_of(part * STEP, STEP), STEP)
        table[at, :width] = (taper * (c * fine_cos - s * fine_sin)).astype(jnp.bfloat16)
        table[at, width:] = (-taper * (s * fine_cos + c * fine_sin)).astype(jnp.bfloat16)
        return carry

    lax.fori_loop(0, parts, fill, 0)

    edge = jnp.zeros((rim, raw.shape[1]), raw.dtype)
    raw[0:rim] = edge
    raw[rim + chan_count * block_rows :] = edge

    for copy in own_copies:
        copy.wait()
    for index in range(2):
        core_copy(index, other).wait_recv()

    def own_rows(block, start, count):
        return pl.ds(pl.multiple_of(rim + block * block_rows + start, piece), count)

    groups = [(0, 0), (1, 0), (0, 1), (1, 1)]

    def block_copy(at, direction, distance, index):
        place = raw.at[at]
        return remote(
            place,
            place,
            block_send[direction],
            block_sems.at[direction, distance, index],
            onward[direction],
        )

    def group_rows(direction, distance, index):
        which, step = groups[index]
        here = core if which == 0 else other
        start = here * rows + (1 - here) * step * group + here * (1 - step) * group
        return own_rows(source_of(direction, distance), start, group)

    def transform(which, p, index):
        at = which * rows + piece_start(which, p)
        chosen = pl.ds(pl.multiple_of(at, piece), piece)
        product = jnp.dot(
            samples[0:2, chosen].reshape(2 * piece, hop),
            table[:hop],
            preferred_element_type=jnp.float32,
        ) + jnp.dot(
            samples[1:3, chosen].reshape(2 * piece, hop),
            table[hop:],
            preferred_element_type=jnp.float32,
        )
        product = product.astype(jnp.bfloat16)
        where = own_rows(me, at, piece)
        for segment in range(2):
            found = product[segment * piece : (segment + 1) * piece]
            raw[where, segment * width : (segment + 1) * width] = found[:, :width]
            raw[where, (2 + segment) * width : (3 + segment) * width] = found[:, width:]
        for direction in range(2):

            @pl.when(ahead[direction])
            def _():
                block_copy(where, direction, 0, index).start()

    def take_weights(distance):
        for direction in range(2):

            @pl.when(exists(direction, distance))
            def _():
                weights_copy(direction, distance, distance - 1).wait_recv()

            if distance < furthest:

                @pl.when(jnp.logical_and(exists(direction, distance), ahead[direction]))
                def _():
                    weights_copy(direction, distance, distance).start()

    def passed(which, p):
        at = samples.at[1 - tm, piece_in_block(which, p)]
        return remote(at, at, pass_send, pass_sems.at[p], other_core)

    tiers = [(0, 0)]
    for p in range(1, PIECES):
        tiers += [(0, p), (1, p - 1)]
    tiers.append((1, PIECES - 1))
    for which, p in tiers:
        index = groups.index((which, 2 * p // PIECES))
        if which == 0:
            span_copy(p).wait_recv()
            passed(core, p).start()
            transform(core, p, index)
        else:
            passed(other, p).wait_recv()
            transform(other, p, index)
        if (which, p) == (0, 2):
            take_weights(1)

    take_weights(2)

    def spread(block, carry):
        for which in range(2):
            weights = jnp.transpose(filters[which, block].astype(jnp.float32))
            wide = jnp.concatenate([weights, jnp.zeros((rows, 128 - taps), jnp.float32)], axis=1)
            for p in range(PIECES):
                rolled = pltpu.roll(
                    wide[p * piece : (p + 1) * piece], 0, 1, stride=1, stride_axis=0
                )
                bands[block, which * PIECES + p] = rolled.astype(jnp.bfloat16)
        return carry

    def whiten(block, tile):
        start = pl.multiple_of(block * block_rows + tile * piece, piece)
        near = raw[pl.ds(start, piece + taps)]
        predicted = jnp.dot(
            bands[block, tile][:, : piece + taps], near, preferred_element_type=jnp.float32
        )
        mine = near[rim : rim + piece].astype(jnp.float32)
        gathered[block, tile * piece : (tile + 1) * piece] = (mine - predicted).astype(
            jnp.bfloat16
        )

    contract = (((1,), (1,)), ((), ()))

    def cross(block):
        partner = gathered[block]
        for part, side in enumerate((gathered[me], turned[...])):
            crossed[block, part] = (
                lax.dot_general(side, partner, contract, preferred_element_type=jnp.float32)
                * scaling
            )

    tile_count = 2 * PIECES

    def finish_own():
        for tile in range(tile_count):
            whiten(me, tile)
        own = gathered[me]
        middle = own.shape[1] // 2
        turned[...] = jnp.concatenate([own[:, middle:], -own[:, :middle]], axis=1)
        cross(me)

    def inner(distance):
        for direction in range(2):

            @pl.when(exists(direction, distance))
            def _():
                block = me - distance if direction == 0 else me + distance
                for tile in range(tile_count - 1):
                    whiten(block, tile + 1 if direction == 0 else tile)

    def finish(distance):
        for direction in range(2):

            @pl.when(exists(direction, distance))
            def _():
                block = me - distance if direction == 0 else me + distance
                whiten(block, 0 if direction == 0 else tile_count - 1)
                cross(block)

    def arrive(distance, index):
        for direction in range(2):
            at = group_rows(direction, distance, index)

            @pl.when(exists(direction, distance))
            def _():
                block_copy(at, direction, distance - 1, index).wait_recv()

            if distance < furthest:

                @pl.when(jnp.logical_and(exists(direction, distance), ahead[direction]))
                def _():
                    block_copy(at, direction, distance, index).start()

    def swap(which):
        at = filters.at[which]
        return remote(at, at, swap_send, core_sems.at[2], other_core)

    for index in range(4):
        arrive(1, index)
    take_weights(3)
    swap(core).start()
    arrive(2, 0)
    arrive(2, 1)
    swap(other).wait_recv()
    lax.fori_loop(0, chan_count, spread, 0)
    arrive(2, 2)
    finish_own()
    arrive(2, 3)
    inner(1)
    finish(1)
    inner(2)
    for index in range(4):
        arrive(3, index)
    finish(2)
    inner(3)
    finish(3)

    whole = samples.at[tm, half(core)]
    remote(whole, whole, span_send, span_sems.at[0], other_tm).wait_send()
    remote(whole, whole, pass_send, pass_sems.at[0], other_core).wait_send()
    both = samples.at[0:2, half(core)]
    remote(both, both, core_send, core_sems.at[0], other_core).wait_send()
    swap(core).wait_send()

    for direction in range(2):
        for count in range(1, chan_count):

            @pl.when(me == (count - 1 if direction == 0 else chan_count - count))
            def _():
                sent = filters.at[core, 0:count]
                remote(
                    sent, sent, filter_send[direction], filter_sems.at[0, 0], onward[direction]
                ).wait_send()
                sent = raw.at[0 : count * block_rows]
                remote(
                    sent, sent, block_send[direction], block_sems.at[0, 0, 0], onward[direction]
                ).wait_send()


def slot_kernel(pairs_ref, crossed, out_ref, blank, sems):
    def store(slot, source):
        return pltpu.make_async_copy(source, out_ref.at[0, slot, 0], sems.at[slot])

    for slot in range(SLOTS):

        @pl.when(pairs_ref[0, slot] >= 0)
        def _():
            store(slot, crossed.at[jnp.maximum(pairs_ref[0, slot], 0)]).start()

    blank[...] = jnp.zeros(blank.shape, blank.dtype)

    for slot in range(SLOTS):

        @pl.when(pairs_ref[0, slot] < 0)
        def _():
            store(slot, blank).start()

    for slot in range(SLOTS):
        store(slot, blank).wait()


def fused(recording, trailing, whiten_filter, pair_list):
    rows, hop = recording.shape
    chan_count = lax.axis_size("chan")
    taps = whiten_filter.shape[1]
    width = FB // (lax.axis_size("tm") * lax.axis_size("freq"))
    block_rows = 2 * rows
    depth = 2 * width
    vmem = pl.BlockSpec(memory_space=pltpu.VMEM)
    hbm = pl.BlockSpec(memory_space=pltpu.HBM)
    crossed = pl.pallas_call(
        functools.partial(spectra_kernel, chan_count, 1.0 / math.sqrt(depth)),
        out_shape=pltpu.VMEM((chan_count, 2, block_rows, block_rows), jnp.float32),
        in_specs=[hbm] * 3,
        out_specs=vmem,
        scratch_shapes=[
            pltpu.VMEM((3, block_rows, hop), jnp.bfloat16),
            pltpu.VMEM((2, chan_count, taps, rows), jnp.bfloat16),
            pltpu.VMEM((chan_count, 2 * PIECES, rows // PIECES, 128), jnp.bfloat16),
            pltpu.VMEM((2 * hop, 2 * width), jnp.bfloat16),
            pltpu.VMEM((4, 2 * hop // STEP, width), jnp.float32),
            pltpu.VMEM((chan_count * block_rows + taps, 2 * depth), jnp.bfloat16),
            pltpu.VMEM((chan_count, block_rows, 2 * depth), jnp.bfloat16),
            pltpu.VMEM((block_rows, 2 * depth), jnp.bfloat16),
            pltpu.SemaphoreType.REGULAR((3,)),
            pltpu.SemaphoreType.DMA((3,)),
            pltpu.SemaphoreType.DMA((8,)),
            pltpu.SemaphoreType.DMA((PIECES,)),
            pltpu.SemaphoreType.DMA((PIECES,)),
            pltpu.SemaphoreType.DMA((3,)),
            pltpu.SemaphoreType.DMA((2, chan_count - 1)),
            pltpu.SemaphoreType.DMA((2, chan_count - 1, 4)),
        ],
        compiler_params=pltpu.CompilerParams(
            collective_id=0, has_side_effects=True, vmem_limit_bytes=SPECTRA_VMEM
        ),
    )(recording, trailing, whiten_filter.T)
    return pl.pallas_call(
        slot_kernel,
        out_shape=jax.ShapeDtypeStruct((1, SLOTS, 1, 2, block_rows, block_rows), jnp.float32),
        in_specs=[pl.BlockSpec(memory_space=pltpu.SMEM), vmem],
        out_specs=hbm,
        scratch_shapes=[
            pltpu.VMEM((2, block_rows, block_rows), jnp.float32),
            pltpu.SemaphoreType.DMA((SLOTS,)),
        ],
        compiler_params=pltpu.CompilerParams(vmem_limit_bytes=SLOT_VMEM),
    )(pair_list, crossed)


def local(recording, trailing, whiten_filter, pair_list):
    shapes = (recording.shape, trailing.shape, whiten_filter.shape)
    counts = (lax.axis_size("tm"), lax.axis_size("freq"))
    whole_reach = lax.axis_size("chan") == REACH + 1
    if shapes == ((128, 1024), (128, 1024), (128, 64)) and counts == (2, 2) and whole_reach:
        return fused(recording, trailing, whiten_filter, pair_list)
    return general(recording, trailing, whiten_filter, pair_list)


def solution(mesh):
    placed = (
        P(("days", "chan", "freq"), "tm"),
        P(("days", "chan", "freq"), None),
        P(("chan", "freq"), None),
        P(("days", "chan"), None),
    )
    return jax.shard_map(
        local,
        mesh=mesh,
        in_specs=placed,
        out_specs=P(("days", "chan"), None, ("tm", "freq"), None, None, None),
        check_vma=False,
    )
```

```python
import functools
import math

import jax
import jax.numpy as jnp
from jax import lax
from jax.experimental import pallas as pl
from jax.experimental.pallas import tpu as pltpu
from jax.sharding import PartitionSpec as P

FB = 512
REACH = 3
SLOTS = 4


def shifted(block, axis, distance):
    devices = range(lax.axis_size(axis))
    route = [(i - distance, i) for i in devices if i - distance in devices]
    return lax.ppermute(block, axis, route)


def extended(value, sides, width):
    for axis, dim in sides:
        size, length = (lax.axis_size(axis), value.shape[dim])
        up = [(i, (i + 1) % size) for i in range(size - 1)]
        down = [(j, i) for i, j in up]
        last = lax.slice_in_dim(value, length - width, length, axis=dim)
        initial = lax.slice_in_dim(value, 0, width, axis=dim)
        before = lax.ppermute(last, axis, up)
        after = lax.ppermute(initial, axis, down)
        value = jnp.concatenate([before, value, after], axis=dim)
    return value


def fourier_table(first_bin, bin_count, length):
    samples = jnp.arange(length, dtype=jnp.int32)[:, None]
    bin_index = first_bin + jnp.arange(bin_count, dtype=jnp.int32)[None, :]
    phase = samples * bin_index % length
    angle = 2.0 * math.pi / length * phase.astype(jnp.float32)
    taper = 0.5 - 0.5 * jnp.cos(
        2.0 * math.pi / length * jnp.arange(length, dtype=jnp.int32).astype(jnp.float32)
    )
    normaliser = 1.0 / math.sqrt(0.375 * length)
    cosine = (taper[:, None] * jnp.cos(angle) * normaliser).astype(jnp.bfloat16)
    sine_table = (-taper[:, None] * jnp.sin(angle) * normaliser).astype(jnp.bfloat16)
    return (cosine, sine_table)


def general(recording, trailing, whiten_filter, pair_list):
    local_rows, local_span = recording.shape
    hop_size = trailing.shape[1]
    window_size = 2 * hop_size
    segment_count = local_span // hop_size
    following = shifted(recording, "tm", -1)
    is_last = lax.axis_index("tm") == lax.axis_size("tm") - 1
    following = jnp.where(is_last, trailing, following)
    signal = jnp.concatenate([recording, following], axis=1)
    segments = jnp.stack([signal], axis=1)
    stacked_segments = segments.reshape(local_rows * segment_count, window_size)
    bin_step = min(256, FB)
    real_bins = []
    imag_bins = []
    for first_bin in range(0, FB, bin_step):
        cosine, sine_table = fourier_table(first_bin, bin_step, window_size)
        joined = jnp.concatenate([cosine, sine_table], axis=1)
        product = jnp.dot(stacked_segments, joined, preferred_element_type=jnp.float32).astype(
            jnp.bfloat16
        )
        real_bins.append(product[:, :bin_step])
        imag_bins.append(product[:, bin_step:])
    real_spec = jnp.concatenate(real_bins, axis=1)
    imag_spec = jnp.concatenate(imag_bins, axis=1)
    raw_spectra = jnp.stack([real_spec, imag_spec])
    tap_count = whiten_filter.shape[1]
    rim_width = tap_count // 2
    reach_rows = local_rows + tap_count
    skewed = jnp.pad(whiten_filter, ((0, 0), (0, local_rows + 1))).reshape(-1)
    band_matrix = skewed[: local_rows * reach_rows].reshape(local_rows, reach_rows)
    padded = extended(raw_spectra, ((("chan", "freq"), 1),), rim_width)
    predicted = jnp.einsum("ij,ajk->aik", band_matrix, padded, preferred_element_type=jnp.float32)
    whitened = (raw_spectra.astype(jnp.float32) - predicted).astype(jnp.bfloat16)
    spectra = whitened.reshape(2, local_rows, segment_count, FB)
    tm_count = lax.axis_size("tm")
    freq_count = lax.axis_size("freq")
    pieces = lax.all_to_all(spectra[None], ("tm", "freq"), split_axis=4, concat_axis=0, tiled=True)
    band_width = pieces.shape[-1]
    pieces = pieces.reshape(tm_count, freq_count, 2, local_rows, segment_count, band_width)
    banded = pieces.transpose(2, 1, 3, 0, 4, 5).reshape(
        2, freq_count * local_rows, tm_count * segment_count, band_width
    )
    block_rows = banded.shape[1]
    own_block = banded.reshape(2, block_rows, -1)
    depth = own_block.shape[2]
    scaling = 1.0 / math.sqrt(depth)
    block_index = lax.axis_index("chan")
    slot_list = pair_list[0]
    nearby = []
    for distance in range(-REACH, REACH + 1):
        if distance == 0:
            nearby.append(own_block)
        else:
            nearby.append(shifted(own_block, "chan", -distance))
    stacked = jnp.stack(nearby)

    def fetch_partner(partner_index):
        return lax.dynamic_index_in_dim(
            stacked, partner_index - block_index + REACH, 0, keepdims=False
        )

    left_side = jnp.concatenate([own_block[0], own_block[1]], axis=1)
    flipped = jnp.concatenate([own_block[1], -own_block[0]], axis=1)
    contract = (((1,), (1,)), ((), ()))

    def one_slot(partner_index):
        partner = fetch_partner(partner_index)
        right_side = jnp.concatenate([partner[0], partner[1]], axis=1)
        real_part = (
            lax.dot_general(left_side, right_side, contract, preferred_element_type=jnp.float32)
            * scaling
        )
        imag_part = (
            lax.dot_general(flipped, right_side, contract, preferred_element_type=jnp.float32)
            * scaling
        )
        crossed = jnp.stack([real_part, imag_part])
        return jnp.where(partner_index >= 0, crossed, jnp.zeros((), jnp.float32))

    result = jnp.stack([one_slot(slot_list[slot_index]) for slot_index in range(SLOTS)])
    return result.reshape(1, SLOTS, 1, 2, block_rows, block_rows)


MESH = pl.DeviceIdType.MESH
PIECES = 4
STEP = 32
SPECTRA_VMEM = 60 * 2**20
SLOT_VMEM = 4 * 2**20


def spectra_kernel(
    chan_count,
    scaling,
    rec_ref,
    trail_ref,
    filt_ref,
    crossed,
    samples,
    filters,
    bands,
    table,
    coarse,
    raw,
    gathered,
    turned,
    guest,
    ready,
    local_sems,
    send_sems,
    span_sems,
    pass_sems,
    core_sems,
    filter_sems,
    block_sems,
    guest_sems,
):
    me = lax.axis_index("chan")
    tm = lax.axis_index("tm")
    core = lax.axis_index("freq")
    rows, hop = rec_ref.shape
    window = 2 * hop
    width = table.shape[1] // 2
    block_rows = 2 * rows
    taps = filt_ref.shape[0]
    rim = taps // 2
    piece = rows // PIECES
    group = piece * PIECES // 2
    furthest = chan_count - 1
    has_left = me > 0
    has_right = me < chan_count - 1
    other = 1 - core
    other_tm = {"tm": 1 - tm}
    other_core = {"freq": 1 - core}
    left = {"chan": me - 1}
    right = {"chan": me + 1}
    ahead = (has_right, has_left)
    onward = (right, left)
    span_send, pass_send, core_send, swap_send = range(4)
    filter_send, block_send = (4, 5), (6, 7)
    guest_send, share_send = 8, 9
    hosting = jnp.logical_or(me == 0, me == furthest)

    def remote(source, target, send, recv, device):
        return pltpu.make_async_remote_copy(
            src_ref=source,
            dst_ref=target,
            send_sem=send_sems.at[send],
            recv_sem=recv,
            device_id=device,
            device_id_type=MESH,
        )

    def half(which):
        return pl.ds(pl.multiple_of(which * rows, rows), rows)

    barrier = pltpu.get_barrier_semaphore()
    later = ((has_right, right), (tm == 0, other_tm), (core == 1, other_core))
    earlier = ((has_left, left), (tm == 1, other_tm), (core == 0, other_core))
    for near, device in later:

        @pl.when(near)
        def _():
            pl.semaphore_signal(barrier, inc=1, device_id=device, device_id_type=MESH)

    own_copies = [
        pltpu.make_async_copy(rec_ref, samples.at[tm, half(core)], local_sems.at[0]),
        pltpu.make_async_copy(trail_ref, samples.at[2, half(core)], local_sems.at[1]),
        pltpu.make_async_copy(filt_ref, filters.at[core, me], local_sems.at[2]),
    ]
    for copy in own_copies:
        copy.start()

    awaited = sum(near.astype(jnp.int32) for near, _ in earlier)

    @pl.when(awaited > 0)
    def _():
        pl.semaphore_wait(barrier, awaited)

    for link, (near, device) in enumerate(earlier):

        @pl.when(near)
        def _():
            pl.semaphore_signal(ready.at[link], inc=1, device_id=device, device_id_type=MESH)

    def meet(link):
        @pl.when(later[link][0])
        def _():
            pl.semaphore_wait(ready.at[link], 1)

    def piece_start(which, step):
        return pl.multiple_of(
            (1 - which) * step * piece + which * (PIECES - 1 - step) * piece, piece
        )

    def piece_in_block(which, step):
        start = which * rows + piece_start(which, step)
        return pl.ds(pl.multiple_of(start, piece), piece)

    def span_copy(p):
        return remote(
            rec_ref.at[pl.ds(piece_start(core, p), piece)],
            samples.at[tm, piece_in_block(core, p)],
            span_send,
            span_sems.at[p],
            other_tm,
        )

    meet(1)
    for p in range(PIECES):
        span_copy(p).start()

    def core_copy(index, which):
        source, place = ((rec_ref, tm), (trail_ref, 2))[index]
        at = samples.at[place, half(which)]
        return remote(source, at, core_send, core_sems.at[index], other_core)

    meet(2)
    for index in range(2):
        core_copy(index, core).start()

    def source_of(direction, distance):
        source = me - distance if direction == 0 else me + distance
        return jnp.clip(source, 0, chan_count - 1)

    def exists(direction, distance):
        return me - distance >= 0 if direction == 0 else me + distance < chan_count

    def weights_copy(direction, distance, sem):
        at = filters.at[core, source_of(direction, distance)]
        return remote(
            filt_ref if distance == 0 else at,
            at,
            filter_send[direction],
            filter_sems.at[direction, sem],
            onward[direction],
        )

    feeding = (me == furthest - 1, me == 1)

    def guest_copy(tm_index, core_index, send, sem, device):
        at = guest.at[tm_index, core_index]
        return remote(at, at, send, guest_sems.at[sem], device)

    for direction in (1, 0):
        if direction == 0:
            meet(0)

        @pl.when(ahead[direction])
        def _():
            weights_copy(direction, 0, 0).start()

        @pl.when(feeding[direction])
        def _():
            first = pl.multiple_of((1 - core) * group, group)
            share = group // 2
            later_rows = pl.multiple_of(first + tm * share, share)
            for source, start, at, count in (
                (rec_ref, first, 0, group),
                (trail_ref, later_rows, group, share),
            ):
                remote(
                    source.at[pl.ds(start, count)],
                    guest.at[tm, core, at : at + count],
                    guest_send,
                    guest_sems.at[0],
                    onward[direction],
                ).start()

    first_bin = (tm * 2 + core) * width
    unit = 2.0 * math.pi / window
    bins = first_bin + lax.broadcasted_iota(jnp.int32, (1, width), 1)

    def angles(count, scale, factor):
        steps = scale * lax.broadcasted_iota(jnp.int32, (count, width), 0)
        return unit * jnp.bitwise_and(steps * factor, window - 1).astype(jnp.float32)

    parts = window // STEP
    coarse_angle = angles(parts, STEP, bins)
    coarse_turn = angles(parts, STEP, 1)
    coarse[0] = jnp.cos(coarse_angle)
    coarse[1] = jnp.sin(coarse_angle)
    coarse[2] = jnp.cos(coarse_turn)
    coarse[3] = jnp.sin(coarse_turn)
    fine_angle = angles(STEP, 1, bins)
    fine_turn = angles(STEP, 1, 1)
    fine_cos, fine_sin = jnp.cos(fine_angle), jnp.sin(fine_angle)
    turn_cos, turn_sin = jnp.cos(fine_turn), jnp.sin(fine_turn)
    normaliser = 1.0 / math.sqrt(0.375 * window)

    def fill(part, carry):
        c, s, tc, ts = (coarse[k, pl.ds(part, 1), :] for k in range(4))
        taper = (0.5 - 0.5 * (tc * turn_cos - ts * turn_sin)) * normaliser
        at = pl.ds(pl.multiple_of(part * STEP, STEP), STEP)
        table[at, :width] = (taper * (c * fine_cos - s * fine_sin)).astype(jnp.bfloat16)
        table[at, width:] = (-taper * (s * fine_cos + c * fine_sin)).astype(jnp.bfloat16)
        return carry

    lax.fori_loop(0, parts, fill, 0)

    edge = jnp.zeros((rim, raw.shape[1]), raw.dtype)
    raw[0:rim] = edge
    raw[rim + chan_count * block_rows :] = edge

    for copy in own_copies:
        copy.wait()
    for index in range(2):
        core_copy(index, other).wait_recv()

    def own_rows(block, start, count):
        return pl.ds(pl.multiple_of(rim + block * block_rows + start, piece), count)

    groups = [(0, 0), (1, 0), (0, 1), (1, 1)]

    def block_copy(at, direction, distance, index):
        place = raw.at[at]
        return remote(
            place,
            place,
            block_send[direction],
            block_sems.at[direction, distance, index],
            onward[direction],
        )

    def group_rows(direction, distance, index):
        which, step = groups[index]
        here = core if which == 0 else other
        start = here * rows + (1 - here) * step * group + here * (1 - step) * group
        return own_rows(source_of(direction, distance), start, group)

    def fill_rows(where, count, early, late):
        product = jnp.dot(early, table[:hop], preferred_element_type=jnp.float32) + jnp.dot(
            late, table[hop:], preferred_element_type=jnp.float32
        )
        product = product.astype(jnp.bfloat16)
        for segment in range(2):
            found = product[segment * count : (segment + 1) * count]
            raw[where, segment * width : (segment + 1) * width] = found[:, :width]
            raw[where, (2 + segment) * width : (3 + segment) * width] = found[:, width:]

    def transform(which, p, index):
        at = which * rows + piece_start(which, p)
        chosen = pl.ds(pl.multiple_of(at, piece), piece)
        where = own_rows(me, at, piece)
        fill_rows(
            where,
            piece,
            samples[0:2, chosen].reshape(2 * piece, hop),
            samples[1:3, chosen].reshape(2 * piece, hop),
        )
        for direction in range(2):
            wanted = ahead[direction]
            if groups[index][1] == 1:
                wanted = jnp.logical_and(wanted, jnp.logical_not(feeding[direction]))

            @pl.when(wanted)
            def _():
                block_copy(where, direction, 0, index).start()

    def guest_transform(which):
        first, second = guest[0, which, :group], guest[1, which, :group]
        third = jnp.concatenate([guest[0, which, group:], guest[1, which, group:]], axis=0)
        near = jnp.where(me == 0, 1, furthest - 1)
        fill_rows(
            own_rows(near, which * rows + (1 - which) * group, group),
            group,
            jnp.concatenate([first, second], axis=0),
            jnp.concatenate([second, third], axis=0),
        )

    def take_weights(distance):
        for direction in range(2):

            @pl.when(exists(direction, distance))
            def _():
                weights_copy(direction, distance, distance - 1).wait_recv()

            if distance < furthest:

                @pl.when(jnp.logical_and(exists(direction, distance), ahead[direction]))
                def _():
                    weights_copy(direction, distance, distance).start()

    def passed(which, p):
        at = samples.at[1 - tm, piece_in_block(which, p)]
        return remote(at, at, pass_send, pass_sems.at[p], other_core)

    tiers = [(0, 0)]
    for p in range(1, PIECES):
        tiers += [(0, p), (1, p - 1)]
    tiers.append((1, PIECES - 1))
    for which, p in tiers:
        index = groups.index((which, 2 * p // PIECES))
        if which == 0:
            span_copy(p).wait_recv()
            passed(core, p).start()
            transform(core, p, index)
        else:
            passed(other, p).wait_recv()
            transform(other, p, index)
        if (which, p) == (0, 2):
            take_weights(1)

    @pl.when(hosting)
    def _():
        guest_copy(tm, core, guest_send, 0, other_tm).wait_recv()
        guest_copy(tm, core, guest_send, 1, other_tm).start()
        guest_copy(tm, core, share_send, 2, other_core).start()

    take_weights(2)

    def spread(block, carry):
        for which in range(2):
            weights = jnp.transpose(filters[which, block].astype(jnp.float32))
            wide = jnp.concatenate([weights, jnp.zeros((rows, 128 - taps), jnp.float32)], axis=1)
            for p in range(PIECES):
                rolled = pltpu.roll(
                    wide[p * piece : (p + 1) * piece], 0, 1, stride=1, stride_axis=0
                )
                bands[block, which * PIECES + p] = rolled.astype(jnp.bfloat16)
        return carry

    def whiten(block, tile):
        start = pl.multiple_of(block * block_rows + tile * piece, piece)
        near = raw[pl.ds(start, piece + taps)]
        predicted = jnp.dot(
            bands[block, tile][:, : piece + taps], near, preferred_element_type=jnp.float32
        )
        mine = near[rim : rim + piece].astype(jnp.float32)
        gathered[block, tile * piece : (tile + 1) * piece] = (mine - predicted).astype(
            jnp.bfloat16
        )

    contract = (((1,), (1,)), ((), ()))

    def cross(block):
        partner = gathered[block]
        for part, side in enumerate((gathered[me], turned[...])):
            crossed[block, part] = (
                lax.dot_general(side, partner, contract, preferred_element_type=jnp.float32)
                * scaling
            )

    tile_count = 2 * PIECES

    def finish_own():
        for tile in range(tile_count):
            whiten(me, tile)
        own = gathered[me]
        middle = own.shape[1] // 2
        turned[...] = jnp.concatenate([own[:, middle:], -own[:, :middle]], axis=1)
        cross(me)

    def inner(distance):
        for direction in range(2):

            @pl.when(exists(direction, distance))
            def _():
                block = me - distance if direction == 0 else me + distance
                for tile in range(tile_count - 1):
                    whiten(block, tile + 1 if direction == 0 else tile)

    def finish(distance):
        for direction in range(2):

            @pl.when(exists(direction, distance))
            def _():
                block = me - distance if direction == 0 else me + distance
                whiten(block, 0 if direction == 0 else tile_count - 1)
                cross(block)

    def arrive(distance, index):
        for direction in range(2):
            at = group_rows(direction, distance, index)

            expected = exists(direction, distance)
            if distance == 1 and groups[index][1] == 1:
                expected = jnp.logical_and(expected, jnp.logical_not(hosting))

            @pl.when(expected)
            def _():
                block_copy(at, direction, distance - 1, index).wait_recv()

            if distance < furthest:

                @pl.when(jnp.logical_and(exists(direction, distance), ahead[direction]))
                def _():
                    block_copy(at, direction, distance, index).start()

    def swap(which):
        at = filters.at[which]
        return remote(at, at, swap_send, core_sems.at[2], other_core)

    for index in range(4):
        arrive(1, index)
    take_weights(3)
    swap(core).start()
    arrive(2, 0)
    arrive(2, 1)
    swap(other).wait_recv()
    lax.fori_loop(0, chan_count, spread, 0)
    arrive(2, 2)
    finish_own()
    arrive(2, 3)

    @pl.when(hosting)
    def _():
        guest_copy(1 - tm, core, guest_send, 1, other_tm).wait_recv()
        guest_copy(1 - tm, core, share_send, 3, other_core).start()

    arrive(3, 0)

    @pl.when(hosting)
    def _():
        guest_copy(tm, other, share_send, 2, other_core).wait_recv()
        guest_transform(core)
        guest_copy(1 - tm, other, share_send, 3, other_core).wait_recv()
        guest_transform(other)

    inner(1)
    finish(1)
    arrive(3, 1)
    inner(2)
    finish(2)
    arrive(3, 2)
    arrive(3, 3)
    inner(3)
    finish(3)

    guest_copy(tm, core, guest_send, 1, other_tm).wait_send()

    @pl.when(hosting)
    def _():
        shared = guest.at[0:2, core]
        remote(shared, shared, share_send, guest_sems.at[2], other_core).wait_send()

    whole = samples.at[tm, half(core)]
    remote(whole, whole, span_send, span_sems.at[0], other_tm).wait_send()
    remote(whole, whole, pass_send, pass_sems.at[0], other_core).wait_send()
    both = samples.at[0:2, half(core)]
    remote(both, both, core_send, core_sems.at[0], other_core).wait_send()
    swap(core).wait_send()

    for direction in range(2):
        for count in range(1, chan_count):

            @pl.when(me == (count - 1 if direction == 0 else chan_count - count))
            def _():
                sent = filters.at[core, 0:count]
                remote(
                    sent, sent, filter_send[direction], filter_sems.at[0, 0], onward[direction]
                ).wait_send()
                fed = rows if count == furthest else 0
                sent = raw.at[0 : count * block_rows - fed]
                remote(
                    sent, sent, block_send[direction], block_sems.at[0, 0, 0], onward[direction]
                ).wait_send()


def slot_kernel(pairs_ref, crossed, out_ref, blank, sems):
    def store(slot, source):
        return pltpu.make_async_copy(source, out_ref.at[0, slot, 0], sems.at[slot])

    for slot in range(SLOTS):

        @pl.when(pairs_ref[0, slot] >= 0)
        def _():
            store(slot, crossed.at[jnp.maximum(pairs_ref[0, slot], 0)]).start()

    blank[...] = jnp.zeros(blank.shape, blank.dtype)

    for slot in range(SLOTS):

        @pl.when(pairs_ref[0, slot] < 0)
        def _():
            store(slot, blank).start()

    for slot in range(SLOTS):
        store(slot, blank).wait()


def fused(recording, trailing, whiten_filter, pair_list):
    rows, hop = recording.shape
    chan_count = lax.axis_size("chan")
    taps = whiten_filter.shape[1]
    width = FB // (lax.axis_size("tm") * lax.axis_size("freq"))
    block_rows = 2 * rows
    depth = 2 * width
    vmem = pl.BlockSpec(memory_space=pltpu.VMEM)
    hbm = pl.BlockSpec(memory_space=pltpu.HBM)
    crossed = pl.pallas_call(
        functools.partial(spectra_kernel, chan_count, 1.0 / math.sqrt(depth)),
        out_shape=pltpu.VMEM((chan_count, 2, block_rows, block_rows), jnp.float32),
        in_specs=[hbm] * 3,
        out_specs=vmem,
        scratch_shapes=[
            pltpu.VMEM((3, block_rows, hop), jnp.bfloat16),
            pltpu.VMEM((2, chan_count, taps, rows), jnp.bfloat16),
            pltpu.VMEM((chan_count, 2 * PIECES, rows // PIECES, 128), jnp.bfloat16),
            pltpu.VMEM((2 * hop, 2 * width), jnp.bfloat16),
            pltpu.VMEM((4, 2 * hop // STEP, width), jnp.float32),
            pltpu.VMEM((chan_count * block_rows + taps, 2 * depth), jnp.bfloat16),
            pltpu.VMEM((chan_count, block_rows, 2 * depth), jnp.bfloat16),
            pltpu.VMEM((block_rows, 2 * depth), jnp.bfloat16),
            pltpu.VMEM((2, 2, 3 * rows // 4, hop), jnp.bfloat16),
            pltpu.SemaphoreType.REGULAR((3,)),
            pltpu.SemaphoreType.DMA((3,)),
            pltpu.SemaphoreType.DMA((10,)),
            pltpu.SemaphoreType.DMA((PIECES,)),
            pltpu.SemaphoreType.DMA((PIECES,)),
            pltpu.SemaphoreType.DMA((3,)),
            pltpu.SemaphoreType.DMA((2, chan_count - 1)),
            pltpu.SemaphoreType.DMA((2, chan_count - 1, 4)),
            pltpu.SemaphoreType.DMA((4,)),
        ],
        compiler_params=pltpu.CompilerParams(
            collective_id=0, has_side_effects=True, vmem_limit_bytes=SPECTRA_VMEM
        ),
    )(recording, trailing, whiten_filter.T)
    return pl.pallas_call(
        slot_kernel,
        out_shape=jax.ShapeDtypeStruct((1, SLOTS, 1, 2, block_rows, block_rows), jnp.float32),
        in_specs=[pl.BlockSpec(memory_space=pltpu.SMEM), vmem],
        out_specs=hbm,
        scratch_shapes=[
            pltpu.VMEM((2, block_rows, block_rows), jnp.float32),
            pltpu.SemaphoreType.DMA((SLOTS,)),
        ],
        compiler_params=pltpu.CompilerParams(vmem_limit_bytes=SLOT_VMEM),
    )(pair_list, crossed)


def local(recording, trailing, whiten_filter, pair_list):
    shapes = (recording.shape, trailing.shape, whiten_filter.shape)
    counts = (lax.axis_size("tm"), lax.axis_size("freq"))
    whole_reach = lax.axis_size("chan") == REACH + 1
    if shapes == ((128, 1024), (128, 1024), (128, 64)) and counts == (2, 2) and whole_reach:
        return fused(recording, trailing, whiten_filter, pair_list)
    return general(recording, trailing, whiten_filter, pair_list)


def solution(mesh):
    placed = (
        P(("days", "chan", "freq"), "tm"),
        P(("days", "chan", "freq"), None),
        P(("chan", "freq"), None),
        P(("days", "chan"), None),
    )
    return jax.shard_map(
        local,
        mesh=mesh,
        in_specs=placed,
        out_specs=P(("days", "chan"), None, ("tm", "freq"), None, None, None),
        check_vma=False,
    )
```

```python
import functools
import math

import jax
import jax.numpy as jnp
from jax import lax
from jax.experimental import pallas as pl
from jax.experimental.pallas import tpu as pltpu
from jax.sharding import PartitionSpec as P

FB = 512
REACH = 3
SLOTS = 4


def shifted(block, axis, distance):
    devices = range(lax.axis_size(axis))
    route = [(i - distance, i) for i in devices if i - distance in devices]
    return lax.ppermute(block, axis, route)


def extended(value, sides, width):
    for axis, dim in sides:
        size, length = (lax.axis_size(axis), value.shape[dim])
        up = [(i, (i + 1) % size) for i in range(size - 1)]
        down = [(j, i) for i, j in up]
        last = lax.slice_in_dim(value, length - width, length, axis=dim)
        initial = lax.slice_in_dim(value, 0, width, axis=dim)
        before = lax.ppermute(last, axis, up)
        after = lax.ppermute(initial, axis, down)
        value = jnp.concatenate([before, value, after], axis=dim)
    return value


def fourier_table(first_bin, bin_count, length):
    samples = jnp.arange(length, dtype=jnp.int32)[:, None]
    bin_index = first_bin + jnp.arange(bin_count, dtype=jnp.int32)[None, :]
    phase = samples * bin_index % length
    angle = 2.0 * math.pi / length * phase.astype(jnp.float32)
    taper = 0.5 - 0.5 * jnp.cos(
        2.0 * math.pi / length * jnp.arange(length, dtype=jnp.int32).astype(jnp.float32)
    )
    normaliser = 1.0 / math.sqrt(0.375 * length)
    cosine = (taper[:, None] * jnp.cos(angle) * normaliser).astype(jnp.bfloat16)
    sine_table = (-taper[:, None] * jnp.sin(angle) * normaliser).astype(jnp.bfloat16)
    return (cosine, sine_table)


def general(recording, trailing, whiten_filter, pair_list):
    local_rows, local_span = recording.shape
    hop_size = trailing.shape[1]
    window_size = 2 * hop_size
    segment_count = local_span // hop_size
    following = shifted(recording, "tm", -1)
    is_last = lax.axis_index("tm") == lax.axis_size("tm") - 1
    following = jnp.where(is_last, trailing, following)
    signal = jnp.concatenate([recording, following], axis=1)
    segments = jnp.stack([signal], axis=1)
    stacked_segments = segments.reshape(local_rows * segment_count, window_size)
    bin_step = min(256, FB)
    real_bins = []
    imag_bins = []
    for first_bin in range(0, FB, bin_step):
        cosine, sine_table = fourier_table(first_bin, bin_step, window_size)
        joined = jnp.concatenate([cosine, sine_table], axis=1)
        product = jnp.dot(stacked_segments, joined, preferred_element_type=jnp.float32).astype(
            jnp.bfloat16
        )
        real_bins.append(product[:, :bin_step])
        imag_bins.append(product[:, bin_step:])
    real_spec = jnp.concatenate(real_bins, axis=1)
    imag_spec = jnp.concatenate(imag_bins, axis=1)
    raw_spectra = jnp.stack([real_spec, imag_spec])
    tap_count = whiten_filter.shape[1]
    rim_width = tap_count // 2
    reach_rows = local_rows + tap_count
    skewed = jnp.pad(whiten_filter, ((0, 0), (0, local_rows + 1))).reshape(-1)
    band_matrix = skewed[: local_rows * reach_rows].reshape(local_rows, reach_rows)
    padded = extended(raw_spectra, ((("chan", "freq"), 1),), rim_width)
    predicted = jnp.einsum("ij,ajk->aik", band_matrix, padded, preferred_element_type=jnp.float32)
    whitened = (raw_spectra.astype(jnp.float32) - predicted).astype(jnp.bfloat16)
    spectra = whitened.reshape(2, local_rows, segment_count, FB)
    tm_count = lax.axis_size("tm")
    freq_count = lax.axis_size("freq")
    pieces = lax.all_to_all(spectra[None], ("tm", "freq"), split_axis=4, concat_axis=0, tiled=True)
    band_width = pieces.shape[-1]
    pieces = pieces.reshape(tm_count, freq_count, 2, local_rows, segment_count, band_width)
    banded = pieces.transpose(2, 1, 3, 0, 4, 5).reshape(
        2, freq_count * local_rows, tm_count * segment_count, band_width
    )
    block_rows = banded.shape[1]
    own_block = banded.reshape(2, block_rows, -1)
    depth = own_block.shape[2]
    scaling = 1.0 / math.sqrt(depth)
    block_index = lax.axis_index("chan")
    slot_list = pair_list[0]
    nearby = []
    for distance in range(-REACH, REACH + 1):
        if distance == 0:
            nearby.append(own_block)
        else:
            nearby.append(shifted(own_block, "chan", -distance))
    stacked = jnp.stack(nearby)

    def fetch_partner(partner_index):
        return lax.dynamic_index_in_dim(
            stacked, partner_index - block_index + REACH, 0, keepdims=False
        )

    left_side = jnp.concatenate([own_block[0], own_block[1]], axis=1)
    flipped = jnp.concatenate([own_block[1], -own_block[0]], axis=1)
    contract = (((1,), (1,)), ((), ()))

    def one_slot(partner_index):
        partner = fetch_partner(partner_index)
        right_side = jnp.concatenate([partner[0], partner[1]], axis=1)
        real_part = (
            lax.dot_general(left_side, right_side, contract, preferred_element_type=jnp.float32)
            * scaling
        )
        imag_part = (
            lax.dot_general(flipped, right_side, contract, preferred_element_type=jnp.float32)
            * scaling
        )
        crossed = jnp.stack([real_part, imag_part])
        return jnp.where(partner_index >= 0, crossed, jnp.zeros((), jnp.float32))

    result = jnp.stack([one_slot(slot_list[slot_index]) for slot_index in range(SLOTS)])
    return result.reshape(1, SLOTS, 1, 2, block_rows, block_rows)


MESH = pl.DeviceIdType.MESH
PIECES = (16, 16, 32, 32, 32)
GROUPS = ((0, 0, 32), (0, 32, 32), (1, 0, 64), (0, 64, 64), (1, 64, 32), (1, 96, 32))
TILE = 32
STEP = 32
SPECTRA_VMEM = 60 * 2**20


def spectra_kernel(
    chan_count,
    scaling,
    rec_ref,
    trail_ref,
    filt_ref,
    pairs_ref,
    out,
    samples,
    filters,
    bands,
    table,
    coarse,
    raw,
    gathered,
    turned,
    guest,
    pairs,
    ready,
    local_sems,
    send_sems,
    span_sems,
    pass_sems,
    core_sems,
    filter_sems,
    block_sems,
    guest_sems,
):
    me = lax.axis_index("chan")
    tm = lax.axis_index("tm")
    core = lax.axis_index("freq")
    rows, hop = rec_ref.shape
    window = 2 * hop
    width = table.shape[1] // 2
    block_rows = 2 * rows
    taps = filt_ref.shape[0]
    rim = taps // 2
    tile_count = block_rows // TILE
    group = rows // 2
    furthest = chan_count - 1
    has_left = me > 0
    has_right = me < chan_count - 1
    other = 1 - core
    other_tm = {"tm": 1 - tm}
    other_core = {"freq": 1 - core}
    left = {"chan": me - 1}
    right = {"chan": me + 1}
    ahead = (has_right, has_left)
    onward = (right, left)
    span_send, pass_send, core_send, swap_send = range(4)
    filter_send, block_send = (4, 5), (6, 7)
    guest_send, share_send = 8, 9
    hosting = jnp.logical_or(me == 0, me == furthest)

    def remote(source, target, send, recv, device):
        return pltpu.make_async_remote_copy(
            src_ref=source,
            dst_ref=target,
            send_sem=send_sems.at[send],
            recv_sem=recv,
            device_id=device,
            device_id_type=MESH,
        )

    def half(which):
        return pl.ds(pl.multiple_of(which * rows, rows), rows)

    barrier = pltpu.get_barrier_semaphore()
    later = ((has_right, right), (tm == 0, other_tm), (core == 1, other_core))
    earlier = ((has_left, left), (tm == 1, other_tm), (core == 0, other_core))
    for near, device in later:

        @pl.when(near)
        def _():
            pl.semaphore_signal(barrier, inc=1, device_id=device, device_id_type=MESH)

    own_copies = [
        pltpu.make_async_copy(rec_ref, samples.at[tm, half(core)], local_sems.at[0]),
        pltpu.make_async_copy(trail_ref, samples.at[2, half(core)], local_sems.at[1]),
        pltpu.make_async_copy(filt_ref, filters.at[me, core], local_sems.at[2]),
        pltpu.make_async_copy(pairs_ref, pairs, local_sems.at[3]),
    ]
    for copy in own_copies:
        copy.start()

    awaited = sum(near.astype(jnp.int32) for near, _ in earlier)

    @pl.when(awaited > 0)
    def _():
        pl.semaphore_wait(barrier, awaited)

    for link, (near, device) in enumerate(earlier):

        @pl.when(near)
        def _():
            pl.semaphore_signal(ready.at[link], inc=1, device_id=device, device_id_type=MESH)

    def meet(link):
        @pl.when(later[link][0])
        def _():
            pl.semaphore_wait(ready.at[link], 1)

    starts = [sum(PIECES[:p]) for p in range(len(PIECES))]

    def place(which, start, count):
        first = (1 - which) * start + which * (rows - start - count)
        return pl.multiple_of(first, math.gcd(start, count, rows))

    def piece_start(which, p):
        return place(which, starts[p], PIECES[p])

    def piece_in_block(which, p):
        start = which * rows + piece_start(which, p)
        return pl.ds(pl.multiple_of(start, math.gcd(starts[p], PIECES[p])), PIECES[p])

    def span_copy(p):
        return remote(
            rec_ref.at[pl.ds(piece_start(core, p), PIECES[p])],
            samples.at[tm, piece_in_block(core, p)],
            span_send,
            span_sems.at[p],
            other_tm,
        )

    meet(1)
    for p in range(len(PIECES)):
        span_copy(p).start()

    def core_copy(index, which):
        source, place = ((rec_ref, tm), (trail_ref, 2))[index]
        at = samples.at[place, half(which)]
        return remote(source, at, core_send, core_sems.at[index], other_core)

    meet(2)
    def lend():
        return remote(filt_ref, filters.at[me, 0], swap_send, core_sems.at[2], other_core)

    @pl.when(core == 0)
    def _():
        lend().start()

    for index in range(2):
        core_copy(index, core).start()

    def source_of(direction, distance):
        source = me - distance if direction == 0 else me + distance
        return jnp.clip(source, 0, chan_count - 1)

    def exists(direction, distance):
        return me - distance >= 0 if direction == 0 else me + distance < chan_count

    def weights_copy(direction, distance, sem):
        at = filters.at[source_of(direction, distance)]
        return remote(
            at,
            at,
            filter_send[direction],
            filter_sems.at[direction, sem],
            onward[direction],
        )

    feeding = (me == furthest - 1, me == 1)

    def guest_copy(tm_index, core_index, send, sem, device):
        at = guest.at[tm_index, core_index]
        return remote(at, at, send, guest_sems.at[sem], device)

    for direction in (1, 0):
        if direction == 0:
            meet(0)

        @pl.when(feeding[direction])
        def _():
            first = pl.multiple_of((1 - core) * group, group)
            share = group // 2
            later_rows = pl.multiple_of(first + tm * share, share)
            for source, start, at, count in (
                (rec_ref, first, 0, group),
                (trail_ref, later_rows, group, share),
            ):
                remote(
                    source.at[pl.ds(start, count)],
                    guest.at[tm, core, at : at + count],
                    guest_send,
                    guest_sems.at[0],
                    onward[direction],
                ).start()

    first_bin = (tm * 2 + core) * width
    unit = 2.0 * math.pi / window
    bins = first_bin + lax.broadcasted_iota(jnp.int32, (1, width), 1)

    def angles(count, scale, factor):
        steps = scale * lax.broadcasted_iota(jnp.int32, (count, width), 0)
        return unit * jnp.bitwise_and(steps * factor, window - 1).astype(jnp.float32)

    parts = window // STEP
    coarse_angle = angles(parts, STEP, bins)
    coarse_turn = angles(parts, STEP, 1)
    coarse[0] = jnp.cos(coarse_angle)
    coarse[1] = jnp.sin(coarse_angle)
    coarse[2] = jnp.cos(coarse_turn)
    coarse[3] = jnp.sin(coarse_turn)
    fine_angle = angles(STEP, 1, bins)
    fine_turn = angles(STEP, 1, 1)
    fine_cos, fine_sin = jnp.cos(fine_angle), jnp.sin(fine_angle)
    turn_cos, turn_sin = jnp.cos(fine_turn), jnp.sin(fine_turn)
    normaliser = 1.0 / math.sqrt(0.375 * window)

    def fill(part, carry):
        c, s, tc, ts = (coarse[k, pl.ds(part, 1), :] for k in range(4))
        taper = (0.5 - 0.5 * (tc * turn_cos - ts * turn_sin)) * normaliser
        at = pl.ds(pl.multiple_of(part * STEP, STEP), STEP)
        table[at, :width] = (taper * (c * fine_cos - s * fine_sin)).astype(jnp.bfloat16)
        table[at, width:] = (-taper * (s * fine_cos + c * fine_sin)).astype(jnp.bfloat16)
        return carry

    lax.fori_loop(0, parts, fill, 0)

    own_copies[2].wait()

    @pl.when(core == 1)
    def _():
        lend().wait_recv()

    for direction in (1, 0):

        @pl.when(jnp.logical_and(ahead[direction], core == 1))
        def _():
            weights_copy(direction, 0, 0).start()

    edge = jnp.zeros((rim, raw.shape[1]), raw.dtype)
    raw[0:rim] = edge
    raw[rim + chan_count * block_rows :] = edge

    for copy in (*own_copies[:2], own_copies[3]):
        copy.wait()
    for index in range(2):
        core_copy(index, other).wait_recv()

    def own_rows(block, start, count):
        return pl.ds(pl.multiple_of(rim + block * block_rows + start, 16), count)

    def block_copy(at, direction, distance, index):
        place = raw.at[at]
        return remote(
            place,
            place,
            block_send[direction],
            block_sems.at[direction, distance, index],
            onward[direction],
        )

    def group_rows(direction, distance, index):
        which, start, count = GROUPS[index]
        here = core if which == 0 else other
        start = here * rows + place(here, start, count)
        return own_rows(source_of(direction, distance), start, count)

    def fill_rows(where, count, early, late):
        product = jnp.dot(early, table[:hop], preferred_element_type=jnp.float32) + jnp.dot(
            late, table[hop:], preferred_element_type=jnp.float32
        )
        product = product.astype(jnp.bfloat16)
        for segment in range(2):
            found = product[segment * count : (segment + 1) * count]
            raw[where, segment * width : (segment + 1) * width] = found[:, :width]
            raw[where, (2 + segment) * width : (3 + segment) * width] = found[:, width:]

    def group_of(which, p):
        return next(
            index
            for index, (side, start, count) in enumerate(GROUPS)
            if side == which and start <= starts[p] < start + count
        )

    def transform(which, p, index):
        at = which * rows + piece_start(which, p)
        chosen = piece_in_block(which, p)
        count = PIECES[p]
        where = own_rows(me, at, count)
        fill_rows(
            where,
            count,
            samples[0:2, chosen].reshape(2 * count, hop),
            samples[1:3, chosen].reshape(2 * count, hop),
        )
        for direction in (1, 0):
            wanted = ahead[direction]
            if starts[p] >= group:
                wanted = jnp.logical_and(wanted, jnp.logical_not(feeding[direction]))

            @pl.when(wanted)
            def _():
                block_copy(where, direction, 0, index).start()

    def guest_transform(which):
        first, second = guest[0, which, :group], guest[1, which, :group]
        third = jnp.concatenate([guest[0, which, group:], guest[1, which, group:]], axis=0)
        near = jnp.where(me == 0, 1, furthest - 1)
        fill_rows(
            own_rows(near, which * rows + (1 - which) * group, group),
            group,
            jnp.concatenate([first, second], axis=0),
            jnp.concatenate([second, third], axis=0),
        )

    def take_weights(distance):
        for direction in (1, 0):

            @pl.when(jnp.logical_and(exists(direction, distance), core == 1))
            def _():
                weights_copy(direction, distance, distance - 1).wait_recv()

            if distance < furthest:

                onwards = jnp.logical_and(exists(direction, distance), ahead[direction])

                @pl.when(jnp.logical_and(onwards, core == 1))
                def _():
                    weights_copy(direction, distance, distance).start()

    def passed(which, p):
        at = samples.at[1 - tm, piece_in_block(which, p)]
        return remote(at, at, pass_send, pass_sems.at[p], other_core)

    def arrive(distance, index):
        for direction in (1, 0):
            at = group_rows(direction, distance, index)

            expected = exists(direction, distance)
            if distance == 1 and GROUPS[index][1] >= group:
                expected = jnp.logical_and(expected, jnp.logical_not(hosting))

            @pl.when(expected)
            def _():
                block_copy(at, direction, distance - 1, index).wait_recv()

            if distance < furthest:

                @pl.when(jnp.logical_and(exists(direction, distance), ahead[direction]))
                def _():
                    block_copy(at, direction, distance, index).start()

    def own_piece(p):
        span_copy(p).wait_recv()
        passed(core, p).start()
        transform(core, p, group_of(0, p))

    def other_piece(p):
        passed(other, p).wait_recv()
        transform(other, p, group_of(1, p))

    own_piece(0)
    own_piece(1)
    other_piece(0)
    own_piece(2)
    other_piece(1)
    take_weights(1)
    own_piece(3)
    other_piece(2)
    arrive(1, 0)
    own_piece(4)
    other_piece(3)
    arrive(1, 1)
    other_piece(4)
    take_weights(2)

    @pl.when(hosting)
    def _():
        guest_copy(tm, core, guest_send, 0, other_tm).wait_recv()
        guest_copy(tm, core, guest_send, 1, other_tm).start()
        guest_copy(tm, core, share_send, 2, other_core).start()

    def spread(block, carry):
        for which in range(2):
            weights = jnp.transpose(filters[block, which].astype(jnp.float32))
            wide = jnp.concatenate([weights, jnp.zeros((rows, 128 - taps), jnp.float32)], axis=1)
            for p in range(tile_count // 2):
                rolled = pltpu.roll(
                    wide[p * TILE : (p + 1) * TILE], 0, 1, stride=1, stride_axis=0
                )
                bands[block, which * tile_count // 2 + p] = rolled.astype(jnp.bfloat16)
        return carry

    def whiten(block, tile):
        start = pl.multiple_of(block * block_rows + tile * TILE, TILE)
        near = raw[pl.ds(start, TILE + taps)]
        predicted = jnp.dot(
            bands[block, tile][:, : TILE + taps], near, preferred_element_type=jnp.float32
        )
        mine = near[rim : rim + TILE].astype(jnp.float32)
        gathered[block, tile * TILE : (tile + 1) * TILE] = (mine - predicted).astype(
            jnp.bfloat16
        )

    contract = (((1,), (1,)), ((), ()))

    def cross(block, first=False):
        partner = gathered[block]
        for part, side in enumerate((gathered[me], turned[...])):
            product = (
                lax.dot_general(side, partner, contract, preferred_element_type=jnp.float32)
                * scaling
            )
            for slot in range(SLOTS):
                before = jnp.zeros_like(product) if first else out[slot, part]
                out[slot, part] = jnp.where(pairs[0, slot] == block, product, before)

    def finish_own():
        for tile in range(tile_count):
            whiten(me, tile)
        own = gathered[me]
        middle = own.shape[1] // 2
        turned[...] = jnp.concatenate([own[:, middle:], -own[:, :middle]], axis=1)
        cross(me, True)

    def inner(distance):
        for direction in (1, 0):

            @pl.when(exists(direction, distance))
            def _():
                block = me - distance if direction == 0 else me + distance
                for tile in range(tile_count - 1):
                    whiten(block, tile + 1 if direction == 0 else tile)

    def finish(distance):
        for direction in (1, 0):

            @pl.when(exists(direction, distance))
            def _():
                block = me - distance if direction == 0 else me + distance
                whiten(block, 0 if direction == 0 else tile_count - 1)
                cross(block)

    def hand():
        return remote(filters, filters, swap_send, core_sems.at[2], other_core)

    for index in range(2, len(GROUPS)):
        arrive(1, index)
    take_weights(3)

    @pl.when(core == 1)
    def _():
        hand().start()

    for index in range(3):
        arrive(2, index)

    @pl.when(core == 0)
    def _():
        hand().wait_recv()

    lax.fori_loop(0, chan_count, spread, 0)
    arrive(2, 3)
    finish_own()
    for index in range(4, len(GROUPS)):
        arrive(2, index)

    @pl.when(hosting)
    def _():
        guest_copy(1 - tm, core, guest_send, 1, other_tm).wait_recv()
        guest_copy(1 - tm, core, share_send, 3, other_core).start()

    arrive(3, 0)
    arrive(3, 1)

    @pl.when(hosting)
    def _():
        guest_copy(tm, other, share_send, 2, other_core).wait_recv()
        guest_transform(core)
        guest_copy(1 - tm, other, share_send, 3, other_core).wait_recv()
        guest_transform(other)

    inner(1)
    finish(1)
    arrive(3, 2)
    inner(2)
    finish(2)
    for index in range(3, len(GROUPS)):
        arrive(3, index)
    inner(3)
    finish(3)

    guest_copy(tm, core, guest_send, 1, other_tm).wait_send()

    @pl.when(hosting)
    def _():
        shared = guest.at[0:2, core]
        remote(shared, shared, share_send, guest_sems.at[2], other_core).wait_send()

    whole = samples.at[tm, half(core)]
    remote(whole, whole, span_send, span_sems.at[0], other_tm).wait_send()
    remote(whole, whole, pass_send, pass_sems.at[0], other_core).wait_send()
    both = samples.at[0:2, half(core)]
    remote(both, both, core_send, core_sems.at[0], other_core).wait_send()

    @pl.when(core == 0)
    def _():
        lend().wait_send()

    @pl.when(core == 1)
    def _():
        hand().wait_send()

    for direction in (1, 0):
        for count in range(1, chan_count):

            @pl.when(me == (count - 1 if direction == 0 else chan_count - count))
            def _():
                @pl.when(core == 1)
                def _():
                    sent = filters.at[0:count]
                    remote(
                        sent, sent, filter_send[direction], filter_sems.at[0, 0], onward[direction]
                    ).wait_send()

                fed = rows if count == furthest else 0
                sent = raw.at[0 : count * block_rows - fed]
                remote(
                    sent, sent, block_send[direction], block_sems.at[0, 0, 0], onward[direction]
                ).wait_send()


def fused(recording, trailing, whiten_filter, pair_list):
    rows, hop = recording.shape
    chan_count = lax.axis_size("chan")
    taps = whiten_filter.shape[1]
    width = FB // (lax.axis_size("tm") * lax.axis_size("freq"))
    block_rows = 2 * rows
    depth = 2 * width
    vmem = pl.BlockSpec(memory_space=pltpu.VMEM)
    hbm = pl.BlockSpec(memory_space=pltpu.HBM)
    slots = pl.pallas_call(
        functools.partial(spectra_kernel, chan_count, 1.0 / math.sqrt(depth)),
        out_shape=pltpu.VMEM((SLOTS, 2, block_rows, block_rows), jnp.float32),
        in_specs=[hbm] * 4,
        out_specs=vmem,
        scratch_shapes=[
            pltpu.VMEM((3, block_rows, hop), jnp.bfloat16),
            pltpu.VMEM((chan_count, 2, taps, rows), jnp.bfloat16),
            pltpu.VMEM((chan_count, block_rows // TILE, TILE, 128), jnp.bfloat16),
            pltpu.VMEM((2 * hop, 2 * width), jnp.bfloat16),
            pltpu.VMEM((4, 2 * hop // STEP, width), jnp.float32),
            pltpu.VMEM((chan_count * block_rows + taps, 2 * depth), jnp.bfloat16),
            pltpu.VMEM((chan_count, block_rows, 2 * depth), jnp.bfloat16),
            pltpu.VMEM((block_rows, 2 * depth), jnp.bfloat16),
            pltpu.VMEM((2, 2, 3 * rows // 4, hop), jnp.bfloat16),
            pltpu.SMEM((1, SLOTS), jnp.int32),
            pltpu.SemaphoreType.REGULAR((3,)),
            pltpu.SemaphoreType.DMA((4,)),
            pltpu.SemaphoreType.DMA((10,)),
            pltpu.SemaphoreType.DMA((len(PIECES),)),
            pltpu.SemaphoreType.DMA((len(PIECES),)),
            pltpu.SemaphoreType.DMA((3,)),
            pltpu.SemaphoreType.DMA((2, chan_count - 1)),
            pltpu.SemaphoreType.DMA((2, chan_count - 1, len(GROUPS))),
            pltpu.SemaphoreType.DMA((4,)),
        ],
        compiler_params=pltpu.CompilerParams(
            collective_id=0, has_side_effects=True, vmem_limit_bytes=SPECTRA_VMEM
        ),
    )(recording, trailing, whiten_filter.T, pair_list)
    return slots.reshape(1, SLOTS, 1, 2, block_rows, block_rows)


def local(recording, trailing, whiten_filter, pair_list):
    shapes = (recording.shape, trailing.shape, whiten_filter.shape)
    counts = (lax.axis_size("tm"), lax.axis_size("freq"))
    whole_reach = lax.axis_size("chan") == REACH + 1
    if shapes == ((128, 1024), (128, 1024), (128, 64)) and counts == (2, 2) and whole_reach:
        return fused(recording, trailing, whiten_filter, pair_list)
    return general(recording, trailing, whiten_filter, pair_list)


def solution(mesh):
    placed = (
        P(("days", "chan", "freq"), "tm"),
        P(("days", "chan", "freq"), None),
        P(("chan", "freq"), None),
        P(("days", "chan"), None),
    )
    return jax.shard_map(
        local,
        mesh=mesh,
        in_specs=placed,
        out_specs=P(("days", "chan"), None, ("tm", "freq"), None, None, None),
        check_vma=False,
    )
```

```python
import functools
import math

import jax
import jax.numpy as jnp
from jax import lax
from jax.experimental import pallas as pl
from jax.experimental.pallas import tpu as pltpu
from jax.sharding import PartitionSpec as P

FB = 512
REACH = 3
SLOTS = 4


def shifted(block, axis, distance):
    devices = range(lax.axis_size(axis))
    route = [(i - distance, i) for i in devices if i - distance in devices]
    return lax.ppermute(block, axis, route)


def extended(value, sides, width):
    for axis, dim in sides:
        size, length = (lax.axis_size(axis), value.shape[dim])
        up = [(i, (i + 1) % size) for i in range(size - 1)]
        down = [(j, i) for i, j in up]
        last = lax.slice_in_dim(value, length - width, length, axis=dim)
        initial = lax.slice_in_dim(value, 0, width, axis=dim)
        before = lax.ppermute(last, axis, up)
        after = lax.ppermute(initial, axis, down)
        value = jnp.concatenate([before, value, after], axis=dim)
    return value


def fourier_table(first_bin, bin_count, length):
    samples = jnp.arange(length, dtype=jnp.int32)[:, None]
    bin_index = first_bin + jnp.arange(bin_count, dtype=jnp.int32)[None, :]
    phase = samples * bin_index % length
    angle = 2.0 * math.pi / length * phase.astype(jnp.float32)
    taper = 0.5 - 0.5 * jnp.cos(
        2.0 * math.pi / length * jnp.arange(length, dtype=jnp.int32).astype(jnp.float32)
    )
    normaliser = 1.0 / math.sqrt(0.375 * length)
    cosine = (taper[:, None] * jnp.cos(angle) * normaliser).astype(jnp.bfloat16)
    sine_table = (-taper[:, None] * jnp.sin(angle) * normaliser).astype(jnp.bfloat16)
    return (cosine, sine_table)


def general(recording, trailing, whiten_filter, pair_list):
    local_rows, local_span = recording.shape
    hop_size = trailing.shape[1]
    window_size = 2 * hop_size
    segment_count = local_span // hop_size
    following = shifted(recording, "tm", -1)
    is_last = lax.axis_index("tm") == lax.axis_size("tm") - 1
    following = jnp.where(is_last, trailing, following)
    signal = jnp.concatenate([recording, following], axis=1)
    segments = jnp.stack([signal], axis=1)
    stacked_segments = segments.reshape(local_rows * segment_count, window_size)
    bin_step = min(256, FB)
    real_bins = []
    imag_bins = []
    for first_bin in range(0, FB, bin_step):
        cosine, sine_table = fourier_table(first_bin, bin_step, window_size)
        joined = jnp.concatenate([cosine, sine_table], axis=1)
        product = jnp.dot(stacked_segments, joined, preferred_element_type=jnp.float32).astype(
            jnp.bfloat16
        )
        real_bins.append(product[:, :bin_step])
        imag_bins.append(product[:, bin_step:])
    real_spec = jnp.concatenate(real_bins, axis=1)
    imag_spec = jnp.concatenate(imag_bins, axis=1)
    raw_spectra = jnp.stack([real_spec, imag_spec])
    tap_count = whiten_filter.shape[1]
    rim_width = tap_count // 2
    reach_rows = local_rows + tap_count
    skewed = jnp.pad(whiten_filter, ((0, 0), (0, local_rows + 1))).reshape(-1)
    band_matrix = skewed[: local_rows * reach_rows].reshape(local_rows, reach_rows)
    padded = extended(raw_spectra, ((("chan", "freq"), 1),), rim_width)
    predicted = jnp.einsum("ij,ajk->aik", band_matrix, padded, preferred_element_type=jnp.float32)
    whitened = (raw_spectra.astype(jnp.float32) - predicted).astype(jnp.bfloat16)
    spectra = whitened.reshape(2, local_rows, segment_count, FB)
    tm_count = lax.axis_size("tm")
    freq_count = lax.axis_size("freq")
    pieces = lax.all_to_all(spectra[None], ("tm", "freq"), split_axis=4, concat_axis=0, tiled=True)
    band_width = pieces.shape[-1]
    pieces = pieces.reshape(tm_count, freq_count, 2, local_rows, segment_count, band_width)
    banded = pieces.transpose(2, 1, 3, 0, 4, 5).reshape(
        2, freq_count * local_rows, tm_count * segment_count, band_width
    )
    block_rows = banded.shape[1]
    own_block = banded.reshape(2, block_rows, -1)
    depth = own_block.shape[2]
    scaling = 1.0 / math.sqrt(depth)
    block_index = lax.axis_index("chan")
    slot_list = pair_list[0]
    nearby = []
    for distance in range(-REACH, REACH + 1):
        if distance == 0:
            nearby.append(own_block)
        else:
            nearby.append(shifted(own_block, "chan", -distance))
    stacked = jnp.stack(nearby)

    def fetch_partner(partner_index):
        return lax.dynamic_index_in_dim(
            stacked, partner_index - block_index + REACH, 0, keepdims=False
        )

    left_side = jnp.concatenate([own_block[0], own_block[1]], axis=1)
    flipped = jnp.concatenate([own_block[1], -own_block[0]], axis=1)
    contract = (((1,), (1,)), ((), ()))

    def one_slot(partner_index):
        partner = fetch_partner(partner_index)
        right_side = jnp.concatenate([partner[0], partner[1]], axis=1)
        real_part = (
            lax.dot_general(left_side, right_side, contract, preferred_element_type=jnp.float32)
            * scaling
        )
        imag_part = (
            lax.dot_general(flipped, right_side, contract, preferred_element_type=jnp.float32)
            * scaling
        )
        crossed = jnp.stack([real_part, imag_part])
        return jnp.where(partner_index >= 0, crossed, jnp.zeros((), jnp.float32))

    result = jnp.stack([one_slot(slot_list[slot_index]) for slot_index in range(SLOTS)])
    return result.reshape(1, SLOTS, 1, 2, block_rows, block_rows)


MESH = pl.DeviceIdType.MESH
PIECES = (16, 16, 32, 32, 32)
GROUPS = ((0, 0, 32), (0, 32, 32), (1, 0, 64), (0, 64, 64), (1, 64, 32), (1, 96, 32))
TILE = 32
STEP = 32
SPECTRA_VMEM = 60 * 2**20


def spectra_kernel(
    chan_count,
    scaling,
    rec_ref,
    trail_ref,
    filt_ref,
    pairs_ref,
    out,
    samples,
    filters,
    bands,
    table,
    coarse,
    raw,
    gathered,
    sides,
    guest,
    pairs,
    ready,
    local_sems,
    send_sems,
    span_sems,
    pass_sems,
    core_sems,
    filter_sems,
    block_sems,
    guest_sems,
):
    me = lax.axis_index("chan")
    tm = lax.axis_index("tm")
    core = lax.axis_index("freq")
    rows, hop = rec_ref.shape
    window = 2 * hop
    width = table.shape[1] // 2
    block_rows = 2 * rows
    taps = filt_ref.shape[0]
    rim = taps // 2
    tile_count = block_rows // TILE
    group = rows // 2
    furthest = chan_count - 1
    has_left = me > 0
    has_right = me < chan_count - 1
    other = 1 - core
    other_tm = {"tm": 1 - tm}
    other_core = {"freq": 1 - core}
    left = {"chan": me - 1}
    right = {"chan": me + 1}
    ahead = (has_right, has_left)
    onward = (right, left)
    span_send, pass_send, core_send, swap_send = range(4)
    filter_send, block_send = (4, 5), (6, 7)
    guest_send, share_send = 8, 9
    hosting = jnp.logical_or(me == 0, me == furthest)

    def remote(source, target, send, recv, device):
        return pltpu.make_async_remote_copy(
            src_ref=source,
            dst_ref=target,
            send_sem=send_sems.at[send],
            recv_sem=recv,
            device_id=device,
            device_id_type=MESH,
        )

    def half(which):
        return pl.ds(pl.multiple_of(which * rows, rows), rows)

    barrier = pltpu.get_barrier_semaphore()
    later = ((has_right, right), (tm == 0, other_tm), (core == 1, other_core))
    earlier = ((has_left, left), (tm == 1, other_tm), (core == 0, other_core))
    for near, device in later:

        @pl.when(near)
        def _():
            pl.semaphore_signal(barrier, inc=1, device_id=device, device_id_type=MESH)

    own_copies = [
        pltpu.make_async_copy(rec_ref, samples.at[tm, half(core)], local_sems.at[0]),
        pltpu.make_async_copy(trail_ref, samples.at[2, half(core)], local_sems.at[1]),
        pltpu.make_async_copy(filt_ref, filters.at[me, core], local_sems.at[2]),
        pltpu.make_async_copy(pairs_ref, pairs, local_sems.at[3]),
    ]
    for copy in own_copies:
        copy.start()

    awaited = sum(near.astype(jnp.int32) for near, _ in earlier)

    @pl.when(awaited > 0)
    def _():
        pl.semaphore_wait(barrier, awaited)

    for link, (near, device) in enumerate(earlier):

        @pl.when(near)
        def _():
            pl.semaphore_signal(ready.at[link], inc=1, device_id=device, device_id_type=MESH)

    def meet(link):
        @pl.when(later[link][0])
        def _():
            pl.semaphore_wait(ready.at[link], 1)

    starts = [sum(PIECES[:p]) for p in range(len(PIECES))]

    def place(which, start, count):
        first = (1 - which) * start + which * (rows - start - count)
        return pl.multiple_of(first, math.gcd(start, count, rows))

    def piece_start(which, p):
        return place(which, starts[p], PIECES[p])

    def piece_in_block(which, p):
        start = which * rows + piece_start(which, p)
        return pl.ds(pl.multiple_of(start, math.gcd(starts[p], PIECES[p])), PIECES[p])

    def span_copy(p):
        return remote(
            rec_ref.at[pl.ds(piece_start(core, p), PIECES[p])],
            samples.at[tm, piece_in_block(core, p)],
            span_send,
            span_sems.at[p],
            other_tm,
        )

    meet(1)
    for p in range(len(PIECES)):
        span_copy(p).start()

    def core_copy(index, which):
        source, place = ((rec_ref, tm), (trail_ref, 2))[index]
        at = samples.at[place, half(which)]
        return remote(source, at, core_send, core_sems.at[index], other_core)

    meet(2)
    def lend():
        return remote(filt_ref, filters.at[me, 0], swap_send, core_sems.at[2], other_core)

    @pl.when(core == 0)
    def _():
        lend().start()

    for index in range(2):
        core_copy(index, core).start()

    def source_of(direction, distance):
        source = me - distance if direction == 0 else me + distance
        return jnp.clip(source, 0, chan_count - 1)

    def exists(direction, distance):
        return me - distance >= 0 if direction == 0 else me + distance < chan_count

    def weights_copy(direction, distance):
        source = source_of(direction, distance)
        at = filters.at[source]
        return remote(
            at,
            at,
            filter_send[direction],
            filter_sems.at[source],
            onward[direction],
        )

    feeding = (me == furthest - 1, me == 1)

    def guest_copy(tm_index, core_index, send, sem, device):
        at = guest.at[tm_index, core_index]
        return remote(at, at, send, guest_sems.at[sem], device)

    for direction in (1, 0):
        if direction == 0:
            meet(0)

        @pl.when(feeding[direction])
        def _():
            first = pl.multiple_of((1 - core) * group, group)
            share = group // 2
            later_rows = pl.multiple_of(first + tm * share, share)
            for source, start, at, count in (
                (rec_ref, first, 0, group),
                (trail_ref, later_rows, group, share),
            ):
                remote(
                    source.at[pl.ds(start, count)],
                    guest.at[tm, core, at : at + count],
                    guest_send,
                    guest_sems.at[0],
                    onward[direction],
                ).start()

    first_bin = (tm * 2 + core) * width
    unit = 2.0 * math.pi / window
    bins = first_bin + lax.broadcasted_iota(jnp.int32, (1, width), 1)

    def angles(count, scale, factor):
        steps = scale * lax.broadcasted_iota(jnp.int32, (count, width), 0)
        return unit * jnp.bitwise_and(steps * factor, window - 1).astype(jnp.float32)

    parts = window // STEP
    coarse_angle = angles(parts, STEP, bins)
    coarse_turn = angles(parts, STEP, 1)
    coarse[0] = jnp.cos(coarse_angle)
    coarse[1] = jnp.sin(coarse_angle)
    coarse[2] = jnp.cos(coarse_turn)
    coarse[3] = jnp.sin(coarse_turn)
    fine_angle = angles(STEP, 1, bins)
    fine_turn = angles(STEP, 1, 1)
    fine_cos, fine_sin = jnp.cos(fine_angle), jnp.sin(fine_angle)
    turn_cos, turn_sin = jnp.cos(fine_turn), jnp.sin(fine_turn)
    normaliser = 1.0 / math.sqrt(0.375 * window)

    def fill(part, carry):
        c, s, tc, ts = (coarse[k, pl.ds(part, 1), :] for k in range(4))
        taper = (0.5 - 0.5 * (tc * turn_cos - ts * turn_sin)) * normaliser
        at = pl.ds(pl.multiple_of(part * STEP, STEP), STEP)
        table[at, :width] = (taper * (c * fine_cos - s * fine_sin)).astype(jnp.bfloat16)
        table[at, width:] = (-taper * (s * fine_cos + c * fine_sin)).astype(jnp.bfloat16)
        return carry

    lax.fori_loop(0, parts, fill, 0)

    own_copies[2].wait()

    @pl.when(core == 1)
    def _():
        lend().wait_recv()

    for direction in (1, 0):

        @pl.when(jnp.logical_and(ahead[direction], core == 1))
        def _():
            weights_copy(direction, 0).start()

    edge = jnp.zeros((rim, raw.shape[1]), raw.dtype)
    raw[0:rim] = edge
    raw[rim + chan_count * block_rows :] = edge

    for copy in (*own_copies[:2], own_copies[3]):
        copy.wait()
    for index in range(2):
        core_copy(index, other).wait_recv()

    def own_rows(block, start, count):
        return pl.ds(pl.multiple_of(rim + block * block_rows + start, 16), count)

    def block_copy(at, direction, distance, index):
        place = raw.at[at]
        return remote(
            place,
            place,
            block_send[direction],
            block_sems.at[source_of(direction, distance), index],
            onward[direction],
        )

    def group_rows(direction, distance, index):
        which, start, count = GROUPS[index]
        here = core if which == 0 else other
        start = here * rows + place(here, start, count)
        return own_rows(source_of(direction, distance), start, count)

    def fill_rows(where, count, early, late):
        product = jnp.dot(early, table[:hop], preferred_element_type=jnp.float32) + jnp.dot(
            late, table[hop:], preferred_element_type=jnp.float32
        )
        product = product.astype(jnp.bfloat16)
        for segment in range(2):
            found = product[segment * count : (segment + 1) * count]
            raw[where, segment * width : (segment + 1) * width] = found[:, :width]
            raw[where, (2 + segment) * width : (3 + segment) * width] = found[:, width:]

    def group_of(which, p):
        return next(
            index
            for index, (side, start, count) in enumerate(GROUPS)
            if side == which and start <= starts[p] < start + count
        )

    def transform(which, p, index):
        at = which * rows + piece_start(which, p)
        chosen = piece_in_block(which, p)
        count = PIECES[p]
        where = own_rows(me, at, count)
        fill_rows(
            where,
            count,
            samples[0:2, chosen].reshape(2 * count, hop),
            samples[1:3, chosen].reshape(2 * count, hop),
        )
        for direction in (1, 0):
            wanted = ahead[direction]
            if starts[p] >= group:
                wanted = jnp.logical_and(wanted, jnp.logical_not(feeding[direction]))

            @pl.when(wanted)
            def _():
                block_copy(where, direction, 0, index).start()

    def guest_transform(which):
        first, second = guest[0, which, :group], guest[1, which, :group]
        third = jnp.concatenate([guest[0, which, group:], guest[1, which, group:]], axis=0)
        near = jnp.where(me == 0, 1, furthest - 1)
        fill_rows(
            own_rows(near, which * rows + (1 - which) * group, group),
            group,
            jnp.concatenate([first, second], axis=0),
            jnp.concatenate([second, third], axis=0),
        )

    def take_weights(distance):
        for direction in (1, 0):

            @pl.when(jnp.logical_and(exists(direction, distance), core == 1))
            def _():
                weights_copy(direction, distance).wait_recv()

            if distance < furthest:

                onwards = jnp.logical_and(exists(direction, distance), ahead[direction])

                @pl.when(jnp.logical_and(onwards, core == 1))
                def _():
                    weights_copy(direction, distance).start()

    def passed(which, p):
        at = samples.at[1 - tm, piece_in_block(which, p)]
        return remote(at, at, pass_send, pass_sems.at[p], other_core)

    def arrive(distance, index):
        for direction in (1, 0):
            at = group_rows(direction, distance, index)

            expected = exists(direction, distance)
            if distance == 1 and GROUPS[index][1] >= group:
                expected = jnp.logical_and(expected, jnp.logical_not(hosting))

            @pl.when(expected)
            def _():
                block_copy(at, direction, distance, index).wait_recv()

            if distance < furthest:

                @pl.when(jnp.logical_and(exists(direction, distance), ahead[direction]))
                def _():
                    block_copy(at, direction, distance, index).start()

    def own_piece(p):
        span_copy(p).wait_recv()
        passed(core, p).start()
        transform(core, p, group_of(0, p))

    def other_piece(p):
        passed(other, p).wait_recv()
        transform(other, p, group_of(1, p))

    own_piece(0)
    own_piece(1)
    other_piece(0)
    own_piece(2)
    other_piece(1)
    take_weights(1)
    own_piece(3)
    other_piece(2)
    arrive(1, 0)
    own_piece(4)
    other_piece(3)
    arrive(1, 1)
    other_piece(4)
    take_weights(2)

    @pl.when(hosting)
    def _():
        guest_copy(tm, core, guest_send, 0, other_tm).wait_recv()
        guest_copy(tm, core, guest_send, 1, other_tm).start()
        guest_copy(tm, core, share_send, 2, other_core).start()

    def spread(block, carry):
        for which in range(2):
            weights = jnp.transpose(filters[block, which].astype(jnp.float32))
            wide = jnp.concatenate([weights, jnp.zeros((rows, 128 - taps), jnp.float32)], axis=1)
            for p in range(tile_count // 2):
                rolled = pltpu.roll(
                    wide[p * TILE : (p + 1) * TILE], 0, 1, stride=1, stride_axis=0
                )
                bands[block, which * tile_count // 2 + p] = rolled.astype(jnp.bfloat16)
        return carry

    def whiten(block, tile):
        start = pl.multiple_of(block * block_rows + tile * TILE, TILE)
        at = pl.ds(pl.multiple_of(tile * TILE, TILE), TILE)
        near = raw[pl.ds(start, TILE + taps)]
        predicted = jnp.dot(
            bands[block, tile][:, : TILE + taps], near, preferred_element_type=jnp.float32
        )
        mine = near[rim : rim + TILE].astype(jnp.float32)
        gathered[block, at] = (mine - predicted).astype(jnp.bfloat16)

    contract = (((1,), (1,)), ((), ()))

    def cross(block, first=False):
        partner = gathered[block]
        both = lax.dot_general(sides[...], partner, contract, preferred_element_type=jnp.float32)
        for part in range(2):
            product = both[part * block_rows : (part + 1) * block_rows] * scaling
            for slot in range(SLOTS):
                before = jnp.zeros_like(product) if first else out[slot, part]
                out[slot, part] = jnp.where(pairs[0, slot] == block, product, before)

    def finish_own():
        for tile in range(tile_count):
            whiten(me, tile)
        own = gathered[me]
        middle = own.shape[1] // 2
        sides[:block_rows] = own
        sides[block_rows:] = jnp.concatenate([own[:, middle:], -own[:, :middle]], axis=1)
        cross(me, True)

    def inner(distance):
        for direction in (1, 0):

            @pl.when(exists(direction, distance))
            def _():
                block = me - distance if direction == 0 else me + distance
                for tile in range(tile_count - 1):
                    whiten(block, tile + 1 if direction == 0 else tile)

    def finish(distance):
        for direction in (1, 0):

            @pl.when(exists(direction, distance))
            def _():
                block = me - distance if direction == 0 else me + distance
                whiten(block, 0 if direction == 0 else tile_count - 1)
                cross(block)

    def hand():
        return remote(filters, filters, swap_send, core_sems.at[2], other_core)

    for index in range(2, len(GROUPS)):
        arrive(1, index)
    take_weights(3)

    @pl.when(core == 1)
    def _():
        hand().start()

    for index in range(len(GROUPS)):
        arrive(2, index)

    @pl.when(hosting)
    def _():
        guest_copy(1 - tm, core, guest_send, 1, other_tm).wait_recv()
        guest_copy(1 - tm, core, share_send, 3, other_core).start()

    @pl.when(core == 0)
    def _():
        hand().wait_recv()

    lax.fori_loop(0, chan_count, spread, 0)
    finish_own()
    arrive(3, 0)
    arrive(3, 1)

    @pl.when(hosting)
    def _():
        guest_copy(tm, other, share_send, 2, other_core).wait_recv()
        guest_transform(core)
        guest_copy(1 - tm, other, share_send, 3, other_core).wait_recv()
        guest_transform(other)

    inner(1)
    finish(1)
    arrive(3, 2)
    inner(2)
    finish(2)
    for index in range(3, len(GROUPS) - 1):
        arrive(3, index)

    def last(tiles, complete):
        for direction in (1, 0):

            @pl.when(exists(direction, furthest))
            def _():
                block = me - furthest if direction == 0 else me + furthest
                for tile in tiles:
                    whiten(block, tile)
                if complete:
                    cross(block)

    last((0, 1, 2 + 3 * core, 6, 7), False)
    arrive(3, len(GROUPS) - 1)
    last([3 - core + tile for tile in range(3)], True)

    guest_copy(tm, core, guest_send, 1, other_tm).wait_send()

    @pl.when(hosting)
    def _():
        shared = guest.at[0:2, core]
        remote(shared, shared, share_send, guest_sems.at[2], other_core).wait_send()

    whole = samples.at[tm, half(core)]
    remote(whole, whole, span_send, span_sems.at[0], other_tm).wait_send()
    remote(whole, whole, pass_send, pass_sems.at[0], other_core).wait_send()
    both = samples.at[0:2, half(core)]
    remote(both, both, core_send, core_sems.at[0], other_core).wait_send()

    @pl.when(core == 0)
    def _():
        lend().wait_send()

    @pl.when(core == 1)
    def _():
        hand().wait_send()

    for direction in (1, 0):
        for count in range(1, chan_count):

            @pl.when(me == (count - 1 if direction == 0 else chan_count - count))
            def _():
                @pl.when(core == 1)
                def _():
                    sent = filters.at[0:count]
                    remote(
                        sent, sent, filter_send[direction], filter_sems.at[0], onward[direction]
                    ).wait_send()

                fed = rows if count == furthest else 0
                sent = raw.at[0 : count * block_rows - fed]
                remote(
                    sent, sent, block_send[direction], block_sems.at[0, 0], onward[direction]
                ).wait_send()


def fused(recording, trailing, whiten_filter, pair_list):
    rows, hop = recording.shape
    chan_count = lax.axis_size("chan")
    taps = whiten_filter.shape[1]
    width = FB // (lax.axis_size("tm") * lax.axis_size("freq"))
    block_rows = 2 * rows
    depth = 2 * width
    vmem = pl.BlockSpec(memory_space=pltpu.VMEM)
    hbm = pl.BlockSpec(memory_space=pltpu.HBM)
    slots = pl.pallas_call(
        functools.partial(spectra_kernel, chan_count, 1.0 / math.sqrt(depth)),
        out_shape=pltpu.VMEM((SLOTS, 2, block_rows, block_rows), jnp.float32),
        in_specs=[hbm] * 4,
        out_specs=vmem,
        scratch_shapes=[
            pltpu.VMEM((3, block_rows, hop), jnp.bfloat16),
            pltpu.VMEM((chan_count, 2, taps, rows), jnp.bfloat16),
            pltpu.VMEM((chan_count, block_rows // TILE, TILE, 128), jnp.bfloat16),
            pltpu.VMEM((2 * hop, 2 * width), jnp.bfloat16),
            pltpu.VMEM((4, 2 * hop // STEP, width), jnp.float32),
            pltpu.VMEM((chan_count * block_rows + taps, 2 * depth), jnp.bfloat16),
            pltpu.VMEM((chan_count, block_rows, 2 * depth), jnp.bfloat16),
            pltpu.VMEM((2 * block_rows, 2 * depth), jnp.bfloat16),
            pltpu.VMEM((2, 2, 3 * rows // 4, hop), jnp.bfloat16),
            pltpu.SMEM((1, SLOTS), jnp.int32),
            pltpu.SemaphoreType.REGULAR((3,)),
            pltpu.SemaphoreType.DMA((4,)),
            pltpu.SemaphoreType.DMA((10,)),
            pltpu.SemaphoreType.DMA((len(PIECES),)),
            pltpu.SemaphoreType.DMA((len(PIECES),)),
            pltpu.SemaphoreType.DMA((3,)),
            pltpu.SemaphoreType.DMA((chan_count,)),
            pltpu.SemaphoreType.DMA((chan_count, len(GROUPS))),
            pltpu.SemaphoreType.DMA((4,)),
        ],
        compiler_params=pltpu.CompilerParams(
            collective_id=0, has_side_effects=True, vmem_limit_bytes=SPECTRA_VMEM
        ),
    )(recording, trailing, whiten_filter.T, pair_list)
    return slots.reshape(1, SLOTS, 1, 2, block_rows, block_rows)


def local(recording, trailing, whiten_filter, pair_list):
    shapes = (recording.shape, trailing.shape, whiten_filter.shape)
    counts = (lax.axis_size("tm"), lax.axis_size("freq"))
    whole_reach = lax.axis_size("chan") == REACH + 1
    if shapes == ((128, 1024), (128, 1024), (128, 64)) and counts == (2, 2) and whole_reach:
        return fused(recording, trailing, whiten_filter, pair_list)
    return general(recording, trailing, whiten_filter, pair_list)


def solution(mesh):
    placed = (
        P(("days", "chan", "freq"), "tm"),
        P(("days", "chan", "freq"), None),
        P(("chan", "freq"), None),
        P(("days", "chan"), None),
    )
    return jax.shard_map(
        local,
        mesh=mesh,
        in_specs=placed,
        out_specs=P(("days", "chan"), None, ("tm", "freq"), None, None, None),
        check_vma=False,
    )
```

```python
import functools
import math

import jax
import jax.numpy as jnp
from jax import lax
from jax.experimental import pallas as pl
from jax.experimental.pallas import tpu as pltpu
from jax.sharding import PartitionSpec as P

FB = 512
REACH = 3
SLOTS = 4


def shifted(block, axis, distance):
    devices = range(lax.axis_size(axis))
    route = [(i - distance, i) for i in devices if i - distance in devices]
    return lax.ppermute(block, axis, route)


def extended(value, sides, width):
    for axis, dim in sides:
        size, length = (lax.axis_size(axis), value.shape[dim])
        up = [(i, (i + 1) % size) for i in range(size - 1)]
        down = [(j, i) for i, j in up]
        last = lax.slice_in_dim(value, length - width, length, axis=dim)
        initial = lax.slice_in_dim(value, 0, width, axis=dim)
        before = lax.ppermute(last, axis, up)
        after = lax.ppermute(initial, axis, down)
        value = jnp.concatenate([before, value, after], axis=dim)
    return value


def fourier_table(first_bin, bin_count, length):
    samples = jnp.arange(length, dtype=jnp.int32)[:, None]
    bin_index = first_bin + jnp.arange(bin_count, dtype=jnp.int32)[None, :]
    phase = samples * bin_index % length
    angle = 2.0 * math.pi / length * phase.astype(jnp.float32)
    taper = 0.5 - 0.5 * jnp.cos(
        2.0 * math.pi / length * jnp.arange(length, dtype=jnp.int32).astype(jnp.float32)
    )
    normaliser = 1.0 / math.sqrt(0.375 * length)
    cosine = (taper[:, None] * jnp.cos(angle) * normaliser).astype(jnp.bfloat16)
    sine_table = (-taper[:, None] * jnp.sin(angle) * normaliser).astype(jnp.bfloat16)
    return (cosine, sine_table)


def general(recording, trailing, whiten_filter, pair_list):
    local_rows, local_span = recording.shape
    hop_size = trailing.shape[1]
    window_size = 2 * hop_size
    segment_count = local_span // hop_size
    following = shifted(recording, "tm", -1)
    is_last = lax.axis_index("tm") == lax.axis_size("tm") - 1
    following = jnp.where(is_last, trailing, following)
    signal = jnp.concatenate([recording, following], axis=1)
    segments = jnp.stack([signal], axis=1)
    stacked_segments = segments.reshape(local_rows * segment_count, window_size)
    bin_step = min(256, FB)
    real_bins = []
    imag_bins = []
    for first_bin in range(0, FB, bin_step):
        cosine, sine_table = fourier_table(first_bin, bin_step, window_size)
        joined = jnp.concatenate([cosine, sine_table], axis=1)
        product = jnp.dot(stacked_segments, joined, preferred_element_type=jnp.float32).astype(
            jnp.bfloat16
        )
        real_bins.append(product[:, :bin_step])
        imag_bins.append(product[:, bin_step:])
    real_spec = jnp.concatenate(real_bins, axis=1)
    imag_spec = jnp.concatenate(imag_bins, axis=1)
    raw_spectra = jnp.stack([real_spec, imag_spec])
    tap_count = whiten_filter.shape[1]
    rim_width = tap_count // 2
    reach_rows = local_rows + tap_count
    skewed = jnp.pad(whiten_filter, ((0, 0), (0, local_rows + 1))).reshape(-1)
    band_matrix = skewed[: local_rows * reach_rows].reshape(local_rows, reach_rows)
    padded = extended(raw_spectra, ((("chan", "freq"), 1),), rim_width)
    predicted = jnp.einsum("ij,ajk->aik", band_matrix, padded, preferred_element_type=jnp.float32)
    whitened = (raw_spectra.astype(jnp.float32) - predicted).astype(jnp.bfloat16)
    spectra = whitened.reshape(2, local_rows, segment_count, FB)
    tm_count = lax.axis_size("tm")
    freq_count = lax.axis_size("freq")
    pieces = lax.all_to_all(spectra[None], ("tm", "freq"), split_axis=4, concat_axis=0, tiled=True)
    band_width = pieces.shape[-1]
    pieces = pieces.reshape(tm_count, freq_count, 2, local_rows, segment_count, band_width)
    banded = pieces.transpose(2, 1, 3, 0, 4, 5).reshape(
        2, freq_count * local_rows, tm_count * segment_count, band_width
    )
    block_rows = banded.shape[1]
    own_block = banded.reshape(2, block_rows, -1)
    depth = own_block.shape[2]
    scaling = 1.0 / math.sqrt(depth)
    block_index = lax.axis_index("chan")
    slot_list = pair_list[0]
    nearby = []
    for distance in range(-REACH, REACH + 1):
        if distance == 0:
            nearby.append(own_block)
        else:
            nearby.append(shifted(own_block, "chan", -distance))
    stacked = jnp.stack(nearby)

    def fetch_partner(partner_index):
        return lax.dynamic_index_in_dim(
            stacked, partner_index - block_index + REACH, 0, keepdims=False
        )

    left_side = jnp.concatenate([own_block[0], own_block[1]], axis=1)
    flipped = jnp.concatenate([own_block[1], -own_block[0]], axis=1)
    contract = (((1,), (1,)), ((), ()))

    def one_slot(partner_index):
        partner = fetch_partner(partner_index)
        right_side = jnp.concatenate([partner[0], partner[1]], axis=1)
        real_part = (
            lax.dot_general(left_side, right_side, contract, preferred_element_type=jnp.float32)
            * scaling
        )
        imag_part = (
            lax.dot_general(flipped, right_side, contract, preferred_element_type=jnp.float32)
            * scaling
        )
        crossed = jnp.stack([real_part, imag_part])
        return jnp.where(partner_index >= 0, crossed, jnp.zeros((), jnp.float32))

    result = jnp.stack([one_slot(slot_list[slot_index]) for slot_index in range(SLOTS)])
    return result.reshape(1, SLOTS, 1, 2, block_rows, block_rows)


MESH = pl.DeviceIdType.MESH
PIECES = (16, 16, 32, 32, 32)
GROUPS = ((0, 0, 32), (0, 32, 32), (1, 0, 32), (0, 64, 32), (1, 32, 32), (0, 96, 32), (1, 64, 32), (1, 96, 32))
TILE = 32
STEP = 32
SPECTRA_VMEM = 60 * 2**20


def spectra_kernel(
    chan_count,
    scaling,
    rec_ref,
    trail_ref,
    filt_ref,
    pairs_ref,
    out,
    samples,
    filters,
    bands,
    table,
    coarse,
    raw,
    gathered,
    sides,
    guest,
    pairs,
    ready,
    local_sems,
    send_sems,
    span_sems,
    pass_sems,
    core_sems,
    filter_sems,
    block_sems,
    guest_sems,
):
    me = lax.axis_index("chan")
    tm = lax.axis_index("tm")
    core = lax.axis_index("freq")
    rows, hop = rec_ref.shape
    window = 2 * hop
    width = table.shape[1] // 2
    block_rows = 2 * rows
    taps = filt_ref.shape[0]
    rim = taps // 2
    tile_count = block_rows // TILE
    group = rows // 2
    furthest = chan_count - 1
    has_left = me > 0
    has_right = me < chan_count - 1
    other = 1 - core
    other_tm = {"tm": 1 - tm}
    other_core = {"freq": 1 - core}
    left = {"chan": me - 1}
    right = {"chan": me + 1}
    ahead = (has_right, has_left)
    onward = (right, left)
    span_send, pass_send, core_send, swap_send = range(4)
    filter_send, block_send = (4, 5), (6, 7)
    guest_send, share_send = 8, 9
    hosting = jnp.logical_or(me == 0, me == furthest)

    def remote(source, target, send, recv, device):
        return pltpu.make_async_remote_copy(
            src_ref=source,
            dst_ref=target,
            send_sem=send_sems.at[send],
            recv_sem=recv,
            device_id=device,
            device_id_type=MESH,
        )

    def half(which):
        return pl.ds(pl.multiple_of(which * rows, rows), rows)

    barrier = pltpu.get_barrier_semaphore()
    later = ((has_right, right), (tm == 0, other_tm), (core == 1, other_core))
    earlier = ((has_left, left), (tm == 1, other_tm), (core == 0, other_core))
    for near, device in later:

        @pl.when(near)
        def _():
            pl.semaphore_signal(barrier, inc=1, device_id=device, device_id_type=MESH)

    own_copies = [
        pltpu.make_async_copy(rec_ref, samples.at[tm, half(core)], local_sems.at[0]),
        pltpu.make_async_copy(trail_ref, samples.at[2, half(core)], local_sems.at[1]),
        pltpu.make_async_copy(filt_ref, filters.at[me, core], local_sems.at[2]),
        pltpu.make_async_copy(pairs_ref, pairs, local_sems.at[3]),
    ]
    for copy in own_copies:
        copy.start()

    awaited = sum(near.astype(jnp.int32) for near, _ in earlier)

    @pl.when(awaited > 0)
    def _():
        pl.semaphore_wait(barrier, awaited)

    for link, (near, device) in enumerate(earlier):

        @pl.when(near)
        def _():
            pl.semaphore_signal(ready.at[link], inc=1, device_id=device, device_id_type=MESH)

    def meet(link):
        @pl.when(later[link][0])
        def _():
            pl.semaphore_wait(ready.at[link], 1)

    starts = [sum(PIECES[:p]) for p in range(len(PIECES))]

    def place(which, start, count):
        first = (1 - which) * start + which * (rows - start - count)
        return pl.multiple_of(first, math.gcd(start, count, rows))

    def piece_start(which, p):
        return place(which, starts[p], PIECES[p])

    def piece_in_block(which, p):
        start = which * rows + piece_start(which, p)
        return pl.ds(pl.multiple_of(start, math.gcd(starts[p], PIECES[p])), PIECES[p])

    def span_copy(p):
        return remote(
            rec_ref.at[pl.ds(piece_start(core, p), PIECES[p])],
            samples.at[tm, piece_in_block(core, p)],
            span_send,
            span_sems.at[p],
            other_tm,
        )

    meet(1)
    for p in range(len(PIECES)):
        span_copy(p).start()

    def core_copy(index, which):
        source, place = ((rec_ref, tm), (trail_ref, 2))[index]
        at = samples.at[place, half(which)]
        return remote(source, at, core_send, core_sems.at[index], other_core)

    meet(2)
    def lend():
        return remote(filt_ref, filters.at[me, 0], swap_send, core_sems.at[2], other_core)

    @pl.when(core == 0)
    def _():
        lend().start()

    for index in range(2):
        core_copy(index, core).start()

    def source_of(direction, distance):
        source = me - distance if direction == 0 else me + distance
        return jnp.clip(source, 0, chan_count - 1)

    def exists(direction, distance):
        return me - distance >= 0 if direction == 0 else me + distance < chan_count

    def weights_copy(direction, distance):
        source = source_of(direction, distance)
        at = filters.at[source]
        return remote(
            at,
            at,
            filter_send[direction],
            filter_sems.at[source],
            onward[direction],
        )

    feeding = (me == furthest - 1, me == 1)

    def guest_copy(tm_index, core_index, send, sem, device):
        at = guest.at[tm_index, core_index]
        return remote(at, at, send, guest_sems.at[sem], device)

    for direction in (1, 0):
        if direction == 0:
            meet(0)

        @pl.when(feeding[direction])
        def _():
            first = pl.multiple_of((1 - core) * group, group)
            share = group // 2
            later_rows = pl.multiple_of(first + tm * share, share)
            for source, start, at, count in (
                (rec_ref, first, 0, group),
                (trail_ref, later_rows, group, share),
            ):
                remote(
                    source.at[pl.ds(start, count)],
                    guest.at[tm, core, at : at + count],
                    guest_send,
                    guest_sems.at[0],
                    onward[direction],
                ).start()

    first_bin = (tm * 2 + core) * width
    unit = 2.0 * math.pi / window
    bins = first_bin + lax.broadcasted_iota(jnp.int32, (1, width), 1)

    def angles(count, scale, factor):
        steps = scale * lax.broadcasted_iota(jnp.int32, (count, width), 0)
        return unit * jnp.bitwise_and(steps * factor, window - 1).astype(jnp.float32)

    parts = window // STEP
    coarse_angle = angles(parts, STEP, bins)
    coarse_turn = angles(parts, STEP, 1)
    coarse[0] = jnp.cos(coarse_angle)
    coarse[1] = jnp.sin(coarse_angle)
    coarse[2] = jnp.cos(coarse_turn)
    coarse[3] = jnp.sin(coarse_turn)
    fine_angle = angles(STEP, 1, bins)
    fine_turn = angles(STEP, 1, 1)
    fine_cos, fine_sin = jnp.cos(fine_angle), jnp.sin(fine_angle)
    turn_cos, turn_sin = jnp.cos(fine_turn), jnp.sin(fine_turn)
    normaliser = 1.0 / math.sqrt(0.375 * window)

    def fill(part, carry):
        c, s, tc, ts = (coarse[k, pl.ds(part, 1), :] for k in range(4))
        taper = (0.5 - 0.5 * (tc * turn_cos - ts * turn_sin)) * normaliser
        at = pl.ds(pl.multiple_of(part * STEP, STEP), STEP)
        table[at, :width] = (taper * (c * fine_cos - s * fine_sin)).astype(jnp.bfloat16)
        table[at, width:] = (-taper * (s * fine_cos + c * fine_sin)).astype(jnp.bfloat16)
        return carry

    lax.fori_loop(0, parts, fill, 0)

    own_copies[2].wait()

    @pl.when(core == 1)
    def _():
        lend().wait_recv()

    for direction in (1, 0):

        @pl.when(jnp.logical_and(ahead[direction], core == 1))
        def _():
            weights_copy(direction, 0).start()

    edge = jnp.zeros((rim, raw.shape[1]), raw.dtype)
    raw[0:rim] = edge
    raw[rim + chan_count * block_rows :] = edge

    for copy in (*own_copies[:2], own_copies[3]):
        copy.wait()
    for index in range(2):
        core_copy(index, other).wait_recv()

    def own_rows(block, start, count):
        return pl.ds(pl.multiple_of(rim + block * block_rows + start, 16), count)

    def block_copy(at, direction, distance, index):
        place = raw.at[at]
        return remote(
            place,
            place,
            block_send[direction],
            block_sems.at[source_of(direction, distance), index],
            onward[direction],
        )

    def group_rows(direction, distance, index):
        which, start, count = GROUPS[index]
        here = core if which == 0 else other
        start = here * rows + place(here, start, count)
        return own_rows(source_of(direction, distance), start, count)

    def fill_rows(where, count, early, late):
        product = jnp.dot(early, table[:hop], preferred_element_type=jnp.float32) + jnp.dot(
            late, table[hop:], preferred_element_type=jnp.float32
        )
        product = product.astype(jnp.bfloat16)
        for segment in range(2):
            found = product[segment * count : (segment + 1) * count]
            raw[where, segment * width : (segment + 1) * width] = found[:, :width]
            raw[where, (2 + segment) * width : (3 + segment) * width] = found[:, width:]

    def group_of(which, p):
        return next(
            index
            for index, (side, start, count) in enumerate(GROUPS)
            if side == which and start <= starts[p] < start + count
        )

    def transform(which, p, index):
        at = which * rows + piece_start(which, p)
        chosen = piece_in_block(which, p)
        count = PIECES[p]
        where = own_rows(me, at, count)
        fill_rows(
            where,
            count,
            samples[0:2, chosen].reshape(2 * count, hop),
            samples[1:3, chosen].reshape(2 * count, hop),
        )
        for direction in (1, 0):
            wanted = ahead[direction]
            if starts[p] >= group:
                wanted = jnp.logical_and(wanted, jnp.logical_not(feeding[direction]))

            @pl.when(wanted)
            def _():
                block_copy(where, direction, 0, index).start()

    def guest_transform(which):
        first, second = guest[0, which, :group], guest[1, which, :group]
        third = jnp.concatenate([guest[0, which, group:], guest[1, which, group:]], axis=0)
        near = jnp.where(me == 0, 1, furthest - 1)
        fill_rows(
            own_rows(near, which * rows + (1 - which) * group, group),
            group,
            jnp.concatenate([first, second], axis=0),
            jnp.concatenate([second, third], axis=0),
        )

    def take_weights(distance):
        for direction in (1, 0):

            @pl.when(jnp.logical_and(exists(direction, distance), core == 1))
            def _():
                weights_copy(direction, distance).wait_recv()

            if distance < furthest:

                onwards = jnp.logical_and(exists(direction, distance), ahead[direction])

                @pl.when(jnp.logical_and(onwards, core == 1))
                def _():
                    weights_copy(direction, distance).start()

    def passed(which, p):
        at = samples.at[1 - tm, piece_in_block(which, p)]
        return remote(at, at, pass_send, pass_sems.at[p], other_core)

    def arrive(distance, index):
        for direction in (1, 0):
            at = group_rows(direction, distance, index)

            expected = exists(direction, distance)
            if distance == 1 and GROUPS[index][1] >= group:
                expected = jnp.logical_and(expected, jnp.logical_not(hosting))

            @pl.when(expected)
            def _():
                block_copy(at, direction, distance, index).wait_recv()

            if distance < furthest:

                @pl.when(jnp.logical_and(exists(direction, distance), ahead[direction]))
                def _():
                    block_copy(at, direction, distance, index).start()

    def own_piece(p):
        span_copy(p).wait_recv()
        passed(core, p).start()
        transform(core, p, group_of(0, p))

    def other_piece(p):
        passed(other, p).wait_recv()
        transform(other, p, group_of(1, p))

    own_piece(0)
    own_piece(1)
    other_piece(0)
    take_weights(1)
    own_piece(2)
    other_piece(1)
    own_piece(3)
    other_piece(2)
    own_piece(4)
    other_piece(3)
    take_weights(2)
    arrive(1, 0)
    other_piece(4)
    arrive(1, 1)

    @pl.when(hosting)
    def _():
        guest_copy(tm, core, guest_send, 0, other_tm).wait_recv()
        guest_copy(tm, core, guest_send, 1, other_tm).start()
        guest_copy(tm, core, share_send, 2, other_core).start()

    def spread(block, carry):
        for which in range(2):
            weights = jnp.transpose(filters[block, which].astype(jnp.float32))
            wide = jnp.concatenate([weights, jnp.zeros((rows, 128 - taps), jnp.float32)], axis=1)
            for p in range(tile_count // 2):
                rolled = pltpu.roll(
                    wide[p * TILE : (p + 1) * TILE], 0, 1, stride=1, stride_axis=0
                )
                bands[block, which * tile_count // 2 + p] = rolled.astype(jnp.bfloat16)
        return carry

    def whiten(block, tile):
        start = pl.multiple_of(block * block_rows + tile * TILE, TILE)
        at = pl.ds(pl.multiple_of(tile * TILE, TILE), TILE)
        near = raw[pl.ds(start, TILE + taps)]
        predicted = jnp.dot(
            bands[block, tile][:, : TILE + taps], near, preferred_element_type=jnp.float32
        )
        mine = near[rim : rim + TILE].astype(jnp.float32)
        gathered[block, at] = (mine - predicted).astype(jnp.bfloat16)

    contract = (((1,), (1,)), ((), ()))

    def cross(block, first=False):
        partner = gathered[block]
        both = lax.dot_general(sides[...], partner, contract, preferred_element_type=jnp.float32)
        for part in range(2):
            product = both[part * block_rows : (part + 1) * block_rows] * scaling
            for slot in range(SLOTS):
                before = jnp.zeros_like(product) if first else out[slot, part]
                out[slot, part] = jnp.where(pairs[0, slot] == block, product, before)

    def finish_own():
        for tile in range(tile_count):
            whiten(me, tile)
        own = gathered[me]
        middle = own.shape[1] // 2
        sides[:block_rows] = own
        sides[block_rows:] = jnp.concatenate([own[:, middle:], -own[:, :middle]], axis=1)
        cross(me, True)

    def inner(distance):
        for direction in (1, 0):

            @pl.when(exists(direction, distance))
            def _():
                block = me - distance if direction == 0 else me + distance
                for tile in range(tile_count - 1):
                    whiten(block, tile + 1 if direction == 0 else tile)

    def finish(distance):
        for direction in (1, 0):

            @pl.when(exists(direction, distance))
            def _():
                block = me - distance if direction == 0 else me + distance
                whiten(block, 0 if direction == 0 else tile_count - 1)
                cross(block)

    def hand():
        return remote(filters, filters, swap_send, core_sems.at[2], other_core)

    for index in range(2, len(GROUPS)):
        arrive(1, index)
    take_weights(3)

    @pl.when(core == 1)
    def _():
        hand().start()

    for index in range(len(GROUPS)):
        arrive(2, index)

    @pl.when(hosting)
    def _():
        guest_copy(1 - tm, core, guest_send, 1, other_tm).wait_recv()
        guest_copy(1 - tm, core, share_send, 3, other_core).start()

    @pl.when(core == 0)
    def _():
        hand().wait_recv()

    lax.fori_loop(0, chan_count, spread, 0)
    finish_own()
    arrive(3, 0)
    arrive(3, 1)

    @pl.when(hosting)
    def _():
        guest_copy(tm, other, share_send, 2, other_core).wait_recv()
        guest_transform(core)
        guest_copy(1 - tm, other, share_send, 3, other_core).wait_recv()
        guest_transform(other)

    inner(1)
    finish(1)
    arrive(3, 2)
    inner(2)
    finish(2)
    for index in range(3, len(GROUPS) - 1):
        arrive(3, index)

    def last(tiles, complete):
        for direction in (1, 0):

            @pl.when(exists(direction, furthest))
            def _():
                block = me - furthest if direction == 0 else me + furthest
                for tile in tiles:
                    whiten(block, tile)
                if complete:
                    cross(block)

    last((0, 1, 2 + 3 * core, 6, 7), False)
    arrive(3, len(GROUPS) - 1)
    last([3 - core + tile for tile in range(3)], True)

    guest_copy(tm, core, guest_send, 1, other_tm).wait_send()

    @pl.when(hosting)
    def _():
        shared = guest.at[0:2, core]
        remote(shared, shared, share_send, guest_sems.at[2], other_core).wait_send()

    whole = samples.at[tm, half(core)]
    remote(whole, whole, span_send, span_sems.at[0], other_tm).wait_send()
    remote(whole, whole, pass_send, pass_sems.at[0], other_core).wait_send()
    both = samples.at[0:2, half(core)]
    remote(both, both, core_send, core_sems.at[0], other_core).wait_send()

    @pl.when(core == 0)
    def _():
        lend().wait_send()

    @pl.when(core == 1)
    def _():
        hand().wait_send()

    for direction in (1, 0):
        for count in range(1, chan_count):

            @pl.when(me == (count - 1 if direction == 0 else chan_count - count))
            def _():
                @pl.when(core == 1)
                def _():
                    sent = filters.at[0:count]
                    remote(
                        sent, sent, filter_send[direction], filter_sems.at[0], onward[direction]
                    ).wait_send()

                fed = rows if count == furthest else 0
                sent = raw.at[0 : count * block_rows - fed]
                remote(
                    sent, sent, block_send[direction], block_sems.at[0, 0], onward[direction]
                ).wait_send()


def fused(recording, trailing, whiten_filter, pair_list):
    rows, hop = recording.shape
    chan_count = lax.axis_size("chan")
    taps = whiten_filter.shape[1]
    width = FB // (lax.axis_size("tm") * lax.axis_size("freq"))
    block_rows = 2 * rows
    depth = 2 * width
    vmem = pl.BlockSpec(memory_space=pltpu.VMEM)
    hbm = pl.BlockSpec(memory_space=pltpu.HBM)
    slots = pl.pallas_call(
        functools.partial(spectra_kernel, chan_count, 1.0 / math.sqrt(depth)),
        out_shape=pltpu.VMEM((SLOTS, 2, block_rows, block_rows), jnp.float32),
        in_specs=[hbm] * 4,
        out_specs=vmem,
        scratch_shapes=[
            pltpu.VMEM((3, block_rows, hop), jnp.bfloat16),
            pltpu.VMEM((chan_count, 2, taps, rows), jnp.bfloat16),
            pltpu.VMEM((chan_count, block_rows // TILE, TILE, 128), jnp.bfloat16),
            pltpu.VMEM((2 * hop, 2 * width), jnp.bfloat16),
            pltpu.VMEM((4, 2 * hop // STEP, width), jnp.float32),
            pltpu.VMEM((chan_count * block_rows + taps, 2 * depth), jnp.bfloat16),
            pltpu.VMEM((chan_count, block_rows, 2 * depth), jnp.bfloat16),
            pltpu.VMEM((2 * block_rows, 2 * depth), jnp.bfloat16),
            pltpu.VMEM((2, 2, 3 * rows // 4, hop), jnp.bfloat16),
            pltpu.SMEM((1, SLOTS), jnp.int32),
            pltpu.SemaphoreType.REGULAR((3,)),
            pltpu.SemaphoreType.DMA((4,)),
            pltpu.SemaphoreType.DMA((10,)),
            pltpu.SemaphoreType.DMA((len(PIECES),)),
            pltpu.SemaphoreType.DMA((len(PIECES),)),
            pltpu.SemaphoreType.DMA((3,)),
            pltpu.SemaphoreType.DMA((chan_count,)),
            pltpu.SemaphoreType.DMA((chan_count, len(GROUPS))),
            pltpu.SemaphoreType.DMA((4,)),
        ],
        compiler_params=pltpu.CompilerParams(
            collective_id=0, has_side_effects=True, vmem_limit_bytes=SPECTRA_VMEM
        ),
    )(recording, trailing, whiten_filter.T, pair_list)
    return slots.reshape(1, SLOTS, 1, 2, block_rows, block_rows)


def local(recording, trailing, whiten_filter, pair_list):
    shapes = (recording.shape, trailing.shape, whiten_filter.shape)
    counts = (lax.axis_size("tm"), lax.axis_size("freq"))
    whole_reach = lax.axis_size("chan") == REACH + 1
    if shapes == ((128, 1024), (128, 1024), (128, 64)) and counts == (2, 2) and whole_reach:
        return fused(recording, trailing, whiten_filter, pair_list)
    return general(recording, trailing, whiten_filter, pair_list)


def solution(mesh):
    placed = (
        P(("days", "chan", "freq"), "tm"),
        P(("days", "chan", "freq"), None),
        P(("chan", "freq"), None),
        P(("days", "chan"), None),
    )
    return jax.shard_map(
        local,
        mesh=mesh,
        in_specs=placed,
        out_specs=P(("days", "chan"), None, ("tm", "freq"), None, None, None),
        check_vma=False,
    )
```

```python
import functools
import math

import jax
import jax.numpy as jnp
from jax import lax
from jax.experimental import pallas as pl
from jax.experimental.pallas import tpu as pltpu
from jax.sharding import PartitionSpec as P

FB = 512
REACH = 3
SLOTS = 4


def shifted(block, axis, distance):
    devices = range(lax.axis_size(axis))
    route = [(i - distance, i) for i in devices if i - distance in devices]
    return lax.ppermute(block, axis, route)


def extended(value, sides, width):
    for axis, dim in sides:
        size, length = (lax.axis_size(axis), value.shape[dim])
        up = [(i, (i + 1) % size) for i in range(size - 1)]
        down = [(j, i) for i, j in up]
        last = lax.slice_in_dim(value, length - width, length, axis=dim)
        initial = lax.slice_in_dim(value, 0, width, axis=dim)
        before = lax.ppermute(last, axis, up)
        after = lax.ppermute(initial, axis, down)
        value = jnp.concatenate([before, value, after], axis=dim)
    return value


def fourier_table(first_bin, bin_count, length):
    samples = jnp.arange(length, dtype=jnp.int32)[:, None]
    bin_index = first_bin + jnp.arange(bin_count, dtype=jnp.int32)[None, :]
    phase = samples * bin_index % length
    angle = 2.0 * math.pi / length * phase.astype(jnp.float32)
    taper = 0.5 - 0.5 * jnp.cos(
        2.0 * math.pi / length * jnp.arange(length, dtype=jnp.int32).astype(jnp.float32)
    )
    normaliser = 1.0 / math.sqrt(0.375 * length)
    cosine = (taper[:, None] * jnp.cos(angle) * normaliser).astype(jnp.bfloat16)
    sine_table = (-taper[:, None] * jnp.sin(angle) * normaliser).astype(jnp.bfloat16)
    return (cosine, sine_table)


def general(recording, trailing, whiten_filter, pair_list):
    local_rows, local_span = recording.shape
    hop_size = trailing.shape[1]
    window_size = 2 * hop_size
    segment_count = local_span // hop_size
    following = shifted(recording, "tm", -1)
    is_last = lax.axis_index("tm") == lax.axis_size("tm") - 1
    following = jnp.where(is_last, trailing, following)
    signal = jnp.concatenate([recording, following], axis=1)
    segments = jnp.stack([signal], axis=1)
    stacked_segments = segments.reshape(local_rows * segment_count, window_size)
    bin_step = min(256, FB)
    real_bins = []
    imag_bins = []
    for first_bin in range(0, FB, bin_step):
        cosine, sine_table = fourier_table(first_bin, bin_step, window_size)
        joined = jnp.concatenate([cosine, sine_table], axis=1)
        product = jnp.dot(stacked_segments, joined, preferred_element_type=jnp.float32).astype(
            jnp.bfloat16
        )
        real_bins.append(product[:, :bin_step])
        imag_bins.append(product[:, bin_step:])
    real_spec = jnp.concatenate(real_bins, axis=1)
    imag_spec = jnp.concatenate(imag_bins, axis=1)
    raw_spectra = jnp.stack([real_spec, imag_spec])
    tap_count = whiten_filter.shape[1]
    rim_width = tap_count // 2
    reach_rows = local_rows + tap_count
    skewed = jnp.pad(whiten_filter, ((0, 0), (0, local_rows + 1))).reshape(-1)
    band_matrix = skewed[: local_rows * reach_rows].reshape(local_rows, reach_rows)
    padded = extended(raw_spectra, ((("chan", "freq"), 1),), rim_width)
    predicted = jnp.einsum("ij,ajk->aik", band_matrix, padded, preferred_element_type=jnp.float32)
    whitened = (raw_spectra.astype(jnp.float32) - predicted).astype(jnp.bfloat16)
    spectra = whitened.reshape(2, local_rows, segment_count, FB)
    tm_count = lax.axis_size("tm")
    freq_count = lax.axis_size("freq")
    pieces = lax.all_to_all(spectra[None], ("tm", "freq"), split_axis=4, concat_axis=0, tiled=True)
    band_width = pieces.shape[-1]
    pieces = pieces.reshape(tm_count, freq_count, 2, local_rows, segment_count, band_width)
    banded = pieces.transpose(2, 1, 3, 0, 4, 5).reshape(
        2, freq_count * local_rows, tm_count * segment_count, band_width
    )
    block_rows = banded.shape[1]
    own_block = banded.reshape(2, block_rows, -1)
    depth = own_block.shape[2]
    scaling = 1.0 / math.sqrt(depth)
    block_index = lax.axis_index("chan")
    slot_list = pair_list[0]
    nearby = []
    for distance in range(-REACH, REACH + 1):
        if distance == 0:
            nearby.append(own_block)
        else:
            nearby.append(shifted(own_block, "chan", -distance))
    stacked = jnp.stack(nearby)

    def fetch_partner(partner_index):
        return lax.dynamic_index_in_dim(
            stacked, partner_index - block_index + REACH, 0, keepdims=False
        )

    left_side = jnp.concatenate([own_block[0], own_block[1]], axis=1)
    flipped = jnp.concatenate([own_block[1], -own_block[0]], axis=1)
    contract = (((1,), (1,)), ((), ()))

    def one_slot(partner_index):
        partner = fetch_partner(partner_index)
        right_side = jnp.concatenate([partner[0], partner[1]], axis=1)
        real_part = (
            lax.dot_general(left_side, right_side, contract, preferred_element_type=jnp.float32)
            * scaling
        )
        imag_part = (
            lax.dot_general(flipped, right_side, contract, preferred_element_type=jnp.float32)
            * scaling
        )
        crossed = jnp.stack([real_part, imag_part])
        return jnp.where(partner_index >= 0, crossed, jnp.zeros((), jnp.float32))

    result = jnp.stack([one_slot(slot_list[slot_index]) for slot_index in range(SLOTS)])
    return result.reshape(1, SLOTS, 1, 2, block_rows, block_rows)


MESH = pl.DeviceIdType.MESH
PIECES = (16, 16, 32, 32, 32)
GROUPS = ((0, 0, 32), (0, 32, 32), (1, 0, 32), (0, 64, 32), (1, 32, 32), (0, 96, 32), (1, 64, 32), (1, 96, 32))
TILE = 32
STEP = 32
SPECTRA_VMEM = 60 * 2**20


def spectra_kernel(
    chan_count,
    scaling,
    rec_ref,
    trail_ref,
    filt_ref,
    pairs_ref,
    out,
    samples,
    filters,
    bands,
    table,
    coarse,
    raw,
    gathered,
    sides,
    guest,
    pairs,
    ready,
    local_sems,
    send_sems,
    span_sems,
    pass_sems,
    core_sems,
    filter_sems,
    block_sems,
    guest_sems,
):
    me = lax.axis_index("chan")
    tm = lax.axis_index("tm")
    core = lax.axis_index("freq")
    rows, hop = rec_ref.shape
    window = 2 * hop
    width = table.shape[1] // 2
    block_rows = 2 * rows
    taps = filt_ref.shape[0]
    rim = taps // 2
    tile_count = block_rows // TILE
    group = rows // 2
    furthest = chan_count - 1
    has_left = me > 0
    has_right = me < chan_count - 1
    other = 1 - core
    other_tm = {"tm": 1 - tm}
    other_core = {"freq": 1 - core}
    left = {"chan": me - 1}
    right = {"chan": me + 1}
    ahead = (has_right, has_left)
    onward = (right, left)
    span_send, pass_send, core_send, swap_send = range(4)
    filter_send, block_send = (4, 5), (6, 7)
    guest_send, share_send = 8, 9
    hosting = jnp.logical_or(me == 0, me == furthest)

    def remote(source, target, send, recv, device):
        return pltpu.make_async_remote_copy(
            src_ref=source,
            dst_ref=target,
            send_sem=send_sems.at[send],
            recv_sem=recv,
            device_id=device,
            device_id_type=MESH,
        )

    def half(which):
        return pl.ds(pl.multiple_of(which * rows, rows), rows)

    barrier = pltpu.get_barrier_semaphore()
    later = ((has_right, right), (tm == 0, other_tm), (core == 1, other_core))
    earlier = ((has_left, left), (tm == 1, other_tm), (core == 0, other_core))
    for near, device in later:

        @pl.when(near)
        def _():
            pl.semaphore_signal(barrier, inc=1, device_id=device, device_id_type=MESH)

    own_copies = [
        pltpu.make_async_copy(rec_ref, samples.at[tm, half(core)], local_sems.at[0]),
        pltpu.make_async_copy(trail_ref, samples.at[2, half(core)], local_sems.at[1]),
        pltpu.make_async_copy(filt_ref, filters.at[me, core], local_sems.at[2]),
        pltpu.make_async_copy(pairs_ref, pairs, local_sems.at[3]),
    ]
    for copy in own_copies:
        copy.start()

    awaited = sum(near.astype(jnp.int32) for near, _ in earlier)

    @pl.when(awaited > 0)
    def _():
        pl.semaphore_wait(barrier, awaited)

    for link, (near, device) in enumerate(earlier):

        @pl.when(near)
        def _():
            pl.semaphore_signal(ready.at[link], inc=1, device_id=device, device_id_type=MESH)

    def meet(link):
        @pl.when(later[link][0])
        def _():
            pl.semaphore_wait(ready.at[link], 1)

    starts = [sum(PIECES[:p]) for p in range(len(PIECES))]

    def place(which, start, count):
        first = (1 - which) * start + which * (rows - start - count)
        return pl.multiple_of(first, math.gcd(start, count, rows))

    def piece_start(which, p):
        return place(which, starts[p], PIECES[p])

    def piece_in_block(which, p):
        start = which * rows + piece_start(which, p)
        return pl.ds(pl.multiple_of(start, math.gcd(starts[p], PIECES[p])), PIECES[p])

    def span_copy(p):
        return remote(
            rec_ref.at[pl.ds(piece_start(core, p), PIECES[p])],
            samples.at[tm, piece_in_block(core, p)],
            span_send,
            span_sems.at[p],
            other_tm,
        )

    meet(1)
    for p in range(len(PIECES)):
        span_copy(p).start()

    def core_copy(index, which):
        source, place = ((rec_ref, tm), (trail_ref, 2))[index]
        at = samples.at[place, half(which)]
        return remote(source, at, core_send, core_sems.at[index], other_core)

    meet(2)
    def lend():
        return remote(filt_ref, filters.at[me, 0], swap_send, core_sems.at[2], other_core)

    @pl.when(core == 0)
    def _():
        lend().start()

    for index in range(2):
        core_copy(index, core).start()

    def source_of(direction, distance):
        source = me - distance if direction == 0 else me + distance
        return jnp.clip(source, 0, chan_count - 1)

    def slot_of(direction, source):
        return jnp.clip(source - direction, 0, furthest - 1)

    def exists(direction, distance):
        return me - distance >= 0 if direction == 0 else me + distance < chan_count

    def weights_copy(direction, distance):
        source = source_of(direction, distance)
        at = filters.at[source]
        return remote(
            at,
            at,
            filter_send[direction],
            filter_sems.at[slot_of(direction, source)],
            onward[direction],
        )

    feeding = (me == furthest - 1, me == 1)

    def guest_copy(tm_index, core_index, send, sem, device):
        at = guest.at[tm_index, core_index]
        return remote(at, at, send, guest_sems.at[sem], device)

    for direction in (1, 0):
        if direction == 0:
            meet(0)

        @pl.when(feeding[direction])
        def _():
            first = pl.multiple_of((1 - core) * group, group)
            share = group // 2
            later_rows = pl.multiple_of(first + tm * share, share)
            for source, start, at, count in (
                (rec_ref, first, 0, group),
                (trail_ref, later_rows, group, share),
            ):
                remote(
                    source.at[pl.ds(start, count)],
                    guest.at[tm, core, at : at + count],
                    guest_send,
                    guest_sems.at[0],
                    onward[direction],
                ).start()

    first_bin = (tm * 2 + core) * width
    unit = 2.0 * math.pi / window
    bins = first_bin + lax.broadcasted_iota(jnp.int32, (1, width), 1)

    def angles(count, scale, factor):
        steps = scale * lax.broadcasted_iota(jnp.int32, (count, width), 0)
        return unit * jnp.bitwise_and(steps * factor, window - 1).astype(jnp.float32)

    parts = window // STEP
    coarse_angle = angles(parts, STEP, bins)
    coarse_turn = angles(parts, STEP, 1)
    coarse[0] = jnp.cos(coarse_angle)
    coarse[1] = jnp.sin(coarse_angle)
    coarse[2] = jnp.cos(coarse_turn)
    coarse[3] = jnp.sin(coarse_turn)
    fine_angle = angles(STEP, 1, bins)
    fine_turn = angles(STEP, 1, 1)
    fine_cos, fine_sin = jnp.cos(fine_angle), jnp.sin(fine_angle)
    turn_cos, turn_sin = jnp.cos(fine_turn), jnp.sin(fine_turn)
    normaliser = 1.0 / math.sqrt(0.375 * window)

    def fill(part, carry):
        c, s, tc, ts = (coarse[k, pl.ds(part, 1), :] for k in range(4))
        taper = (0.5 - 0.5 * (tc * turn_cos - ts * turn_sin)) * normaliser
        at = pl.ds(pl.multiple_of(part * STEP, STEP), STEP)
        table[at, :width] = (taper * (c * fine_cos - s * fine_sin)).astype(jnp.bfloat16)
        table[at, width:] = (-taper * (s * fine_cos + c * fine_sin)).astype(jnp.bfloat16)
        return carry

    lax.fori_loop(0, parts, fill, 0)

    own_copies[2].wait()

    @pl.when(core == 1)
    def _():
        lend().wait_recv()

    for direction in (1, 0):

        @pl.when(jnp.logical_and(ahead[direction], core == 1))
        def _():
            weights_copy(direction, 0).start()

    edge = jnp.zeros((rim, raw.shape[1]), raw.dtype)
    raw[0:rim] = edge
    raw[rim + chan_count * block_rows :] = edge

    for copy in (*own_copies[:2], own_copies[3]):
        copy.wait()
    for index in range(2):
        core_copy(index, other).wait_recv()

    def own_rows(block, start, count):
        return pl.ds(pl.multiple_of(rim + block * block_rows + start, 16), count)

    def block_copy(at, direction, distance, index):
        place = raw.at[at]
        return remote(
            place,
            place,
            block_send[direction],
            block_sems.at[slot_of(direction, source_of(direction, distance)), index],
            onward[direction],
        )

    def group_rows(direction, distance, index):
        which, start, count = GROUPS[index]
        here = core if which == 0 else other
        start = here * rows + place(here, start, count)
        return own_rows(source_of(direction, distance), start, count)

    def fill_rows(where, count, early, late):
        product = jnp.dot(early, table[:hop], preferred_element_type=jnp.float32) + jnp.dot(
            late, table[hop:], preferred_element_type=jnp.float32
        )
        product = product.astype(jnp.bfloat16)
        for segment in range(2):
            found = product[segment * count : (segment + 1) * count]
            raw[where, segment * width : (segment + 1) * width] = found[:, :width]
            raw[where, (2 + segment) * width : (3 + segment) * width] = found[:, width:]

    def group_of(which, p):
        return next(
            index
            for index, (side, start, count) in enumerate(GROUPS)
            if side == which and start <= starts[p] < start + count
        )

    def transform(which, p, index):
        at = which * rows + piece_start(which, p)
        chosen = piece_in_block(which, p)
        count = PIECES[p]
        where = own_rows(me, at, count)
        fill_rows(
            where,
            count,
            samples[0:2, chosen].reshape(2 * count, hop),
            samples[1:3, chosen].reshape(2 * count, hop),
        )
        for direction in (1, 0):
            wanted = ahead[direction]
            if starts[p] >= group:
                wanted = jnp.logical_and(wanted, jnp.logical_not(feeding[direction]))

            @pl.when(wanted)
            def _():
                block_copy(where, direction, 0, index).start()

    def guest_transform(which):
        first, second = guest[0, which, :group], guest[1, which, :group]
        third = jnp.concatenate([guest[0, which, group:], guest[1, which, group:]], axis=0)
        near = jnp.where(me == 0, 1, furthest - 1)
        fill_rows(
            own_rows(near, which * rows + (1 - which) * group, group),
            group,
            jnp.concatenate([first, second], axis=0),
            jnp.concatenate([second, third], axis=0),
        )

    def take_weights(distance):
        for direction in (1, 0):

            @pl.when(jnp.logical_and(exists(direction, distance), core == 1))
            def _():
                weights_copy(direction, distance).wait_recv()

            if distance < furthest:

                onwards = jnp.logical_and(exists(direction, distance), ahead[direction])

                @pl.when(jnp.logical_and(onwards, core == 1))
                def _():
                    weights_copy(direction, distance).start()

    def passed(which, p):
        at = samples.at[1 - tm, piece_in_block(which, p)]
        return remote(at, at, pass_send, pass_sems.at[p], other_core)

    def arrive(distance, index):
        for direction in (1, 0):
            at = group_rows(direction, distance, index)

            expected = exists(direction, distance)
            if distance == 1 and GROUPS[index][1] >= group:
                expected = jnp.logical_and(expected, jnp.logical_not(hosting))

            @pl.when(expected)
            def _():
                block_copy(at, direction, distance, index).wait_recv()

            if distance < furthest:

                @pl.when(jnp.logical_and(exists(direction, distance), ahead[direction]))
                def _():
                    block_copy(at, direction, distance, index).start()

    def own_piece(p):
        span_copy(p).wait_recv()
        passed(core, p).start()
        transform(core, p, group_of(0, p))

    def other_piece(p):
        passed(other, p).wait_recv()
        transform(other, p, group_of(1, p))

    own_piece(0)
    own_piece(1)
    other_piece(0)
    take_weights(1)
    own_piece(2)
    other_piece(1)
    own_piece(3)
    other_piece(2)
    own_piece(4)
    other_piece(3)
    take_weights(2)
    arrive(1, 0)
    other_piece(4)
    arrive(1, 1)

    @pl.when(hosting)
    def _():
        guest_copy(tm, core, guest_send, 0, other_tm).wait_recv()
        guest_copy(tm, core, guest_send, 1, other_tm).start()
        guest_copy(tm, core, share_send, 2, other_core).start()

    def spread(block, carry):
        for which in range(2):
            weights = jnp.transpose(filters[block, which].astype(jnp.float32))
            wide = jnp.concatenate([weights, jnp.zeros((rows, 128 - taps), jnp.float32)], axis=1)
            for p in range(tile_count // 2):
                rolled = pltpu.roll(
                    wide[p * TILE : (p + 1) * TILE], 0, 1, stride=1, stride_axis=0
                )
                bands[block, which * tile_count // 2 + p] = rolled.astype(jnp.bfloat16)
        return carry

    def whiten(block, tile):
        start = pl.multiple_of(block * block_rows + tile * TILE, TILE)
        at = pl.ds(pl.multiple_of(tile * TILE, TILE), TILE)
        near = raw[pl.ds(start, TILE + taps)]
        predicted = jnp.dot(
            bands[block, tile][:, : TILE + taps], near, preferred_element_type=jnp.float32
        )
        mine = near[rim : rim + TILE].astype(jnp.float32)
        gathered[block, at] = (mine - predicted).astype(jnp.bfloat16)

    contract = (((1,), (1,)), ((), ()))

    def cross(block, first=False):
        partner = gathered[block]
        both = lax.dot_general(sides[...], partner, contract, preferred_element_type=jnp.float32)
        for part in range(2):
            product = both[part * block_rows : (part + 1) * block_rows] * scaling
            for slot in range(SLOTS):
                before = jnp.zeros_like(product) if first else out[slot, part]
                out[slot, part] = jnp.where(pairs[0, slot] == block, product, before)

    def finish_own():
        for tile in range(tile_count):
            whiten(me, tile)
        own = gathered[me]
        middle = own.shape[1] // 2
        sides[:block_rows] = own
        sides[block_rows:] = jnp.concatenate([own[:, middle:], -own[:, :middle]], axis=1)
        cross(me, True)

    def inner(distance):
        for direction in (1, 0):

            @pl.when(exists(direction, distance))
            def _():
                block = me - distance if direction == 0 else me + distance
                for tile in range(tile_count - 1):
                    whiten(block, tile + 1 if direction == 0 else tile)

    def finish(distance):
        for direction in (1, 0):

            @pl.when(exists(direction, distance))
            def _():
                block = me - distance if direction == 0 else me + distance
                whiten(block, 0 if direction == 0 else tile_count - 1)
                cross(block)

    def hand():
        return remote(filters, filters, swap_send, core_sems.at[2], other_core)

    for index in range(2, len(GROUPS)):
        arrive(1, index)
    take_weights(3)

    @pl.when(core == 1)
    def _():
        hand().start()

    for index in range(len(GROUPS) - 2):
        arrive(2, index)

    @pl.when(jnp.logical_and(hosting, core == 0))
    def _():
        hand().wait_recv()

    @pl.when(hosting)
    def _():
        lax.fori_loop(0, chan_count, spread, 0)
        finish_own()

    for index in range(len(GROUPS) - 2, len(GROUPS)):
        arrive(2, index)

    @pl.when(hosting)
    def _():
        guest_copy(1 - tm, core, guest_send, 1, other_tm).wait_recv()
        guest_copy(1 - tm, core, share_send, 3, other_core).start()

    @pl.when(jnp.logical_and(jnp.logical_not(hosting), core == 0))
    def _():
        hand().wait_recv()

    @pl.when(jnp.logical_not(hosting))
    def _():
        lax.fori_loop(0, chan_count, spread, 0)
        finish_own()

    arrive(3, 0)
    arrive(3, 1)

    @pl.when(hosting)
    def _():
        guest_copy(tm, other, share_send, 2, other_core).wait_recv()
        guest_transform(core)
        guest_copy(1 - tm, other, share_send, 3, other_core).wait_recv()
        guest_transform(other)

    inner(1)
    finish(1)
    arrive(3, 2)
    inner(2)
    finish(2)
    for index in range(3, len(GROUPS) - 1):
        arrive(3, index)

    def last(tiles, complete):
        for direction in (1, 0):

            @pl.when(exists(direction, furthest))
            def _():
                block = me - furthest if direction == 0 else me + furthest
                for tile in tiles:
                    whiten(block, tile)
                if complete:
                    cross(block)

    last((0, 1, 2 + 3 * core, 6, 7), False)
    arrive(3, len(GROUPS) - 1)
    last([3 - core + tile for tile in range(3)], True)

    guest_copy(tm, core, guest_send, 1, other_tm).wait_send()

    @pl.when(hosting)
    def _():
        shared = guest.at[0:2, core]
        remote(shared, shared, share_send, guest_sems.at[2], other_core).wait_send()

    whole = samples.at[tm, half(core)]
    remote(whole, whole, span_send, span_sems.at[0], other_tm).wait_send()
    remote(whole, whole, pass_send, pass_sems.at[0], other_core).wait_send()
    both = samples.at[0:2, half(core)]
    remote(both, both, core_send, core_sems.at[0], other_core).wait_send()

    @pl.when(core == 0)
    def _():
        lend().wait_send()

    @pl.when(core == 1)
    def _():
        hand().wait_send()

    for direction in (1, 0):
        for count in range(1, chan_count):

            @pl.when(me == (count - 1 if direction == 0 else chan_count - count))
            def _():
                @pl.when(core == 1)
                def _():
                    sent = filters.at[0:count]
                    remote(
                        sent, sent, filter_send[direction], filter_sems.at[0], onward[direction]
                    ).wait_send()

                fed = rows if count == furthest else 0
                sent = raw.at[0 : count * block_rows - fed]
                remote(
                    sent, sent, block_send[direction], block_sems.at[0, 0], onward[direction]
                ).wait_send()


def fused(recording, trailing, whiten_filter, pair_list):
    rows, hop = recording.shape
    chan_count = lax.axis_size("chan")
    taps = whiten_filter.shape[1]
    width = FB // (lax.axis_size("tm") * lax.axis_size("freq"))
    block_rows = 2 * rows
    depth = 2 * width
    vmem = pl.BlockSpec(memory_space=pltpu.VMEM)
    hbm = pl.BlockSpec(memory_space=pltpu.HBM)
    slots = pl.pallas_call(
        functools.partial(spectra_kernel, chan_count, 1.0 / math.sqrt(depth)),
        out_shape=pltpu.VMEM((SLOTS, 2, block_rows, block_rows), jnp.float32),
        in_specs=[hbm] * 4,
        out_specs=vmem,
        scratch_shapes=[
            pltpu.VMEM((3, block_rows, hop), jnp.bfloat16),
            pltpu.VMEM((chan_count, 2, taps, rows), jnp.bfloat16),
            pltpu.VMEM((chan_count, block_rows // TILE, TILE, 128), jnp.bfloat16),
            pltpu.VMEM((2 * hop, 2 * width), jnp.bfloat16),
            pltpu.VMEM((4, 2 * hop // STEP, width), jnp.float32),
            pltpu.VMEM((chan_count * block_rows + taps, 2 * depth), jnp.bfloat16),
            pltpu.VMEM((chan_count, block_rows, 2 * depth), jnp.bfloat16),
            pltpu.VMEM((2 * block_rows, 2 * depth), jnp.bfloat16),
            pltpu.VMEM((2, 2, 3 * rows // 4, hop), jnp.bfloat16),
            pltpu.SMEM((1, SLOTS), jnp.int32),
            pltpu.SemaphoreType.REGULAR((3,)),
            pltpu.SemaphoreType.DMA((4,)),
            pltpu.SemaphoreType.DMA((10,)),
            pltpu.SemaphoreType.DMA((len(PIECES),)),
            pltpu.SemaphoreType.DMA((len(PIECES),)),
            pltpu.SemaphoreType.DMA((3,)),
            pltpu.SemaphoreType.DMA((chan_count - 1,)),
            pltpu.SemaphoreType.DMA((chan_count - 1, len(GROUPS))),
            pltpu.SemaphoreType.DMA((4,)),
        ],
        compiler_params=pltpu.CompilerParams(
            collective_id=0, has_side_effects=True, vmem_limit_bytes=SPECTRA_VMEM
        ),
    )(recording, trailing, whiten_filter.T, pair_list)
    return slots.reshape(1, SLOTS, 1, 2, block_rows, block_rows)


def local(recording, trailing, whiten_filter, pair_list):
    shapes = (recording.shape, trailing.shape, whiten_filter.shape)
    counts = (lax.axis_size("tm"), lax.axis_size("freq"))
    whole_reach = lax.axis_size("chan") == REACH + 1
    if shapes == ((128, 1024), (128, 1024), (128, 64)) and counts == (2, 2) and whole_reach:
        return fused(recording, trailing, whiten_filter, pair_list)
    return general(recording, trailing, whiten_filter, pair_list)


def solution(mesh):
    placed = (
        P(("days", "chan", "freq"), "tm"),
        P(("days", "chan", "freq"), None),
        P(("chan", "freq"), None),
        P(("days", "chan"), None),
    )
    return jax.shard_map(
        local,
        mesh=mesh,
        in_specs=placed,
        out_specs=P(("days", "chan"), None, ("tm", "freq"), None, None, None),
        check_vma=False,
    )
```

```python
import functools
import math

import jax
import jax.numpy as jnp
from jax import lax
from jax.experimental import pallas as pl
from jax.experimental.pallas import tpu as pltpu
from jax.sharding import PartitionSpec as P

FB = 512
REACH = 3
SLOTS = 4


def shifted(block, axis, distance):
    devices = range(lax.axis_size(axis))
    route = [(i - distance, i) for i in devices if i - distance in devices]
    return lax.ppermute(block, axis, route)


def extended(value, sides, width):
    for axis, dim in sides:
        size, length = (lax.axis_size(axis), value.shape[dim])
        up = [(i, (i + 1) % size) for i in range(size - 1)]
        down = [(j, i) for i, j in up]
        last = lax.slice_in_dim(value, length - width, length, axis=dim)
        initial = lax.slice_in_dim(value, 0, width, axis=dim)
        before = lax.ppermute(last, axis, up)
        after = lax.ppermute(initial, axis, down)
        value = jnp.concatenate([before, value, after], axis=dim)
    return value


def fourier_table(first_bin, bin_count, length):
    samples = jnp.arange(length, dtype=jnp.int32)[:, None]
    bin_index = first_bin + jnp.arange(bin_count, dtype=jnp.int32)[None, :]
    phase = samples * bin_index % length
    angle = 2.0 * math.pi / length * phase.astype(jnp.float32)
    taper = 0.5 - 0.5 * jnp.cos(
        2.0 * math.pi / length * jnp.arange(length, dtype=jnp.int32).astype(jnp.float32)
    )
    normaliser = 1.0 / math.sqrt(0.375 * length)
    cosine = (taper[:, None] * jnp.cos(angle) * normaliser).astype(jnp.bfloat16)
    sine_table = (-taper[:, None] * jnp.sin(angle) * normaliser).astype(jnp.bfloat16)
    return (cosine, sine_table)


def general(recording, trailing, whiten_filter, pair_list):
    local_rows, local_span = recording.shape
    hop_size = trailing.shape[1]
    window_size = 2 * hop_size
    segment_count = local_span // hop_size
    following = shifted(recording, "tm", -1)
    is_last = lax.axis_index("tm") == lax.axis_size("tm") - 1
    following = jnp.where(is_last, trailing, following)
    signal = jnp.concatenate([recording, following], axis=1)
    segments = jnp.stack([signal], axis=1)
    stacked_segments = segments.reshape(local_rows * segment_count, window_size)
    bin_step = min(256, FB)
    real_bins = []
    imag_bins = []
    for first_bin in range(0, FB, bin_step):
        cosine, sine_table = fourier_table(first_bin, bin_step, window_size)
        joined = jnp.concatenate([cosine, sine_table], axis=1)
        product = jnp.dot(stacked_segments, joined, preferred_element_type=jnp.float32).astype(
            jnp.bfloat16
        )
        real_bins.append(product[:, :bin_step])
        imag_bins.append(product[:, bin_step:])
    real_spec = jnp.concatenate(real_bins, axis=1)
    imag_spec = jnp.concatenate(imag_bins, axis=1)
    raw_spectra = jnp.stack([real_spec, imag_spec])
    tap_count = whiten_filter.shape[1]
    rim_width = tap_count // 2
    reach_rows = local_rows + tap_count
    skewed = jnp.pad(whiten_filter, ((0, 0), (0, local_rows + 1))).reshape(-1)
    band_matrix = skewed[: local_rows * reach_rows].reshape(local_rows, reach_rows)
    padded = extended(raw_spectra, ((("chan", "freq"), 1),), rim_width)
    predicted = jnp.einsum("ij,ajk->aik", band_matrix, padded, preferred_element_type=jnp.float32)
    whitened = (raw_spectra.astype(jnp.float32) - predicted).astype(jnp.bfloat16)
    spectra = whitened.reshape(2, local_rows, segment_count, FB)
    tm_count = lax.axis_size("tm")
    freq_count = lax.axis_size("freq")
    pieces = lax.all_to_all(spectra[None], ("tm", "freq"), split_axis=4, concat_axis=0, tiled=True)
    band_width = pieces.shape[-1]
    pieces = pieces.reshape(tm_count, freq_count, 2, local_rows, segment_count, band_width)
    banded = pieces.transpose(2, 1, 3, 0, 4, 5).reshape(
        2, freq_count * local_rows, tm_count * segment_count, band_width
    )
    block_rows = banded.shape[1]
    own_block = banded.reshape(2, block_rows, -1)
    depth = own_block.shape[2]
    scaling = 1.0 / math.sqrt(depth)
    block_index = lax.axis_index("chan")
    slot_list = pair_list[0]
    nearby = []
    for distance in range(-REACH, REACH + 1):
        if distance == 0:
            nearby.append(own_block)
        else:
            nearby.append(shifted(own_block, "chan", -distance))
    stacked = jnp.stack(nearby)

    def fetch_partner(partner_index):
        return lax.dynamic_index_in_dim(
            stacked, partner_index - block_index + REACH, 0, keepdims=False
        )

    left_side = jnp.concatenate([own_block[0], own_block[1]], axis=1)
    flipped = jnp.concatenate([own_block[1], -own_block[0]], axis=1)
    contract = (((1,), (1,)), ((), ()))

    def one_slot(partner_index):
        partner = fetch_partner(partner_index)
        right_side = jnp.concatenate([partner[0], partner[1]], axis=1)
        real_part = (
            lax.dot_general(left_side, right_side, contract, preferred_element_type=jnp.float32)
            * scaling
        )
        imag_part = (
            lax.dot_general(flipped, right_side, contract, preferred_element_type=jnp.float32)
            * scaling
        )
        crossed = jnp.stack([real_part, imag_part])
        return jnp.where(partner_index >= 0, crossed, jnp.zeros((), jnp.float32))

    result = jnp.stack([one_slot(slot_list[slot_index]) for slot_index in range(SLOTS)])
    return result.reshape(1, SLOTS, 1, 2, block_rows, block_rows)


MESH = pl.DeviceIdType.MESH
PIECES = (16, 16, 32, 32, 32)
GROUPS = ((0, 0, 32), (0, 32, 32), (1, 0, 32), (0, 64, 32), (1, 32, 32), (0, 96, 32), (1, 64, 32), (1, 96, 32))
TILE = 32
STEP = 32
SPECTRA_VMEM = 60 * 2**20


def spectra_kernel(
    chan_count,
    scaling,
    rec_ref,
    trail_ref,
    filt_ref,
    pairs_ref,
    out,
    samples,
    filters,
    bands,
    table,
    coarse,
    raw,
    gathered,
    sides,
    guest,
    pairs,
    ready,
    local_sems,
    send_sems,
    span_sems,
    pass_sems,
    core_sems,
    filter_sems,
    block_sems,
    guest_sems,
):
    me = lax.axis_index("chan")
    tm = lax.axis_index("tm")
    core = lax.axis_index("freq")
    rows, hop = rec_ref.shape
    window = 2 * hop
    width = table.shape[1] // 2
    block_rows = 2 * rows
    taps = filt_ref.shape[0]
    rim = taps // 2
    tile_count = block_rows // TILE
    group = rows // 2
    furthest = chan_count - 1
    has_left = me > 0
    has_right = me < chan_count - 1
    other = 1 - core
    other_tm = {"tm": 1 - tm}
    other_core = {"freq": 1 - core}
    left = {"chan": me - 1}
    right = {"chan": me + 1}
    ahead = (has_right, has_left)
    onward = (right, left)
    span_send, pass_send, core_send, swap_send = range(4)
    filter_send, block_send = (4, 5), (6, 7)
    guest_send, share_send = 8, 9
    hosting = jnp.logical_or(me == 0, me == furthest)

    def remote(source, target, send, recv, device):
        return pltpu.make_async_remote_copy(
            src_ref=source,
            dst_ref=target,
            send_sem=send_sems.at[send],
            recv_sem=recv,
            device_id=device,
            device_id_type=MESH,
        )

    def half(which):
        return pl.ds(pl.multiple_of(which * rows, rows), rows)

    barrier = pltpu.get_barrier_semaphore()
    later = ((has_right, right), (tm == 0, other_tm), (core == 1, other_core))
    earlier = ((has_left, left), (tm == 1, other_tm), (core == 0, other_core))
    for near, device in later:

        @pl.when(near)
        def _():
            pl.semaphore_signal(barrier, inc=1, device_id=device, device_id_type=MESH)

    own_copies = [
        pltpu.make_async_copy(rec_ref, samples.at[tm, half(core)], local_sems.at[0]),
        pltpu.make_async_copy(trail_ref, samples.at[2, half(core)], local_sems.at[1]),
        pltpu.make_async_copy(filt_ref, filters.at[me, core], local_sems.at[2]),
        pltpu.make_async_copy(pairs_ref, pairs, local_sems.at[3]),
    ]
    for copy in own_copies:
        copy.start()

    awaited = sum(near.astype(jnp.int32) for near, _ in earlier)

    @pl.when(awaited > 0)
    def _():
        pl.semaphore_wait(barrier, awaited)

    for link, (near, device) in enumerate(earlier):

        @pl.when(near)
        def _():
            pl.semaphore_signal(ready.at[link], inc=1, device_id=device, device_id_type=MESH)

    def meet(link):
        @pl.when(later[link][0])
        def _():
            pl.semaphore_wait(ready.at[link], 1)

    starts = [sum(PIECES[:p]) for p in range(len(PIECES))]

    def place(which, start, count):
        first = (1 - which) * start + which * (rows - start - count)
        return pl.multiple_of(first, math.gcd(start, count, rows))

    def piece_start(which, p):
        return place(which, starts[p], PIECES[p])

    def piece_in_block(which, p):
        start = which * rows + piece_start(which, p)
        return pl.ds(pl.multiple_of(start, math.gcd(starts[p], PIECES[p])), PIECES[p])

    def span_copy(p):
        return remote(
            rec_ref.at[pl.ds(piece_start(core, p), PIECES[p])],
            samples.at[tm, piece_in_block(core, p)],
            span_send,
            span_sems.at[p],
            other_tm,
        )

    meet(1)
    for p in range(len(PIECES)):
        span_copy(p).start()

    def core_copy(index, which):
        source, place = ((rec_ref, tm), (trail_ref, 2))[index]
        at = samples.at[place, half(which)]
        return remote(source, at, core_send, core_sems.at[index], other_core)

    meet(2)
    def lend():
        return remote(filt_ref, filters.at[me, 0], swap_send, core_sems.at[2], other_core)

    @pl.when(core == 0)
    def _():
        lend().start()

    for index in range(2):
        core_copy(index, core).start()

    def source_of(direction, distance):
        source = me - distance if direction == 0 else me + distance
        return jnp.clip(source, 0, chan_count - 1)

    def slot_of(direction, source):
        return jnp.clip(source - direction, 0, furthest - 1)

    def exists(direction, distance):
        return me - distance >= 0 if direction == 0 else me + distance < chan_count

    def weights_copy(direction, distance):
        source = source_of(direction, distance)
        at = filters.at[source]
        return remote(
            at,
            at,
            filter_send[direction],
            filter_sems.at[slot_of(direction, source)],
            onward[direction],
        )

    feeding = (me == furthest - 1, me == 1)

    def guest_copy(tm_index, core_index, send, sem, device):
        at = guest.at[tm_index, core_index]
        return remote(at, at, send, guest_sems.at[sem], device)

    for direction in (1, 0):
        if direction == 0:
            meet(0)

        @pl.when(feeding[direction])
        def _():
            first = pl.multiple_of((1 - core) * group, group)
            share = group // 2
            later_rows = pl.multiple_of(first + tm * share, share)
            for source, start, at, count in (
                (rec_ref, first, 0, group),
                (trail_ref, later_rows, group, share),
            ):
                remote(
                    source.at[pl.ds(start, count)],
                    guest.at[tm, core, at : at + count],
                    guest_send,
                    guest_sems.at[0],
                    onward[direction],
                ).start()

    first_bin = (tm * 2 + core) * width
    unit = 2.0 * math.pi / window
    bins = first_bin + lax.broadcasted_iota(jnp.int32, (1, width), 1)

    def angles(count, scale, factor):
        steps = scale * lax.broadcasted_iota(jnp.int32, (count, width), 0)
        return unit * jnp.bitwise_and(steps * factor, window - 1).astype(jnp.float32)

    parts = window // STEP
    coarse_angle = angles(parts, STEP, bins)
    coarse_turn = angles(parts, STEP, 1)
    coarse[0] = jnp.cos(coarse_angle)
    coarse[1] = jnp.sin(coarse_angle)
    coarse[2] = jnp.cos(coarse_turn)
    coarse[3] = jnp.sin(coarse_turn)
    fine_angle = angles(STEP, 1, bins)
    fine_turn = angles(STEP, 1, 1)
    fine_cos, fine_sin = jnp.cos(fine_angle), jnp.sin(fine_angle)
    turn_cos, turn_sin = jnp.cos(fine_turn), jnp.sin(fine_turn)
    normaliser = 1.0 / math.sqrt(0.375 * window)

    def fill(part, carry):
        c, s, tc, ts = (coarse[k, pl.ds(part, 1), :] for k in range(4))
        taper = (0.5 - 0.5 * (tc * turn_cos - ts * turn_sin)) * normaliser
        at = pl.ds(pl.multiple_of(part * STEP, STEP), STEP)
        table[at, :width] = (taper * (c * fine_cos - s * fine_sin)).astype(jnp.bfloat16)
        table[at, width:] = (-taper * (s * fine_cos + c * fine_sin)).astype(jnp.bfloat16)
        return carry

    lax.fori_loop(0, parts, fill, 0)

    own_copies[2].wait()

    @pl.when(core == 1)
    def _():
        lend().wait_recv()

    for direction in (1, 0):

        @pl.when(jnp.logical_and(ahead[direction], core == 1))
        def _():
            weights_copy(direction, 0).start()

    edge = jnp.zeros((rim, raw.shape[1]), raw.dtype)
    raw[0:rim] = edge
    raw[rim + chan_count * block_rows :] = edge

    for copy in (*own_copies[:2], own_copies[3]):
        copy.wait()
    for index in range(2):
        core_copy(index, other).wait_recv()

    def own_rows(block, start, count):
        return pl.ds(pl.multiple_of(rim + block * block_rows + start, 16), count)

    def block_copy(at, direction, distance, index):
        place = raw.at[at]
        return remote(
            place,
            place,
            block_send[direction],
            block_sems.at[slot_of(direction, source_of(direction, distance)), index],
            onward[direction],
        )

    def group_rows(direction, distance, index):
        which, start, count = GROUPS[index]
        here = core if which == 0 else other
        start = here * rows + place(here, start, count)
        return own_rows(source_of(direction, distance), start, count)

    def fill_rows(where, count, early, late):
        product = jnp.dot(early, table[:hop], preferred_element_type=jnp.float32) + jnp.dot(
            late, table[hop:], preferred_element_type=jnp.float32
        )
        product = product.astype(jnp.bfloat16)
        for segment in range(2):
            found = product[segment * count : (segment + 1) * count]
            raw[where, segment * width : (segment + 1) * width] = found[:, :width]
            raw[where, (2 + segment) * width : (3 + segment) * width] = found[:, width:]

    def group_of(which, p):
        return next(
            index
            for index, (side, start, count) in enumerate(GROUPS)
            if side == which and start <= starts[p] < start + count
        )

    def transform(which, p, index):
        at = which * rows + piece_start(which, p)
        chosen = piece_in_block(which, p)
        count = PIECES[p]
        where = own_rows(me, at, count)
        fill_rows(
            where,
            count,
            samples[0:2, chosen].reshape(2 * count, hop),
            samples[1:3, chosen].reshape(2 * count, hop),
        )
        for direction in (1, 0):
            wanted = ahead[direction]
            if starts[p] >= group:
                wanted = jnp.logical_and(wanted, jnp.logical_not(feeding[direction]))

            @pl.when(wanted)
            def _():
                block_copy(where, direction, 0, index).start()

    def guest_transform(which):
        first, second = guest[0, which, :group], guest[1, which, :group]
        third = jnp.concatenate([guest[0, which, group:], guest[1, which, group:]], axis=0)
        near = jnp.where(me == 0, 1, furthest - 1)
        fill_rows(
            own_rows(near, which * rows + (1 - which) * group, group),
            group,
            jnp.concatenate([first, second], axis=0),
            jnp.concatenate([second, third], axis=0),
        )

    def take_weights(distance):
        for direction in (1, 0):

            @pl.when(jnp.logical_and(exists(direction, distance), core == 1))
            def _():
                weights_copy(direction, distance).wait_recv()

            if distance < furthest:

                onwards = jnp.logical_and(exists(direction, distance), ahead[direction])

                @pl.when(jnp.logical_and(onwards, core == 1))
                def _():
                    weights_copy(direction, distance).start()

    def passed(which, p):
        at = samples.at[1 - tm, piece_in_block(which, p)]
        return remote(at, at, pass_send, pass_sems.at[p], other_core)

    def arrive(distance, index):
        for direction in (1, 0):
            at = group_rows(direction, distance, index)

            expected = exists(direction, distance)
            if distance == 1 and GROUPS[index][1] >= group:
                expected = jnp.logical_and(expected, jnp.logical_not(hosting))

            @pl.when(expected)
            def _():
                block_copy(at, direction, distance, index).wait_recv()

            if distance < furthest:

                @pl.when(jnp.logical_and(exists(direction, distance), ahead[direction]))
                def _():
                    block_copy(at, direction, distance, index).start()

    def own_piece(p):
        span_copy(p).wait_recv()
        passed(core, p).start()
        transform(core, p, group_of(0, p))

    def other_piece(p):
        passed(other, p).wait_recv()
        transform(other, p, group_of(1, p))

    own_piece(0)
    own_piece(1)
    other_piece(0)
    take_weights(1)
    own_piece(2)
    other_piece(1)
    own_piece(3)
    other_piece(2)
    own_piece(4)
    other_piece(3)

    @pl.when(hosting)
    def _():
        guest_copy(tm, core, guest_send, 0, other_tm).wait_recv()
        guest_copy(tm, core, guest_send, 1, other_tm).start()
        guest_copy(tm, core, share_send, 2, other_core).start()

    take_weights(2)

    @pl.when(jnp.logical_not(hosting))
    def _():
        arrive(1, 0)

    other_piece(4)

    @pl.when(jnp.logical_not(hosting))
    def _():
        arrive(1, 1)

    @pl.when(hosting)
    def _():
        arrive(1, 0)
        arrive(1, 1)

    def spread(block, carry):
        for which in range(2):
            weights = jnp.transpose(filters[block, which].astype(jnp.float32))
            wide = jnp.concatenate([weights, jnp.zeros((rows, 128 - taps), jnp.float32)], axis=1)
            for p in range(tile_count // 2):
                rolled = pltpu.roll(
                    wide[p * TILE : (p + 1) * TILE], 0, 1, stride=1, stride_axis=0
                )
                bands[block, which * tile_count // 2 + p] = rolled.astype(jnp.bfloat16)
        return carry

    def whiten(block, tile):
        start = pl.multiple_of(block * block_rows + tile * TILE, TILE)
        at = pl.ds(pl.multiple_of(tile * TILE, TILE), TILE)
        near = raw[pl.ds(start, TILE + taps)]
        predicted = jnp.dot(
            bands[block, tile][:, : TILE + taps], near, preferred_element_type=jnp.float32
        )
        mine = near[rim : rim + TILE].astype(jnp.float32)
        gathered[block, at] = (mine - predicted).astype(jnp.bfloat16)

    contract = (((1,), (1,)), ((), ()))

    def cross(block, first=False):
        partner = gathered[block]
        both = lax.dot_general(sides[...], partner, contract, preferred_element_type=jnp.float32)
        for part in range(2):
            product = both[part * block_rows : (part + 1) * block_rows] * scaling
            for slot in range(SLOTS):
                before = jnp.zeros_like(product) if first else out[slot, part]
                out[slot, part] = jnp.where(pairs[0, slot] == block, product, before)

    def finish_own():
        for tile in range(tile_count):
            whiten(me, tile)
        own = gathered[me]
        middle = own.shape[1] // 2
        sides[:block_rows] = own
        sides[block_rows:] = jnp.concatenate([own[:, middle:], -own[:, :middle]], axis=1)
        cross(me, True)

    def inner(distance):
        for direction in (1, 0):

            @pl.when(exists(direction, distance))
            def _():
                block = me - distance if direction == 0 else me + distance
                for tile in range(tile_count - 1):
                    whiten(block, tile + 1 if direction == 0 else tile)

    def finish(distance):
        for direction in (1, 0):

            @pl.when(exists(direction, distance))
            def _():
                block = me - distance if direction == 0 else me + distance
                whiten(block, 0 if direction == 0 else tile_count - 1)
                cross(block)

    def hand():
        return remote(filters, filters, swap_send, core_sems.at[2], other_core)

    for index in range(2, len(GROUPS)):
        arrive(1, index)
    take_weights(3)

    @pl.when(core == 1)
    def _():
        hand().start()

    for index in range(len(GROUPS) - 2):
        arrive(2, index)

    @pl.when(jnp.logical_and(hosting, core == 0))
    def _():
        hand().wait_recv()

    @pl.when(hosting)
    def _():
        lax.fori_loop(0, chan_count, spread, 0)
        finish_own()

    for index in range(len(GROUPS) - 2, len(GROUPS)):
        arrive(2, index)

    @pl.when(hosting)
    def _():
        guest_copy(1 - tm, core, guest_send, 1, other_tm).wait_recv()
        guest_copy(1 - tm, core, share_send, 3, other_core).start()

    @pl.when(jnp.logical_and(jnp.logical_not(hosting), core == 0))
    def _():
        hand().wait_recv()

    @pl.when(jnp.logical_not(hosting))
    def _():
        lax.fori_loop(0, chan_count, spread, 0)
        finish_own()

    arrive(3, 0)
    arrive(3, 1)

    @pl.when(hosting)
    def _():
        guest_copy(tm, other, share_send, 2, other_core).wait_recv()
        guest_transform(core)
        guest_copy(1 - tm, other, share_send, 3, other_core).wait_recv()
        guest_transform(other)

    inner(1)
    finish(1)
    arrive(3, 2)
    inner(2)
    finish(2)
    for index in range(3, len(GROUPS) - 1):
        arrive(3, index)

    def last(tiles, complete):
        for direction in (1, 0):

            @pl.when(exists(direction, furthest))
            def _():
                block = me - furthest if direction == 0 else me + furthest
                for tile in tiles:
                    whiten(block, tile)
                if complete:
                    cross(block)

    last((0, 1, 2 + 3 * core, 6, 7), False)
    arrive(3, len(GROUPS) - 1)
    last([3 - core + tile for tile in range(3)], True)

    guest_copy(tm, core, guest_send, 1, other_tm).wait_send()

    @pl.when(hosting)
    def _():
        shared = guest.at[0:2, core]
        remote(shared, shared, share_send, guest_sems.at[2], other_core).wait_send()

    whole = samples.at[tm, half(core)]
    remote(whole, whole, span_send, span_sems.at[0], other_tm).wait_send()
    remote(whole, whole, pass_send, pass_sems.at[0], other_core).wait_send()
    both = samples.at[0:2, half(core)]
    remote(both, both, core_send, core_sems.at[0], other_core).wait_send()

    @pl.when(core == 0)
    def _():
        lend().wait_send()

    @pl.when(core == 1)
    def _():
        hand().wait_send()

    for direction in (1, 0):
        for count in range(1, chan_count):

            @pl.when(me == (count - 1 if direction == 0 else chan_count - count))
            def _():
                @pl.when(core == 1)
                def _():
                    sent = filters.at[0:count]
                    remote(
                        sent, sent, filter_send[direction], filter_sems.at[0], onward[direction]
                    ).wait_send()

                fed = rows if count == furthest else 0
                sent = raw.at[0 : count * block_rows - fed]
                remote(
                    sent, sent, block_send[direction], block_sems.at[0, 0], onward[direction]
                ).wait_send()


def fused(recording, trailing, whiten_filter, pair_list):
    rows, hop = recording.shape
    chan_count = lax.axis_size("chan")
    taps = whiten_filter.shape[1]
    width = FB // (lax.axis_size("tm") * lax.axis_size("freq"))
    block_rows = 2 * rows
    depth = 2 * width
    vmem = pl.BlockSpec(memory_space=pltpu.VMEM)
    hbm = pl.BlockSpec(memory_space=pltpu.HBM)
    slots = pl.pallas_call(
        functools.partial(spectra_kernel, chan_count, 1.0 / math.sqrt(depth)),
        out_shape=pltpu.VMEM((SLOTS, 2, block_rows, block_rows), jnp.float32),
        in_specs=[hbm] * 4,
        out_specs=vmem,
        scratch_shapes=[
            pltpu.VMEM((3, block_rows, hop), jnp.bfloat16),
            pltpu.VMEM((chan_count, 2, taps, rows), jnp.bfloat16),
            pltpu.VMEM((chan_count, block_rows // TILE, TILE, 128), jnp.bfloat16),
            pltpu.VMEM((2 * hop, 2 * width), jnp.bfloat16),
            pltpu.VMEM((4, 2 * hop // STEP, width), jnp.float32),
            pltpu.VMEM((chan_count * block_rows + taps, 2 * depth), jnp.bfloat16),
            pltpu.VMEM((chan_count, block_rows, 2 * depth), jnp.bfloat16),
            pltpu.VMEM((2 * block_rows, 2 * depth), jnp.bfloat16),
            pltpu.VMEM((2, 2, 3 * rows // 4, hop), jnp.bfloat16),
            pltpu.SMEM((1, SLOTS), jnp.int32),
            pltpu.SemaphoreType.REGULAR((3,)),
            pltpu.SemaphoreType.DMA((4,)),
            pltpu.SemaphoreType.DMA((10,)),
            pltpu.SemaphoreType.DMA((len(PIECES),)),
            pltpu.SemaphoreType.DMA((len(PIECES),)),
            pltpu.SemaphoreType.DMA((3,)),
            pltpu.SemaphoreType.DMA((chan_count - 1,)),
            pltpu.SemaphoreType.DMA((chan_count - 1, len(GROUPS))),
            pltpu.SemaphoreType.DMA((4,)),
        ],
        compiler_params=pltpu.CompilerParams(
            collective_id=0, has_side_effects=True, vmem_limit_bytes=SPECTRA_VMEM
        ),
    )(recording, trailing, whiten_filter.T, pair_list)
    return slots.reshape(1, SLOTS, 1, 2, block_rows, block_rows)


def local(recording, trailing, whiten_filter, pair_list):
    shapes = (recording.shape, trailing.shape, whiten_filter.shape)
    counts = (lax.axis_size("tm"), lax.axis_size("freq"))
    whole_reach = lax.axis_size("chan") == REACH + 1
    if shapes == ((128, 1024), (128, 1024), (128, 64)) and counts == (2, 2) and whole_reach:
        return fused(recording, trailing, whiten_filter, pair_list)
    return general(recording, trailing, whiten_filter, pair_list)


def solution(mesh):
    placed = (
        P(("days", "chan", "freq"), "tm"),
        P(("days", "chan", "freq"), None),
        P(("chan", "freq"), None),
        P(("days", "chan"), None),
    )
    return jax.shard_map(
        local,
        mesh=mesh,
        in_specs=placed,
        out_specs=P(("days", "chan"), None, ("tm", "freq"), None, None, None),
        check_vma=False,
    )
```
